256 devices in a mesh: gx: 16 (over x_lo, y, core), gy: 16 (over x_hi, z).
Axes of the slice: x: 4 (x_hi: 2, x_lo: 2; x = x_hi * 2 + x_lo), y: 4, z: 8, core: 2. Of those that a mesh axis runs over, the one named last changes fastest.
Arguments:
- concentration: float32 [512, 512, 256], P('gx', 'gy'), may hold values from 0 to 1
- order_field: float32 [512, 512, 256], P('gx', 'gy'), may hold values from 0 to 1
- phase_labels: int32 [512, 512, 256], P('gx', 'gy'), may hold values from 0 to 2
- displacement: float32 [3, 256, 128, 256], P(None, 'gx', 'gy'), may hold values from -4 to 4
- body_load: float32 [3, 256, 128, 256], P(None, 'gx', 'gy'), may hold values from -6 to 6
Outputs:
- concentration_out: float32 [512, 512, 256], P('gx', 'gy')
- order_out: float32 [512, 512, 256], P('gx', 'gy')
- displacement_out: float32 [3, 256, 128, 256], P(None, 'gx', 'gy')
- energy_tiles: float32 [256, 256, 128], P('gx', 'gy')
The draws below stay inside these ranges and needn't reach their ends.
All inputs are finite; a program needn't handle non-finite values.
Results may differ from the reference program's by a relative error of at most 0.0003.
Values sent between devices are 32-bit elements; how exact they have to be, the bound alone decides.
A program may use at most 192 MiB of HBM per device.

```python
import jax
import jax.numpy as jnp

STEPS = 4
NX = 512
NY = 512
NZ = 256
NXC = 256
NYC = 256
NZC = 128


def plant(array, stream_key, smallest, largest):
    place = [jax.random.randint(jax.random.fold_in(stream_key, axis), (), 0, length) for axis, length in enumerate(array.shape)]
    widest = array.shape.index(max(array.shape))
    neighbour = place[:widest] + [(place[widest] + 1) % array.shape[widest]] + place[widest + 1:]
    return array.at[tuple(place)].set(smallest).at[tuple(neighbour)].set(largest)


def block_scale(rng, extent, cuts, low, high):
    gain, own = 1.0, jax.random.fold_in(rng, 6)
    for dim, shards_of in cuts:
        draws = jnp.exp(jax.random.uniform(jax.random.fold_in(own, dim), (shards_of,), jnp.float32, low / len(cuts), high / len(cuts)))
        gain = gain * jnp.repeat(draws, extent[dim] // shards_of).reshape([-1 if axis == dim else 1 for axis in range(len(extent))])
    return gain


def gaussian(rng, dims, spread, reach, pieces=(), kind=jnp.bfloat16):
    gain = block_scale(rng, dims, pieces, -0.22, 0.18) if pieces else 1.0
    values = jax.random.normal(rng, dims, jnp.float32) * spread * gain
    return jnp.minimum(jnp.maximum(values, -reach), reach).astype(kind)


def setup_inputs(seed: int = 0) -> dict:
    key_of = jax.random.split(jax.random.key(seed), 6)
    concentration = jnp.clip(1.0 * jax.random.uniform(key_of[0], (NX, NY, NZ), jnp.float32) ** block_scale(key_of[0], (NX, NY, NZ), ((0, 16), (1, 16)), -0.2, 0.2), 0.0, 1.0)
    order_field = jnp.clip(1.0 * jax.random.uniform(key_of[1], (NX, NY, NZ), jnp.float32) ** block_scale(key_of[1], (NX, NY, NZ), ((0, 16), (1, 16)), -0.2, 0.2), 0.0, 1.0)
    phase_labels = plant(jax.random.randint(key_of[2], (NX, NY, NZ), 0, 3), jax.random.fold_in(key_of[2], 1), 0, 2).astype(jnp.int32)
    displacement = gaussian(key_of[3], (3, NXC, NZC, NYC), 0.5, 4.0, ((1, 16), (2, 16)), jnp.float32)
    body_load = gaussian(key_of[4], (3, NXC, NZC, NYC), 1.0, 6.0, ((1, 16), (2, 16)), jnp.float32)
    return dict(concentration=concentration, order_field=order_field, phase_labels=phase_labels, displacement=displacement, body_load=body_load)


rate_conc = 0.15
rate_order = 0.15
well_height = 1.0
drive_coupling = 0.5
spring_term = 0.2
first_weight = 0.5956
second_weight = 2.695


def fine_laplace(padded):
    zpad = jnp.pad(padded, ((0, 0), (0, 0), (1, 1)))
    center = zpad[1:-1, 1:-1, 1:-1]
    total = zpad[2:, 1:-1, 1:-1] + zpad[:-2, 1:-1, 1:-1]
    total = total + zpad[1:-1, 2:, 1:-1] + zpad[1:-1, :-2, 1:-1]
    total = total + zpad[1:-1, 1:-1, 2:] + zpad[1:-1, 1:-1, :-2]
    return total - 6.0 * center


def advance(conc_pad, order_pad, mobility):
    chem = conc_pad - order_pad * order_pad * (3.0 - 2.0 * order_pad)
    conc_in = conc_pad[1:-1, 1:-1]
    order_in = order_pad[1:-1, 1:-1]
    chem_in = chem[1:-1, 1:-1]
    conc_new = conc_in + rate_conc * fine_laplace(chem)
    dh_term = 6.0 * order_in * (1.0 - order_in)
    dg_term = 2.0 * order_in * (1.0 - order_in) * (1.0 - 2.0 * order_in)
    order_new = order_in + mobility * (rate_order * fine_laplace(order_pad) - well_height * dg_term + drive_coupling * chem_in * dh_term)
    return conc_new, order_new


def mobility_of(labels):
    return (0.5 * (labels == 0) + 1.0 * (labels == 1) + 0.25 * (labels == 2)).astype(jnp.float32)


def restrict(order_out):
    sx, sy, sz = order_out.shape
    sq = (order_out * order_out).reshape(sx // 2, 2, sy // 2, 2, sz // 2, 2)
    return 0.1 + 0.125 * jnp.sum(sq, axis=(1, 3, 5))


def shifted(padded):
    return [padded[..., 2:, 1:-1, 1:-1], padded[..., :-2, 1:-1, 1:-1],
            padded[..., 1:-1, 2:, 1:-1], padded[..., 1:-1, :-2, 1:-1],
            padded[..., 1:-1, 1:-1, 2:], padded[..., 1:-1, 1:-1, :-2]]


def face_terms(stiff_pad):
    center = stiff_pad[1:-1, 1:-1, 1:-1]
    faces = [0.5 * (center + other) for other in shifted(stiff_pad)]
    diag = faces[0] + faces[1] + faces[2] + faces[3] + faces[4] + faces[5] + spring_term * center
    return faces, diag


def apply_op(disp_pad, faces, diag):
    center = disp_pad[:, 1:-1, 1:-1, 1:-1]
    result = diag * center
    for face, other in zip(faces, shifted(disp_pad)):
        result = result - face * other
    return result


def strain_energy(disp_pad, faces):
    center = disp_pad[:, 1:-1, 1:-1, 1:-1]
    total = jnp.zeros(center.shape, jnp.float32)
    for face, other in zip(faces, shifted(disp_pad)):
        diff = center - other
        total = total + face * diff * diff
    return 0.25 * jnp.sum(total, axis=0)


def reference(concentration, order_field, phase_labels, displacement, body_load):
    mobility = mobility_of(phase_labels)
    conc, order = concentration, order_field
    for step in range(STEPS):
        conc_pad = jnp.pad(conc, ((1, 1), (1, 1), (0, 0)))
        order_pad = jnp.pad(order, ((1, 1), (1, 1), (0, 0)))
        conc, order = advance(conc_pad, order_pad, mobility)
    stiff = jnp.transpose(restrict(order), (0, 2, 1))
    faces, diag = face_terms(jnp.pad(stiff, 1))
    widths = ((0, 0), (1, 1), (1, 1), (1, 1))
    disp = displacement
    for weight in (first_weight, second_weight):
        disp = disp + weight * (body_load - apply_op(jnp.pad(disp, widths), faces, diag)) / diag
    energy = strain_energy(jnp.pad(disp, widths), faces)
    return conc, order, disp, jnp.transpose(energy, (0, 2, 1))
```

```python
import jax
import jax.numpy as jnp
import numpy as np
from jax import lax
from jax.sharding import PartitionSpec as P

STEPS = 4
FINE_HALO = 4
MECH_HALO = 3

rate_conc = 0.15
rate_order = 0.15
well_height = 1.0
drive_coupling = 0.5
spring_term = 0.2
first_weight = 0.5956
second_weight = 2.695


def padded_2(block, sides, width):
    for axis, dim in sides:
        count = lax.axis_size(axis)
        forward = [(i, i + 1) for i in range(count - 1)]
        backward = [(target, source) for source, target in forward]
        low = lax.ppermute(
            lax.slice_in_dim(block, block.shape[dim] - width, None, axis=dim), axis, forward
        )
        high = lax.ppermute(lax.slice_in_dim(block, 0, width, axis=dim), axis, backward)
        block = jnp.concatenate([low, block, high], axis=dim)
    return block


def fine_laplace(padded):
    zpad = jnp.pad(padded, ((0, 0), (0, 0), (1, 1)))
    center = zpad[1:-1, 1:-1, 1:-1]
    total = zpad[2:, 1:-1, 1:-1] + zpad[:-2, 1:-1, 1:-1]
    total = total + zpad[1:-1, 2:, 1:-1] + zpad[1:-1, :-2, 1:-1]
    total = total + zpad[1:-1, 1:-1, 2:] + zpad[1:-1, 1:-1, :-2]
    return total - 6.0 * center


def advance(conc_pad, order_pad, mob_pad, last):
    chem = conc_pad - order_pad * order_pad * (3.0 - 2.0 * order_pad)
    conc_in = conc_pad[1:-1, 1:-1]
    order_in = order_pad[1:-1, 1:-1]
    chem_in = chem[1:-1, 1:-1]
    mobility = mob_pad[1:-1, 1:-1]
    conc_new = conc_in + rate_conc * fine_laplace(chem)
    dh_term = 6.0 * order_in * (1.0 - order_in)
    dg_term = 2.0 * order_in * (1.0 - order_in) * (1.0 - 2.0 * order_in)
    order_new = order_in + mobility * (
        rate_order * fine_laplace(order_pad)
        - well_height * dg_term
        + drive_coupling * chem_in * dh_term
    )
    if not last:
        conc_new = jnp.where(mobility > 0, conc_new, 0.0)
    return conc_new, order_new, mobility


def mobility_of(labels):
    return (0.5 * (labels == 0) + 1.0 * (labels == 1) + 0.25 * (labels == 2)).astype(jnp.float32)


def restrict_xzy(order_out):
    sx, sy, sz = order_out.shape
    sq = order_out * order_out
    sq = sq.reshape(sx // 2, 2, sy, sz).sum(axis=1)
    sq = sq.reshape(sx // 2, sy // 2, 2, sz).sum(axis=2)
    pairs = jnp.asarray(np.repeat(np.eye(sz // 2, dtype=np.float32), 2, axis=0))
    summed = jnp.einsum("xyz,zw->xwy", sq, pairs, precision=lax.Precision.HIGHEST)
    return 0.1 + 0.125 * summed


def y_shift(v, step):
    if step > 0:
        return jnp.pad(v[..., step:], [(0, 0)] * (v.ndim - 1) + [(0, step)])
    return jnp.pad(v[..., :step], [(0, 0)] * (v.ndim - 1) + [(-step, 0)])


def face_terms(stiff_pad):
    center = stiff_pad[1:-1, 1:-1]
    others = [stiff_pad[2:, 1:-1], stiff_pad[:-2, 1:-1], stiff_pad[1:-1, 2:], stiff_pad[1:-1, :-2],
              y_shift(center, 1), y_shift(center, -1)]
    faces = [0.5 * (center + other) for other in others]
    diag = faces[0] + faces[1] + faces[2] + faces[3] + faces[4] + faces[5] + spring_term * center
    return faces, diag, center


def neighbours(u_pad):
    center = u_pad[:, 1:-1, 1:-1]
    return center, [u_pad[:, 2:, 1:-1], u_pad[:, :-2, 1:-1], u_pad[:, 1:-1, 2:], u_pad[:, 1:-1, :-2],
                    y_shift(center, 1), y_shift(center, -1)]


def apply_op(u_pad, faces, diag):
    center, others = neighbours(u_pad)
    result = diag * center
    for face, other in zip(faces, others):
        result = result - face * other
    return result, center


def strain_energy(u_pad, faces):
    center, others = neighbours(u_pad)
    total = jnp.zeros(center.shape, jnp.float32)
    for face, other in zip(faces, others):
        diff = center - other
        total = total + face * diff * diff
    return 0.25 * jnp.sum(total, axis=0)


def on_device(concentration, order_field, phase_labels, displacement, body_load):
    h = FINE_HALO
    fields = jnp.stack([concentration, order_field, mobility_of(phase_labels)])
    fields = padded_2(fields, (("gx", 1), ("gy", 2)), h)
    conc, order, mob = fields[0], fields[1], fields[2]
    for step in range(STEPS):
        conc, order, mob = advance(conc, order, mob, step == STEPS - 1)

    m = MECH_HALO
    ub = padded_2(jnp.concatenate([displacement, body_load]), (("gx", 1), ("gy", 2)), m)
    disp, load = ub[:3], ub[3:]

    coarse = restrict_xzy(order)
    stiff = lax.all_to_all(coarse, "gy", split_axis=1, concat_axis=2, tiled=True)
    stiff_pad = padded_2(stiff, (("gx", 0), ("gy", 1)), m)

    faces, diag, center = face_terms(stiff_pad)
    for weight in (first_weight, second_weight):
        load = load[:, 1:-1, 1:-1]
        result, u_c = apply_op(disp, faces, diag)
        new = u_c + weight * (load - result) / diag
        disp = jnp.where(center > 0, new, 0.0)
        faces = [f[1:-1, 1:-1] for f in faces]
        diag = diag[1:-1, 1:-1]
        center = center[1:-1, 1:-1]
    energy = strain_energy(disp, faces)
    disp = disp[:, 1:-1, 1:-1]
    tiles = lax.all_to_all(energy, "gy", split_axis=2, concat_axis=1, tiled=True)
    return (conc, order, disp, jnp.transpose(tiles, (0, 2, 1)))


def solution(mesh):
    return jax.shard_map(
        on_device,
        mesh=mesh,
        in_specs=(
            P("gx", "gy", None),
            P("gx", "gy", None),
            P("gx", "gy", None),
            P(None, "gx", "gy", None),
            P(None, "gx", "gy", None),
        ),
        out_specs=(
            P("gx", "gy", None),
            P("gx", "gy", None),
            P(None, "gx", "gy", None),
            P("gx", "gy", None),
        ),
        check_vma=False,
    )
```

```python
import jax
import jax.numpy as jnp
import numpy as np
from jax import lax
from jax.sharding import PartitionSpec as P

STEPS = 4
FINE_HALO = 4
MECH_HALO = 3

rate_conc = 0.15
rate_order = 0.15
well_height = 1.0
drive_coupling = 0.5
spring_term = 0.2
first_weight = 0.5956
second_weight = 2.695


def padded_2(block, sides, width):
    for axis, dim in sides:
        count = lax.axis_size(axis)
        forward = [(i, i + 1) for i in range(count - 1)]
        backward = [(target, source) for source, target in forward]
        low = lax.ppermute(
            lax.slice_in_dim(block, block.shape[dim] - width, None, axis=dim), axis, forward
        )
        high = lax.ppermute(lax.slice_in_dim(block, 0, width, axis=dim), axis, backward)
        block = jnp.concatenate([low, block, high], axis=dim)
    return block


def halo_2d(block, dims, width):
    (ax0, d0), (ax1, d1) = dims
    n0, n1 = lax.axis_size(ax0), lax.axis_size(ax1)
    w = width

    def part(v, dim, side):
        if side > 0:
            return lax.slice_in_dim(v, v.shape[dim] - w, None, axis=dim)
        if side < 0:
            return lax.slice_in_dim(v, 0, w, axis=dim)
        return v

    got = {}
    for s0 in (-1, 0, 1):
        for s1 in (-1, 0, 1):
            if s0 == 0 and s1 == 0:
                continue
            piece = part(part(block, d0, s0), d1, s1)
            pairs = []
            for i in range(n0):
                for j in range(n1):
                    ti, tj = i + s0, j + s1
                    if 0 <= ti < n0 and 0 <= tj < n1:
                        pairs.append((i * n1 + j, ti * n1 + tj))
            got[(s0, s1)] = lax.ppermute(piece, (ax0, ax1), pairs)
    got[(0, 0)] = block
    rows = [jnp.concatenate([got[(s0, 1)], got[(s0, 0)], got[(s0, -1)]], axis=d1) for s0 in (1, 0, -1)]
    return jnp.concatenate(rows, axis=d0)


def fine_laplace(padded):
    zpad = jnp.pad(padded, ((0, 0), (0, 0), (1, 1)))
    center = zpad[1:-1, 1:-1, 1:-1]
    total = zpad[2:, 1:-1, 1:-1] + zpad[:-2, 1:-1, 1:-1]
    total = total + zpad[1:-1, 2:, 1:-1] + zpad[1:-1, :-2, 1:-1]
    total = total + zpad[1:-1, 1:-1, 2:] + zpad[1:-1, 1:-1, :-2]
    return total - 6.0 * center


def advance(conc_pad, order_pad, mob_pad, last):
    chem = conc_pad - order_pad * order_pad * (3.0 - 2.0 * order_pad)
    conc_in = conc_pad[1:-1, 1:-1]
    order_in = order_pad[1:-1, 1:-1]
    chem_in = chem[1:-1, 1:-1]
    mobility = mob_pad[1:-1, 1:-1]
    conc_new = conc_in + rate_conc * fine_laplace(chem)
    dh_term = 6.0 * order_in * (1.0 - order_in)
    dg_term = 2.0 * order_in * (1.0 - order_in) * (1.0 - 2.0 * order_in)
    order_new = order_in + mobility * (
        rate_order * fine_laplace(order_pad)
        - well_height * dg_term
        + drive_coupling * chem_in * dh_term
    )
    if not last:
        conc_new = jnp.where(mobility > 0, conc_new, 0.0)
    return conc_new, order_new, mobility


def mobility_of(labels):
    return (0.5 * (labels == 0) + 1.0 * (labels == 1) + 0.25 * (labels == 2)).astype(jnp.float32)


def restrict_xzy(order_out):
    sx, sy, sz = order_out.shape
    sq = order_out * order_out
    sq = sq.reshape(sx // 2, 2, sy, sz).sum(axis=1)
    sq = sq.reshape(sx // 2, sy // 2, 2, sz).sum(axis=2)
    pairs = jnp.asarray(np.repeat(np.eye(sz // 2, dtype=np.float32), 2, axis=0))
    summed = jnp.einsum("xyz,zw->xwy", sq, pairs, precision=lax.Precision.HIGHEST)
    return 0.1 + 0.125 * summed


def y_shift(v, step):
    if step > 0:
        return jnp.pad(v[..., step:], [(0, 0)] * (v.ndim - 1) + [(0, step)])
    return jnp.pad(v[..., :step], [(0, 0)] * (v.ndim - 1) + [(-step, 0)])


def face_terms(stiff_pad):
    center = stiff_pad[1:-1, 1:-1]
    others = [stiff_pad[2:, 1:-1], stiff_pad[:-2, 1:-1], stiff_pad[1:-1, 2:], stiff_pad[1:-1, :-2],
              y_shift(center, 1), y_shift(center, -1)]
    faces = [0.5 * (center + other) for other in others]
    diag = faces[0] + faces[1] + faces[2] + faces[3] + faces[4] + faces[5] + spring_term * center
    return faces, diag, center


def neighbours(u_pad):
    center = u_pad[:, 1:-1, 1:-1]
    return center, [u_pad[:, 2:, 1:-1], u_pad[:, :-2, 1:-1], u_pad[:, 1:-1, 2:], u_pad[:, 1:-1, :-2],
                    y_shift(center, 1), y_shift(center, -1)]


def apply_op(u_pad, faces, diag):
    center, others = neighbours(u_pad)
    result = diag * center
    for face, other in zip(faces, others):
        result = result - face * other
    return result, center


def strain_energy(u_pad, faces):
    center, others = neighbours(u_pad)
    total = jnp.zeros(center.shape, jnp.float32)
    for face, other in zip(faces, others):
        diff = center - other
        total = total + face * diff * diff
    return 0.25 * jnp.sum(total, axis=0)


def on_device(concentration, order_field, phase_labels, displacement, body_load):
    h = FINE_HALO
    fields = jnp.stack([concentration, order_field, mobility_of(phase_labels)])
    fields = halo_2d(fields, (("gx", 1), ("gy", 2)), h)
    conc, order, mob = fields[0], fields[1], fields[2]
    for step in range(STEPS):
        conc, order, mob = advance(conc, order, mob, step == STEPS - 1)

    m = MECH_HALO
    ub = halo_2d(jnp.concatenate([displacement, body_load]), (("gx", 1), ("gy", 2)), m)
    disp, load = ub[:3], ub[3:]

    coarse = restrict_xzy(order)
    stiff = lax.all_to_all(coarse, "gy", split_axis=1, concat_axis=2, tiled=True)
    stiff_pad = halo_2d(stiff, (("gx", 0), ("gy", 1)), m)

    faces, diag, center = face_terms(stiff_pad)
    for weight in (first_weight, second_weight):
        load = load[:, 1:-1, 1:-1]
        result, u_c = apply_op(disp, faces, diag)
        new = u_c + weight * (load - result) / diag
        disp = jnp.where(center > 0, new, 0.0)
        faces = [f[1:-1, 1:-1] for f in faces]
        diag = diag[1:-1, 1:-1]
        center = center[1:-1, 1:-1]
    energy = strain_energy(disp, faces)
    disp = disp[:, 1:-1, 1:-1]
    tiles = lax.all_to_all(energy, "gy", split_axis=2, concat_axis=1, tiled=True)
    return (conc, order, disp, jnp.transpose(tiles, (0, 2, 1)))


def solution(mesh):
    return jax.shard_map(
        on_device,
        mesh=mesh,
        in_specs=(
            P("gx", "gy", None),
            P("gx", "gy", None),
            P("gx", "gy", None),
            P(None, "gx", "gy", None),
            P(None, "gx", "gy", None),
        ),
        out_specs=(
            P("gx", "gy", None),
            P("gx", "gy", None),
            P(None, "gx", "gy", None),
            P("gx", "gy", None),
        ),
        check_vma=False,
    )
```

```python
import jax
import jax.numpy as jnp
import functools

import numpy as np
from jax import lax
from jax.experimental import pallas as pl
from jax.experimental.pallas import tpu as pltpu
from jax.sharding import PartitionSpec as P

STEPS = 4
FINE_HALO = 4
MECH_HALO = 3

rate_conc = 0.15
rate_order = 0.15
well_height = 1.0
drive_coupling = 0.5
spring_term = 0.2
first_weight = 0.5956
second_weight = 2.695


MESH = pl.DeviceIdType.MESH


def exchange_kernel(n, src_ref, out_ref, recv, send_sem, recv_sem):
    me = lax.axis_index("gy")
    row = lax.axis_index("gx")
    barrier = pltpu.get_barrier_semaphore()
    for d in range(1, n):
        peer = lax.rem(me + d, n)
        pl.semaphore_signal(barrier, inc=1, device_id=(row, peer), device_id_type=MESH)
    pl.semaphore_wait(barrier, n - 1)
    copies = []
    for d in range(1, n):
        peer = lax.rem(me + d, n)
        copy = pltpu.make_async_remote_copy(
            src_ref=src_ref.at[peer],
            dst_ref=recv.at[me],
            send_sem=send_sem.at[d],
            recv_sem=recv_sem.at[d],
            device_id=(row, peer),
            device_id_type=MESH,
        )
        copy.start()
        copies.append(copy)
    recv[me] = src_ref[me]
    for copy in copies:
        copy.wait()
    out_ref[...] = recv[...]


def all_to_all_gy(src, cid):
    n = src.shape[0]
    return pl.pallas_call(
        functools.partial(exchange_kernel, n),
        out_shape=jax.ShapeDtypeStruct(src.shape, src.dtype),
        in_specs=[pl.BlockSpec(memory_space=pltpu.VMEM)],
        out_specs=pl.BlockSpec(memory_space=pltpu.VMEM),
        scratch_shapes=[
            pltpu.VMEM(src.shape, src.dtype),
            pltpu.SemaphoreType.DMA((n,)),
            pltpu.SemaphoreType.DMA((n,)),
        ],
        compiler_params=pltpu.CompilerParams(collective_id=cid, has_side_effects=True),
    )(src)


def padded_2(block, sides, width):
    for axis, dim in sides:
        count = lax.axis_size(axis)
        forward = [(i, i + 1) for i in range(count - 1)]
        backward = [(target, source) for source, target in forward]
        low = lax.ppermute(
            lax.slice_in_dim(block, block.shape[dim] - width, None, axis=dim), axis, forward
        )
        high = lax.ppermute(lax.slice_in_dim(block, 0, width, axis=dim), axis, backward)
        block = jnp.concatenate([low, block, high], axis=dim)
    return block


def fine_laplace(padded):
    zpad = jnp.pad(padded, ((0, 0), (0, 0), (1, 1)))
    center = zpad[1:-1, 1:-1, 1:-1]
    total = zpad[2:, 1:-1, 1:-1] + zpad[:-2, 1:-1, 1:-1]
    total = total + zpad[1:-1, 2:, 1:-1] + zpad[1:-1, :-2, 1:-1]
    total = total + zpad[1:-1, 1:-1, 2:] + zpad[1:-1, 1:-1, :-2]
    return total - 6.0 * center


def advance(conc_pad, order_pad, mob_pad, last):
    chem = conc_pad - order_pad * order_pad * (3.0 - 2.0 * order_pad)
    conc_in = conc_pad[1:-1, 1:-1]
    order_in = order_pad[1:-1, 1:-1]
    chem_in = chem[1:-1, 1:-1]
    mobility = mob_pad[1:-1, 1:-1]
    conc_new = conc_in + rate_conc * fine_laplace(chem)
    dh_term = 6.0 * order_in * (1.0 - order_in)
    dg_term = 2.0 * order_in * (1.0 - order_in) * (1.0 - 2.0 * order_in)
    order_new = order_in + mobility * (
        rate_order * fine_laplace(order_pad)
        - well_height * dg_term
        + drive_coupling * chem_in * dh_term
    )
    if not last:
        conc_new = jnp.where(mobility > 0, conc_new, 0.0)
    return conc_new, order_new, mobility


def mobility_of(labels):
    return (0.5 * (labels == 0) + 1.0 * (labels == 1) + 0.25 * (labels == 2)).astype(jnp.float32)


def restrict_xzy(order_out):
    sx, sy, sz = order_out.shape
    sq = order_out * order_out
    sq = sq.reshape(sx // 2, 2, sy, sz).sum(axis=1)
    sq = sq.reshape(sx // 2, sy // 2, 2, sz).sum(axis=2)
    pairs = jnp.asarray(np.repeat(np.eye(sz // 2, dtype=np.float32), 2, axis=0))
    summed = jnp.einsum("xyz,zw->xwy", sq, pairs, precision=lax.Precision.HIGHEST)
    return 0.1 + 0.125 * summed


def y_shift(v, step):
    if step > 0:
        return jnp.pad(v[..., step:], [(0, 0)] * (v.ndim - 1) + [(0, step)])
    return jnp.pad(v[..., :step], [(0, 0)] * (v.ndim - 1) + [(-step, 0)])


def face_terms(stiff_pad):
    center = stiff_pad[1:-1, 1:-1]
    others = [stiff_pad[2:, 1:-1], stiff_pad[:-2, 1:-1], stiff_pad[1:-1, 2:], stiff_pad[1:-1, :-2],
              y_shift(center, 1), y_shift(center, -1)]
    faces = [0.5 * (center + other) for other in others]
    diag = faces[0] + faces[1] + faces[2] + faces[3] + faces[4] + faces[5] + spring_term * center
    return faces, diag, center


def neighbours(u_pad):
    center = u_pad[:, 1:-1, 1:-1]
    return center, [u_pad[:, 2:, 1:-1], u_pad[:, :-2, 1:-1], u_pad[:, 1:-1, 2:], u_pad[:, 1:-1, :-2],
                    y_shift(center, 1), y_shift(center, -1)]


def apply_op(u_pad, faces, diag):
    center, others = neighbours(u_pad)
    result = diag * center
    for face, other in zip(faces, others):
        result = result - face * other
    return result, center


def strain_energy(u_pad, faces):
    center, others = neighbours(u_pad)
    total = jnp.zeros(center.shape, jnp.float32)
    for face, other in zip(faces, others):
        diff = center - other
        total = total + face * diff * diff
    return 0.25 * jnp.sum(total, axis=0)


def on_device(concentration, order_field, phase_labels, displacement, body_load):
    h = FINE_HALO
    fields = jnp.stack([concentration, order_field, mobility_of(phase_labels)])
    fields = padded_2(fields, (("gx", 1), ("gy", 2)), h)
    conc, order, mob = fields[0], fields[1], fields[2]
    for step in range(STEPS):
        conc, order, mob = advance(conc, order, mob, step == STEPS - 1)

    m = MECH_HALO
    ub = padded_2(jnp.concatenate([displacement, body_load]), (("gx", 1), ("gy", 2)), m)
    disp, load = ub[:3], ub[3:]

    coarse = restrict_xzy(order)
    n = lax.axis_size("gy")
    cx, cz, cy = coarse.shape
    zc = cz // n
    src = coarse.reshape(cx, n, zc, cy).transpose(1, 0, 2, 3).reshape(n, cx, zc * cy)
    got = all_to_all_gy(src, 0)
    stiff = got.reshape(n, cx, zc, cy).transpose(1, 2, 0, 3).reshape(cx, zc, n * cy)
    stiff_pad = padded_2(stiff, (("gx", 0), ("gy", 1)), m)

    faces, diag, center = face_terms(stiff_pad)
    for weight in (first_weight, second_weight):
        load = load[:, 1:-1, 1:-1]
        result, u_c = apply_op(disp, faces, diag)
        new = u_c + weight * (load - result) / diag
        disp = jnp.where(center > 0, new, 0.0)
        faces = [f[1:-1, 1:-1] for f in faces]
        diag = diag[1:-1, 1:-1]
        center = center[1:-1, 1:-1]
    energy = strain_energy(disp, faces)
    disp = disp[:, 1:-1, 1:-1]
    src = energy.reshape(cx, zc, n, cy).transpose(2, 0, 1, 3).reshape(n, cx, zc * cy)
    got = all_to_all_gy(src, 1)
    tiles = got.reshape(n, cx, zc, cy).transpose(1, 3, 0, 2).reshape(cx, cy, n * zc)
    return (conc, order, disp, tiles)


def solution(mesh):
    return jax.shard_map(
        on_device,
        mesh=mesh,
        in_specs=(
            P("gx", "gy", None),
            P("gx", "gy", None),
            P("gx", "gy", None),
            P(None, "gx", "gy", None),
            P(None, "gx", "gy", None),
        ),
        out_specs=(
            P("gx", "gy", None),
            P("gx", "gy", None),
            P(None, "gx", "gy", None),
            P("gx", "gy", None),
        ),
        check_vma=False,
    )
```

```python
import jax
import jax.numpy as jnp
import numpy as np
from jax import lax
from jax.sharding import PartitionSpec as P

STEPS = 4
FINE_HALO = 4
MECH_HALO = 3

rate_conc = 0.15
rate_order = 0.15
well_height = 1.0
drive_coupling = 0.5
spring_term = 0.2
first_weight = 0.5956
second_weight = 2.695


def padded_2(block, sides, width):
    for axis, dim in sides:
        count = lax.axis_size(axis)
        forward = [(i, i + 1) for i in range(count - 1)]
        backward = [(target, source) for source, target in forward]
        low = lax.ppermute(
            lax.slice_in_dim(block, block.shape[dim] - width, None, axis=dim), axis, forward
        )
        high = lax.ppermute(lax.slice_in_dim(block, 0, width, axis=dim), axis, backward)
        block = jnp.concatenate([low, block, high], axis=dim)
    return block


def fine_laplace(padded):
    zpad = jnp.pad(padded, ((0, 0), (0, 0), (1, 1)))
    center = zpad[1:-1, 1:-1, 1:-1]
    total = zpad[2:, 1:-1, 1:-1] + zpad[:-2, 1:-1, 1:-1]
    total = total + zpad[1:-1, 2:, 1:-1] + zpad[1:-1, :-2, 1:-1]
    total = total + zpad[1:-1, 1:-1, 2:] + zpad[1:-1, 1:-1, :-2]
    return total - 6.0 * center


def advance(conc_pad, order_pad, mob_pad, last):
    chem = conc_pad - order_pad * order_pad * (3.0 - 2.0 * order_pad)
    conc_in = conc_pad[1:-1, 1:-1]
    order_in = order_pad[1:-1, 1:-1]
    chem_in = chem[1:-1, 1:-1]
    mobility = mob_pad[1:-1, 1:-1]
    conc_new = conc_in + rate_conc * fine_laplace(chem)
    dh_term = 6.0 * order_in * (1.0 - order_in)
    dg_term = 2.0 * order_in * (1.0 - order_in) * (1.0 - 2.0 * order_in)
    order_new = order_in + mobility * (
        rate_order * fine_laplace(order_pad)
        - well_height * dg_term
        + drive_coupling * chem_in * dh_term
    )
    if not last:
        conc_new = jnp.where(mobility > 0, conc_new, 0.0)
    return conc_new, order_new, mobility


def mobility_of(labels):
    return (0.5 * (labels == 0) + 1.0 * (labels == 1) + 0.25 * (labels == 2)).astype(jnp.float32)


def restrict_xzy(order_out):
    sx, sy, sz = order_out.shape
    sq = order_out * order_out
    sq = sq.reshape(sx // 2, 2, sy, sz).sum(axis=1)
    sq = sq.reshape(sx // 2, sy // 2, 2, sz).sum(axis=2)
    pairs = jnp.asarray(np.repeat(np.eye(sz // 2, dtype=np.float32), 2, axis=0))
    summed = jnp.einsum("xyz,zw->xwy", sq, pairs, precision=lax.Precision.HIGHEST)
    return 0.1 + 0.125 * summed


def y_shift(v, step):
    if step > 0:
        return jnp.pad(v[..., step:], [(0, 0)] * (v.ndim - 1) + [(0, step)])
    return jnp.pad(v[..., :step], [(0, 0)] * (v.ndim - 1) + [(-step, 0)])


def face_terms(stiff_pad):
    center = stiff_pad[1:-1, 1:-1]
    others = [stiff_pad[2:, 1:-1], stiff_pad[:-2, 1:-1], stiff_pad[1:-1, 2:], stiff_pad[1:-1, :-2],
              y_shift(center, 1), y_shift(center, -1)]
    faces = [0.5 * (center + other) for other in others]
    diag = faces[0] + faces[1] + faces[2] + faces[3] + faces[4] + faces[5] + spring_term * center
    return faces, diag, center


def neighbours(u_pad):
    center = u_pad[:, 1:-1, 1:-1]
    return center, [u_pad[:, 2:, 1:-1], u_pad[:, :-2, 1:-1], u_pad[:, 1:-1, 2:], u_pad[:, 1:-1, :-2],
                    y_shift(center, 1), y_shift(center, -1)]


def apply_op(u_pad, faces, diag):
    center, others = neighbours(u_pad)
    result = diag * center
    for face, other in zip(faces, others):
        result = result - face * other
    return result, center


def strain_energy(u_pad, faces):
    center, others = neighbours(u_pad)
    total = jnp.zeros(center.shape, jnp.float32)
    for face, other in zip(faces, others):
        diff = center - other
        total = total + face * diff * diff
    return 0.25 * jnp.sum(total, axis=0)


def on_device(concentration, order_field, phase_labels, displacement, body_load):
    h = FINE_HALO
    m = MECH_HALO
    hx = h + 2 * m
    fields = jnp.stack([concentration, order_field, mobility_of(phase_labels)])
    fields = padded_2(fields, (("gx", 1),), hx)
    fields = padded_2(fields, (("gy", 2),), h)
    conc, order, mob = fields[0], fields[1], fields[2]
    for step in range(STEPS):
        conc, order, mob = advance(conc, order, mob, step == STEPS - 1)
    fx = concentration.shape[0]
    conc = conc[2 * m:2 * m + fx]
    order_x = order
    order = order[2 * m:2 * m + fx]

    ub = padded_2(jnp.concatenate([displacement, body_load]), (("gx", 1), ("gy", 2)), m)
    disp, load = ub[:3], ub[3:]

    coarse = restrict_xzy(order_x)
    cx, cz, cy = coarse.shape
    bx = cx - 2 * m
    n = lax.axis_size("gy")
    gxi = lax.axis_index("gx")
    xg = gxi * bx - m + lax.broadcasted_iota(jnp.int32, (cx, 1, 1), 0)
    coarse = jnp.where((xg >= 0) & (xg < bx * lax.axis_size("gx")), coarse, 0.0)
    zc = cz // n
    zpad = jnp.pad(coarse, ((0, 0), (m, m), (0, 0)))
    windows = jnp.stack([zpad[:, j * zc:j * zc + zc + 2 * m] for j in range(n)])
    got = lax.all_to_all(windows, "gy", split_axis=0, concat_axis=0, tiled=True)
    stiff_pad = got.transpose(1, 2, 0, 3).reshape(cx, zc + 2 * m, n * cy)

    faces, diag, center = face_terms(stiff_pad)
    for weight in (first_weight, second_weight):
        load = load[:, 1:-1, 1:-1]
        result, u_c = apply_op(disp, faces, diag)
        new = u_c + weight * (load - result) / diag
        disp = jnp.where(center > 0, new, 0.0)
        faces = [f[1:-1, 1:-1] for f in faces]
        diag = diag[1:-1, 1:-1]
        center = center[1:-1, 1:-1]
    energy = strain_energy(disp, faces)
    disp = disp[:, 1:-1, 1:-1]
    tiles = lax.all_to_all(energy, "gy", split_axis=2, concat_axis=1, tiled=True)
    return (conc, order, disp, jnp.transpose(tiles, (0, 2, 1)))


def solution(mesh):
    return jax.shard_map(
        on_device,
        mesh=mesh,
        in_specs=(
            P("gx", "gy", None),
            P("gx", "gy", None),
            P("gx", "gy", None),
            P(None, "gx", "gy", None),
            P(None, "gx", "gy", None),
        ),
        out_specs=(
            P("gx", "gy", None),
            P("gx", "gy", None),
            P(None, "gx", "gy", None),
            P("gx", "gy", None),
        ),
        check_vma=False,
    )
```

```python
import jax
import jax.numpy as jnp
import functools

import numpy as np
from jax import lax
from jax.experimental import pallas as pl
from jax.experimental.pallas import tpu as pltpu
from jax.sharding import PartitionSpec as P

STEPS = 4
FINE_HALO = 4
MECH_HALO = 3

rate_conc = 0.15
rate_order = 0.15
well_height = 1.0
drive_coupling = 0.5
spring_term = 0.2
first_weight = 0.5956
second_weight = 2.695


MESH = pl.DeviceIdType.MESH
TILE = 8
DIRS = [(sx, sy) for sx in (-1, 0, 1) for sy in (-1, 0, 1) if (sx, sy) != (0, 0)]


def _src_window(side, size, width):
    return {1: slice(size - width, size), -1: slice(0, width), 0: slice(0, size)}[side]


def _dst_window(side, size, width):
    return {1: slice(0, width), -1: slice(width + size, size + 2 * width), 0: slice(width, width + size)}[side]


def halo_kernel(hx, nx, ny, blk_ref, out_ref, ext, send_sem, recv_sem):
    c, x, y, z = blk_ref.shape
    t = TILE
    gx = lax.axis_index("gx")
    gy = lax.axis_index("gy")

    def exists(sx, sy):
        return (gx + sx >= 0) & (gx + sx < nx) & (gy + sy >= 0) & (gy + sy < ny)

    barrier = pltpu.get_barrier_semaphore()
    for sx, sy in DIRS:
        @pl.when(exists(sx, sy))
        def _():
            pl.semaphore_signal(barrier, inc=1, device_id=(gx + sx, gy + sy), device_id_type=MESH)
    row = (gx + nx - 1) // nx + 1 + (2 * nx - 2 - gx) // nx
    col = (gy + ny - 1) // ny + 1 + (2 * ny - 2 - gy) // ny
    pl.semaphore_wait(barrier, row * col - 1)

    copies = []
    for k, (sx, sy) in enumerate(DIRS):
        copy = pltpu.make_async_remote_copy(
            src_ref=blk_ref.at[:, _src_window(sx, x, hx), _src_window(sy, y, t), :],
            dst_ref=ext.at[:, _dst_window(sx, x, hx), _dst_window(sy, y, t), :],
            send_sem=send_sem.at[k],
            recv_sem=recv_sem.at[k],
            device_id=(lax.rem(gx + sx + nx, nx), lax.rem(gy + sy + ny, ny)),
            device_id_type=MESH,
        )
        copies.append(copy)

        @pl.when(exists(sx, sy))
        def _():
            copy.start()

    ext[:, hx:hx + x, t:t + y, :] = blk_ref[...]
    for sx, sy in DIRS:
        xs, ys = _dst_window(sx, x, hx), _dst_window(sy, y, t)

        @pl.when(jnp.logical_not(exists(-sx, -sy)))
        def _():
            ext[:, xs, ys, :] = jnp.zeros((c, xs.stop - xs.start, ys.stop - ys.start, z), ext.dtype)

    for (sx, sy), copy in zip(DIRS, copies):
        @pl.when(exists(sx, sy))
        def _():
            copy.wait_send()

        @pl.when(exists(-sx, -sy))
        def _():
            copy.wait_recv()
    out_ref[...] = ext[...]


def halo_exchange(block, hx, cid):
    c, x, y, z = block.shape
    nx, ny = lax.axis_size("gx"), lax.axis_size("gy")
    shape = (c, x + 2 * hx, y + 2 * TILE, z)
    return pl.pallas_call(
        functools.partial(halo_kernel, hx, nx, ny),
        out_shape=jax.ShapeDtypeStruct(shape, block.dtype),
        in_specs=[pl.BlockSpec(memory_space=pltpu.VMEM)],
        out_specs=pl.BlockSpec(memory_space=pltpu.VMEM),
        scratch_shapes=[
            pltpu.VMEM(shape, block.dtype),
            pltpu.SemaphoreType.DMA((len(DIRS),)),
            pltpu.SemaphoreType.DMA((len(DIRS),)),
        ],
        compiler_params=pltpu.CompilerParams(collective_id=cid, has_side_effects=True),
    )(block)


def padded_2(block, sides, width):
    for axis, dim in sides:
        count = lax.axis_size(axis)
        forward = [(i, i + 1) for i in range(count - 1)]
        backward = [(target, source) for source, target in forward]
        low = lax.ppermute(
            lax.slice_in_dim(block, block.shape[dim] - width, None, axis=dim), axis, forward
        )
        high = lax.ppermute(lax.slice_in_dim(block, 0, width, axis=dim), axis, backward)
        block = jnp.concatenate([low, block, high], axis=dim)
    return block


def fine_laplace(padded):
    zpad = jnp.pad(padded, ((0, 0), (0, 0), (1, 1)))
    center = zpad[1:-1, 1:-1, 1:-1]
    total = zpad[2:, 1:-1, 1:-1] + zpad[:-2, 1:-1, 1:-1]
    total = total + zpad[1:-1, 2:, 1:-1] + zpad[1:-1, :-2, 1:-1]
    total = total + zpad[1:-1, 1:-1, 2:] + zpad[1:-1, 1:-1, :-2]
    return total - 6.0 * center


def advance(conc_pad, order_pad, mob_pad, last):
    chem = conc_pad - order_pad * order_pad * (3.0 - 2.0 * order_pad)
    conc_in = conc_pad[1:-1, 1:-1]
    order_in = order_pad[1:-1, 1:-1]
    chem_in = chem[1:-1, 1:-1]
    mobility = mob_pad[1:-1, 1:-1]
    conc_new = conc_in + rate_conc * fine_laplace(chem)
    dh_term = 6.0 * order_in * (1.0 - order_in)
    dg_term = 2.0 * order_in * (1.0 - order_in) * (1.0 - 2.0 * order_in)
    order_new = order_in + mobility * (
        rate_order * fine_laplace(order_pad)
        - well_height * dg_term
        + drive_coupling * chem_in * dh_term
    )
    if not last:
        conc_new = jnp.where(mobility > 0, conc_new, 0.0)
    return conc_new, order_new, mobility


def mobility_of(labels):
    return (0.5 * (labels == 0) + 1.0 * (labels == 1) + 0.25 * (labels == 2)).astype(jnp.float32)


def restrict_xzy(order_out):
    sx, sy, sz = order_out.shape
    sq = order_out * order_out
    sq = sq.reshape(sx // 2, 2, sy, sz).sum(axis=1)
    sq = sq.reshape(sx // 2, sy // 2, 2, sz).sum(axis=2)
    pairs = jnp.asarray(np.repeat(np.eye(sz // 2, dtype=np.float32), 2, axis=0))
    summed = jnp.einsum("xyz,zw->xwy", sq, pairs, precision=lax.Precision.HIGHEST)
    return 0.1 + 0.125 * summed


def y_shift(v, step):
    if step > 0:
        return jnp.pad(v[..., step:], [(0, 0)] * (v.ndim - 1) + [(0, step)])
    return jnp.pad(v[..., :step], [(0, 0)] * (v.ndim - 1) + [(-step, 0)])


def face_terms(stiff_pad):
    center = stiff_pad[1:-1, 1:-1]
    others = [stiff_pad[2:, 1:-1], stiff_pad[:-2, 1:-1], stiff_pad[1:-1, 2:], stiff_pad[1:-1, :-2],
              y_shift(center, 1), y_shift(center, -1)]
    faces = [0.5 * (center + other) for other in others]
    diag = faces[0] + faces[1] + faces[2] + faces[3] + faces[4] + faces[5] + spring_term * center
    return faces, diag, center


def neighbours(u_pad):
    center = u_pad[:, 1:-1, 1:-1]
    return center, [u_pad[:, 2:, 1:-1], u_pad[:, :-2, 1:-1], u_pad[:, 1:-1, 2:], u_pad[:, 1:-1, :-2],
                    y_shift(center, 1), y_shift(center, -1)]


def apply_op(u_pad, faces, diag):
    center, others = neighbours(u_pad)
    result = diag * center
    for face, other in zip(faces, others):
        result = result - face * other
    return result, center


def strain_energy(u_pad, faces):
    center, others = neighbours(u_pad)
    total = jnp.zeros(center.shape, jnp.float32)
    for face, other in zip(faces, others):
        diff = center - other
        total = total + face * diff * diff
    return 0.25 * jnp.sum(total, axis=0)


def on_device(concentration, order_field, phase_labels, displacement, body_load):
    h = FINE_HALO
    fields = jnp.stack([concentration, order_field, mobility_of(phase_labels)])
    fields = halo_exchange(fields, h, 0)[:, :, TILE - h:TILE - h + fields.shape[2] + 2 * h]
    conc, order, mob = fields[0], fields[1], fields[2]
    for step in range(STEPS):
        conc, order, mob = advance(conc, order, mob, step == STEPS - 1)

    m = MECH_HALO
    ub = padded_2(jnp.concatenate([displacement, body_load]), (("gx", 1), ("gy", 2)), m)
    disp, load = ub[:3], ub[3:]

    coarse = restrict_xzy(order)
    stiff = lax.all_to_all(coarse, "gy", split_axis=1, concat_axis=2, tiled=True)
    stiff_pad = halo_exchange(stiff[None], m, 1)[0, :, TILE - m:TILE - m + stiff.shape[1] + 2 * m]

    faces, diag, center = face_terms(stiff_pad)
    for weight in (first_weight, second_weight):
        load = load[:, 1:-1, 1:-1]
        result, u_c = apply_op(disp, faces, diag)
        new = u_c + weight * (load - result) / diag
        disp = jnp.where(center > 0, new, 0.0)
        faces = [f[1:-1, 1:-1] for f in faces]
        diag = diag[1:-1, 1:-1]
        center = center[1:-1, 1:-1]
    energy = strain_energy(disp, faces)
    disp = disp[:, 1:-1, 1:-1]
    tiles = lax.all_to_all(energy, "gy", split_axis=2, concat_axis=1, tiled=True)
    return (conc, order, disp, jnp.transpose(tiles, (0, 2, 1)))


def solution(mesh):
    return jax.shard_map(
        on_device,
        mesh=mesh,
        in_specs=(
            P("gx", "gy", None),
            P("gx", "gy", None),
            P("gx", "gy", None),
            P(None, "gx", "gy", None),
            P(None, "gx", "gy", None),
        ),
        out_specs=(
            P("gx", "gy", None),
            P("gx", "gy", None),
            P(None, "gx", "gy", None),
            P("gx", "gy", None),
        ),
        check_vma=False,
    )
```

```python
import jax
import jax.numpy as jnp
import functools

import numpy as np
from jax import lax
from jax.experimental import pallas as pl
from jax.experimental.pallas import tpu as pltpu
from jax.sharding import PartitionSpec as P

STEPS = 4
FINE_HALO = 4
MECH_HALO = 3

rate_conc = 0.15
rate_order = 0.15
well_height = 1.0
drive_coupling = 0.5
spring_term = 0.2
first_weight = 0.5956
second_weight = 2.695


MESH = pl.DeviceIdType.MESH
TILE = 8
DIRS = [(sx, sy) for sx in (-1, 0, 1) for sy in (-1, 0, 1) if (sx, sy) != (0, 0)]


def _src_window(side, size, width):
    return {1: slice(size - width, size), -1: slice(0, width), 0: slice(0, size)}[side]


def _dst_window(side, size, width):
    return {1: slice(0, width), -1: slice(width + size, size + 2 * width), 0: slice(width, width + size)}[side]


def halo_kernel(hx, nx, ny, blk_ref, out_ref, ext, send_sem, recv_sem):
    c, x, y, z = blk_ref.shape
    t = TILE
    gx = lax.axis_index("gx")
    gy = lax.axis_index("gy")

    def exists(sx, sy):
        return (gx + sx >= 0) & (gx + sx < nx) & (gy + sy >= 0) & (gy + sy < ny)

    barrier = pltpu.get_barrier_semaphore()
    for sx, sy in DIRS:
        @pl.when(exists(sx, sy))
        def _():
            pl.semaphore_signal(barrier, inc=1, device_id=(gx + sx, gy + sy), device_id_type=MESH)
    row = (gx + nx - 1) // nx + 1 + (2 * nx - 2 - gx) // nx
    col = (gy + ny - 1) // ny + 1 + (2 * ny - 2 - gy) // ny
    pl.semaphore_wait(barrier, row * col - 1)

    copies = []
    for k, (sx, sy) in enumerate(DIRS):
        copy = pltpu.make_async_remote_copy(
            src_ref=blk_ref.at[:, _src_window(sx, x, hx), _src_window(sy, y, t), :],
            dst_ref=ext.at[:, _dst_window(sx, x, hx), _dst_window(sy, y, t), :],
            send_sem=send_sem.at[k],
            recv_sem=recv_sem.at[k],
            device_id=(lax.rem(gx + sx + nx, nx), lax.rem(gy + sy + ny, ny)),
            device_id_type=MESH,
        )
        copies.append(copy)

        @pl.when(exists(sx, sy))
        def _():
            copy.start()

    ext[:, hx:hx + x, t:t + y, :] = blk_ref[...]
    for sx, sy in DIRS:
        xs, ys = _dst_window(sx, x, hx), _dst_window(sy, y, t)

        @pl.when(jnp.logical_not(exists(-sx, -sy)))
        def _():
            ext[:, xs, ys, :] = jnp.zeros((c, xs.stop - xs.start, ys.stop - ys.start, z), ext.dtype)

    for (sx, sy), copy in zip(DIRS, copies):
        @pl.when(exists(sx, sy))
        def _():
            copy.wait_send()

        @pl.when(exists(-sx, -sy))
        def _():
            copy.wait_recv()
    out_ref[...] = ext[...]


def halo_exchange(block, hx, cid):
    c, x, y, z = block.shape
    nx, ny = lax.axis_size("gx"), lax.axis_size("gy")
    shape = (c, x + 2 * hx, y + 2 * TILE, z)
    return pl.pallas_call(
        functools.partial(halo_kernel, hx, nx, ny),
        out_shape=jax.ShapeDtypeStruct(shape, block.dtype),
        in_specs=[pl.BlockSpec(memory_space=pltpu.VMEM)],
        out_specs=pl.BlockSpec(memory_space=pltpu.VMEM),
        scratch_shapes=[
            pltpu.VMEM(shape, block.dtype),
            pltpu.SemaphoreType.DMA((len(DIRS),)),
            pltpu.SemaphoreType.DMA((len(DIRS),)),
        ],
        compiler_params=pltpu.CompilerParams(collective_id=cid, has_side_effects=True),
    )(block)


def padded_2(block, sides, width):
    for axis, dim in sides:
        count = lax.axis_size(axis)
        forward = [(i, i + 1) for i in range(count - 1)]
        backward = [(target, source) for source, target in forward]
        low = lax.ppermute(
            lax.slice_in_dim(block, block.shape[dim] - width, None, axis=dim), axis, forward
        )
        high = lax.ppermute(lax.slice_in_dim(block, 0, width, axis=dim), axis, backward)
        block = jnp.concatenate([low, block, high], axis=dim)
    return block


def fine_laplace(padded):
    zpad = jnp.pad(padded, ((0, 0), (0, 0), (1, 1)))
    center = zpad[1:-1, 1:-1, 1:-1]
    total = zpad[2:, 1:-1, 1:-1] + zpad[:-2, 1:-1, 1:-1]
    total = total + zpad[1:-1, 2:, 1:-1] + zpad[1:-1, :-2, 1:-1]
    total = total + zpad[1:-1, 1:-1, 2:] + zpad[1:-1, 1:-1, :-2]
    return total - 6.0 * center


def advance(conc_pad, order_pad, mob_pad, last):
    chem = conc_pad - order_pad * order_pad * (3.0 - 2.0 * order_pad)
    conc_in = conc_pad[1:-1, 1:-1]
    order_in = order_pad[1:-1, 1:-1]
    chem_in = chem[1:-1, 1:-1]
    mobility = mob_pad[1:-1, 1:-1]
    conc_new = conc_in + rate_conc * fine_laplace(chem)
    dh_term = 6.0 * order_in * (1.0 - order_in)
    dg_term = 2.0 * order_in * (1.0 - order_in) * (1.0 - 2.0 * order_in)
    order_new = order_in + mobility * (
        rate_order * fine_laplace(order_pad)
        - well_height * dg_term
        + drive_coupling * chem_in * dh_term
    )
    if not last:
        conc_new = jnp.where(mobility > 0, conc_new, 0.0)
    return conc_new, order_new, mobility


def mobility_of(labels):
    return (0.5 * (labels == 0) + 1.0 * (labels == 1) + 0.25 * (labels == 2)).astype(jnp.float32)


def restrict_xzy(order_out):
    sx, sy, sz = order_out.shape
    sq = order_out * order_out
    sq = sq.reshape(sx // 2, 2, sy, sz).sum(axis=1)
    sq = sq.reshape(sx // 2, sy // 2, 2, sz).sum(axis=2)
    pairs = jnp.asarray(np.repeat(np.eye(sz // 2, dtype=np.float32), 2, axis=0))
    summed = jnp.einsum("xyz,zw->xwy", sq, pairs, precision=lax.Precision.HIGHEST)
    return 0.1 + 0.125 * summed


def y_shift(v, step):
    if step > 0:
        return jnp.pad(v[..., step:], [(0, 0)] * (v.ndim - 1) + [(0, step)])
    return jnp.pad(v[..., :step], [(0, 0)] * (v.ndim - 1) + [(-step, 0)])


def face_terms(stiff_pad):
    center = stiff_pad[1:-1, 1:-1]
    others = [stiff_pad[2:, 1:-1], stiff_pad[:-2, 1:-1], stiff_pad[1:-1, 2:], stiff_pad[1:-1, :-2],
              y_shift(center, 1), y_shift(center, -1)]
    faces = [0.5 * (center + other) for other in others]
    diag = faces[0] + faces[1] + faces[2] + faces[3] + faces[4] + faces[5] + spring_term * center
    return faces, diag, center


def neighbours(u_pad):
    center = u_pad[:, 1:-1, 1:-1]
    return center, [u_pad[:, 2:, 1:-1], u_pad[:, :-2, 1:-1], u_pad[:, 1:-1, 2:], u_pad[:, 1:-1, :-2],
                    y_shift(center, 1), y_shift(center, -1)]


def apply_op(u_pad, faces, diag):
    center, others = neighbours(u_pad)
    result = diag * center
    for face, other in zip(faces, others):
        result = result - face * other
    return result, center


def strain_energy(u_pad, faces):
    center, others = neighbours(u_pad)
    total = jnp.zeros(center.shape, jnp.float32)
    for face, other in zip(faces, others):
        diff = center - other
        total = total + face * diff * diff
    return 0.25 * jnp.sum(total, axis=0)


def on_device(concentration, order_field, phase_labels, displacement, body_load):
    h = FINE_HALO
    fields = jnp.stack([concentration, order_field, mobility_of(phase_labels)])
    fields = padded_2(fields, (("gx", 1), ("gy", 2)), h)
    conc, order, mob = fields[0], fields[1], fields[2]
    for step in range(STEPS):
        conc, order, mob = advance(conc, order, mob, step == STEPS - 1)

    m = MECH_HALO
    ub = padded_2(jnp.concatenate([displacement, body_load]), (("gx", 1), ("gy", 2)), m)
    disp, load = ub[:3], ub[3:]

    coarse = restrict_xzy(order)
    stiff = lax.all_to_all(coarse, "gy", split_axis=1, concat_axis=2, tiled=True)
    stiff_pad = halo_exchange(stiff[None], m, 0)[0, :, TILE - m:TILE - m + stiff.shape[1] + 2 * m]

    faces, diag, center = face_terms(stiff_pad)
    for weight in (first_weight, second_weight):
        load = load[:, 1:-1, 1:-1]
        result, u_c = apply_op(disp, faces, diag)
        new = u_c + weight * (load - result) / diag
        disp = jnp.where(center > 0, new, 0.0)
        faces = [f[1:-1, 1:-1] for f in faces]
        diag = diag[1:-1, 1:-1]
        center = center[1:-1, 1:-1]
    energy = strain_energy(disp, faces)
    disp = disp[:, 1:-1, 1:-1]
    tiles = lax.all_to_all(energy, "gy", split_axis=2, concat_axis=1, tiled=True)
    return (conc, order, disp, jnp.transpose(tiles, (0, 2, 1)))


def solution(mesh):
    return jax.shard_map(
        on_device,
        mesh=mesh,
        in_specs=(
            P("gx", "gy", None),
            P("gx", "gy", None),
            P("gx", "gy", None),
            P(None, "gx", "gy", None),
            P(None, "gx", "gy", None),
        ),
        out_specs=(
            P("gx", "gy", None),
            P("gx", "gy", None),
            P(None, "gx", "gy", None),
            P("gx", "gy", None),
        ),
        check_vma=False,
    )
```

```python
import jax
import jax.numpy as jnp
import functools

import numpy as np
from jax import lax
from jax.experimental import pallas as pl
from jax.experimental.pallas import tpu as pltpu
from jax.sharding import PartitionSpec as P

STEPS = 4
FINE_HALO = 4
MECH_HALO = 3

rate_conc = 0.15
rate_order = 0.15
well_height = 1.0
drive_coupling = 0.5
spring_term = 0.2
first_weight = 0.5956
second_weight = 2.695


MESH = pl.DeviceIdType.MESH
TILE = 8
DIRS = [(sx, sy) for sx in (-1, 0, 1) for sy in (-1, 0, 1) if (sx, sy) != (0, 0)]


def _src_window(side, size, width):
    return {1: slice(size - width, size), -1: slice(0, width), 0: slice(0, size)}[side]


def _dst_window(side, size, width):
    return {1: slice(0, width), -1: slice(width + size, size + 2 * width), 0: slice(width, width + size)}[side]


def halo_kernel(hx, nx, ny, blk_ref, out_ref, ext, send_sem, recv_sem):
    c, x, y, z = blk_ref.shape
    t = TILE
    gx = lax.axis_index("gx")
    gy = lax.axis_index("gy")

    def exists(sx, sy):
        return (gx + sx >= 0) & (gx + sx < nx) & (gy + sy >= 0) & (gy + sy < ny)

    barrier = pltpu.get_barrier_semaphore()
    for sx, sy in DIRS:
        @pl.when(exists(sx, sy))
        def _():
            pl.semaphore_signal(barrier, inc=1, device_id=(gx + sx, gy + sy), device_id_type=MESH)
    row = (gx + nx - 1) // nx + 1 + (2 * nx - 2 - gx) // nx
    col = (gy + ny - 1) // ny + 1 + (2 * ny - 2 - gy) // ny
    pl.semaphore_wait(barrier, row * col - 1)

    copies = []
    for k, (sx, sy) in enumerate(DIRS):
        copy = pltpu.make_async_remote_copy(
            src_ref=blk_ref.at[:, _src_window(sx, x, hx), _src_window(sy, y, t), :],
            dst_ref=ext.at[:, _dst_window(sx, x, hx), _dst_window(sy, y, t), :],
            send_sem=send_sem.at[k],
            recv_sem=recv_sem.at[k],
            device_id=(lax.rem(gx + sx + nx, nx), lax.rem(gy + sy + ny, ny)),
            device_id_type=MESH,
        )
        copies.append(copy)

        @pl.when(exists(sx, sy))
        def _():
            copy.start()

    ext[:, hx:hx + x, t:t + y, :] = blk_ref[...]
    for sx, sy in DIRS:
        xs, ys = _dst_window(sx, x, hx), _dst_window(sy, y, t)

        @pl.when(jnp.logical_not(exists(-sx, -sy)))
        def _():
            ext[:, xs, ys, :] = jnp.zeros((c, xs.stop - xs.start, ys.stop - ys.start, z), ext.dtype)

    for (sx, sy), copy in zip(DIRS, copies):
        @pl.when(exists(sx, sy))
        def _():
            copy.wait_send()

        @pl.when(exists(-sx, -sy))
        def _():
            copy.wait_recv()
    out_ref[...] = ext[...]


def halo_exchange(block, hx, cid):
    c, x, y, z = block.shape
    nx, ny = lax.axis_size("gx"), lax.axis_size("gy")
    shape = (c, x + 2 * hx, y + 2 * TILE, z)
    return pl.pallas_call(
        functools.partial(halo_kernel, hx, nx, ny),
        out_shape=jax.ShapeDtypeStruct(shape, block.dtype),
        in_specs=[pl.BlockSpec(memory_space=pltpu.VMEM)],
        out_specs=pl.BlockSpec(memory_space=pltpu.VMEM),
        scratch_shapes=[
            pltpu.VMEM(shape, block.dtype),
            pltpu.SemaphoreType.DMA((len(DIRS),)),
            pltpu.SemaphoreType.DMA((len(DIRS),)),
        ],
        compiler_params=pltpu.CompilerParams(collective_id=cid, has_side_effects=True),
    )(block)


def padded_2(block, sides, width):
    for axis, dim in sides:
        count = lax.axis_size(axis)
        forward = [(i, i + 1) for i in range(count - 1)]
        backward = [(target, source) for source, target in forward]
        low = lax.ppermute(
            lax.slice_in_dim(block, block.shape[dim] - width, None, axis=dim), axis, forward
        )
        high = lax.ppermute(lax.slice_in_dim(block, 0, width, axis=dim), axis, backward)
        block = jnp.concatenate([low, block, high], axis=dim)
    return block


def fine_laplace(padded):
    zpad = jnp.pad(padded, ((0, 0), (0, 0), (1, 1)))
    center = zpad[1:-1, 1:-1, 1:-1]
    total = zpad[2:, 1:-1, 1:-1] + zpad[:-2, 1:-1, 1:-1]
    total = total + zpad[1:-1, 2:, 1:-1] + zpad[1:-1, :-2, 1:-1]
    total = total + zpad[1:-1, 1:-1, 2:] + zpad[1:-1, 1:-1, :-2]
    return total - 6.0 * center


def advance(conc_pad, order_pad, mob_pad, last):
    chem = conc_pad - order_pad * order_pad * (3.0 - 2.0 * order_pad)
    conc_in = conc_pad[1:-1, 1:-1]
    order_in = order_pad[1:-1, 1:-1]
    chem_in = chem[1:-1, 1:-1]
    mobility = mob_pad[1:-1, 1:-1]
    conc_new = conc_in + rate_conc * fine_laplace(chem)
    dh_term = 6.0 * order_in * (1.0 - order_in)
    dg_term = 2.0 * order_in * (1.0 - order_in) * (1.0 - 2.0 * order_in)
    order_new = order_in + mobility * (
        rate_order * fine_laplace(order_pad)
        - well_height * dg_term
        + drive_coupling * chem_in * dh_term
    )
    if not last:
        conc_new = jnp.where(mobility > 0, conc_new, 0.0)
    return conc_new, order_new, mobility


def mobility_of(labels):
    return (0.5 * (labels == 0) + 1.0 * (labels == 1) + 0.25 * (labels == 2)).astype(jnp.float32)


def restrict_xzy(order_out):
    sx, sy, sz = order_out.shape
    sq = order_out * order_out
    sq = sq.reshape(sx // 2, 2, sy, sz).sum(axis=1)
    sq = sq.reshape(sx // 2, sy // 2, 2, sz).sum(axis=2)
    pairs = jnp.asarray(np.repeat(np.eye(sz // 2, dtype=np.float32), 2, axis=0))
    summed = jnp.einsum("xyz,zw->xwy", sq, pairs, precision=lax.Precision.HIGHEST)
    return 0.1 + 0.125 * summed


def y_shift(v, step):
    if step > 0:
        return jnp.pad(v[..., step:], [(0, 0)] * (v.ndim - 1) + [(0, step)])
    return jnp.pad(v[..., :step], [(0, 0)] * (v.ndim - 1) + [(-step, 0)])


def face_terms(stiff_pad):
    center = stiff_pad[1:-1, 1:-1]
    others = [stiff_pad[2:, 1:-1], stiff_pad[:-2, 1:-1], stiff_pad[1:-1, 2:], stiff_pad[1:-1, :-2],
              y_shift(center, 1), y_shift(center, -1)]
    faces = [0.5 * (center + other) for other in others]
    diag = faces[0] + faces[1] + faces[2] + faces[3] + faces[4] + faces[5] + spring_term * center
    return faces, diag, center


def neighbours(u_pad):
    center = u_pad[:, 1:-1, 1:-1]
    return center, [u_pad[:, 2:, 1:-1], u_pad[:, :-2, 1:-1], u_pad[:, 1:-1, 2:], u_pad[:, 1:-1, :-2],
                    y_shift(center, 1), y_shift(center, -1)]


def apply_op(u_pad, faces, diag):
    center, others = neighbours(u_pad)
    result = diag * center
    for face, other in zip(faces, others):
        result = result - face * other
    return result, center


def strain_energy(u_pad, faces):
    center, others = neighbours(u_pad)
    total = jnp.zeros(center.shape, jnp.float32)
    for face, other in zip(faces, others):
        diff = center - other
        total = total + face * diff * diff
    return 0.25 * jnp.sum(total, axis=0)


def on_device(concentration, order_field, phase_labels, displacement, body_load):
    h = FINE_HALO
    fields = jnp.stack([concentration, order_field, mobility_of(phase_labels)])
    fields = padded_2(fields, (("gx", 1), ("gy", 2)), h)
    conc, order, mob = fields[0], fields[1], fields[2]
    for step in range(STEPS):
        conc, order, mob = advance(conc, order, mob, step == STEPS - 1)

    m = MECH_HALO
    order, ub = lax.optimization_barrier((order, jnp.concatenate([displacement, body_load])))
    ub = padded_2(ub, (("gx", 1), ("gy", 2)), m)
    disp, load = ub[:3], ub[3:]

    coarse = restrict_xzy(order)
    stiff = lax.all_to_all(coarse, "gy", split_axis=1, concat_axis=2, tiled=True)
    stiff_pad = halo_exchange(stiff[None], m, 0)[0, :, TILE - m:TILE - m + stiff.shape[1] + 2 * m]

    faces, diag, center = face_terms(stiff_pad)
    for weight in (first_weight, second_weight):
        load = load[:, 1:-1, 1:-1]
        result, u_c = apply_op(disp, faces, diag)
        new = u_c + weight * (load - result) / diag
        disp = jnp.where(center > 0, new, 0.0)
        faces = [f[1:-1, 1:-1] for f in faces]
        diag = diag[1:-1, 1:-1]
        center = center[1:-1, 1:-1]
    energy = strain_energy(disp, faces)
    disp = disp[:, 1:-1, 1:-1]
    tiles = lax.all_to_all(energy, "gy", split_axis=2, concat_axis=1, tiled=True)
    return (conc, order, disp, jnp.transpose(tiles, (0, 2, 1)))


def solution(mesh):
    return jax.shard_map(
        on_device,
        mesh=mesh,
        in_specs=(
            P("gx", "gy", None),
            P("gx", "gy", None),
            P("gx", "gy", None),
            P(None, "gx", "gy", None),
            P(None, "gx", "gy", None),
        ),
        out_specs=(
            P("gx", "gy", None),
            P("gx", "gy", None),
            P(None, "gx", "gy", None),
            P("gx", "gy", None),
        ),
        check_vma=False,
    )
```

```python
import jax
import jax.numpy as jnp
import functools

import numpy as np
from jax import lax
from jax.experimental import pallas as pl
from jax.experimental.pallas import tpu as pltpu
from jax.sharding import PartitionSpec as P

STEPS = 4
FINE_HALO = 4
MECH_HALO = 3

rate_conc = 0.15
rate_order = 0.15
well_height = 1.0
drive_coupling = 0.5
spring_term = 0.2
first_weight = 0.5956
second_weight = 2.695


MESH = pl.DeviceIdType.MESH
TILE = 8
DIRS = [(sx, sy) for sx in (-1, 0, 1) for sy in (-1, 0, 1) if (sx, sy) != (0, 0)]


def _src_window(side, size, width):
    return {1: slice(size - width, size), -1: slice(0, width), 0: slice(0, size)}[side]


def _dst_window(side, size, width):
    return {1: slice(0, width), -1: slice(width + size, size + 2 * width), 0: slice(width, width + size)}[side]


def halo_kernel(hx, nx, ny, blk_ref, out_ref, ext, send_sem, recv_sem):
    c, x, y, z = blk_ref.shape
    t = TILE
    gx = lax.axis_index("gx")
    gy = lax.axis_index("gy")

    def exists(sx, sy):
        return (gx + sx >= 0) & (gx + sx < nx) & (gy + sy >= 0) & (gy + sy < ny)

    barrier = pltpu.get_barrier_semaphore()
    for sx, sy in DIRS:
        @pl.when(exists(sx, sy))
        def _():
            pl.semaphore_signal(barrier, inc=1, device_id=(gx + sx, gy + sy), device_id_type=MESH)
    row = (gx + nx - 1) // nx + 1 + (2 * nx - 2 - gx) // nx
    col = (gy + ny - 1) // ny + 1 + (2 * ny - 2 - gy) // ny
    pl.semaphore_wait(barrier, row * col - 1)

    copies = []
    for k, (sx, sy) in enumerate(DIRS):
        copy = pltpu.make_async_remote_copy(
            src_ref=blk_ref.at[:, _src_window(sx, x, hx), _src_window(sy, y, t), :],
            dst_ref=ext.at[:, _dst_window(sx, x, hx), _dst_window(sy, y, t), :],
            send_sem=send_sem.at[k],
            recv_sem=recv_sem.at[k],
            device_id=(lax.rem(gx + sx + nx, nx), lax.rem(gy + sy + ny, ny)),
            device_id_type=MESH,
        )
        copies.append(copy)

        @pl.when(exists(sx, sy))
        def _():
            copy.start()

    ext[:, hx:hx + x, t:t + y, :] = blk_ref[...]
    for sx, sy in DIRS:
        xs, ys = _dst_window(sx, x, hx), _dst_window(sy, y, t)

        @pl.when(jnp.logical_not(exists(-sx, -sy)))
        def _():
            ext[:, xs, ys, :] = jnp.zeros((c, xs.stop - xs.start, ys.stop - ys.start, z), ext.dtype)

    for (sx, sy), copy in zip(DIRS, copies):
        @pl.when(exists(sx, sy))
        def _():
            copy.wait_send()

        @pl.when(exists(-sx, -sy))
        def _():
            copy.wait_recv()
    out_ref[...] = ext[...]


def halo_exchange(block, hx, cid):
    c, x, y, z = block.shape
    nx, ny = lax.axis_size("gx"), lax.axis_size("gy")
    shape = (c, x + 2 * hx, y + 2 * TILE, z)
    return pl.pallas_call(
        functools.partial(halo_kernel, hx, nx, ny),
        out_shape=jax.ShapeDtypeStruct(shape, block.dtype),
        in_specs=[pl.BlockSpec(memory_space=pltpu.VMEM)],
        out_specs=pl.BlockSpec(memory_space=pltpu.VMEM),
        scratch_shapes=[
            pltpu.VMEM(shape, block.dtype),
            pltpu.SemaphoreType.DMA((len(DIRS),)),
            pltpu.SemaphoreType.DMA((len(DIRS),)),
        ],
        compiler_params=pltpu.CompilerParams(collective_id=cid, has_side_effects=True),
    )(block)


def padded_many(blocks, rounds):
    blocks = list(blocks)
    for axis, specs in rounds:
        count = lax.axis_size(axis)
        forward = [(i, i + 1) for i in range(count - 1)]
        backward = [(target, source) for source, target in forward]
        highs, lows = [], []
        for block, (dim, width) in zip(blocks, specs):
            highs.append(lax.slice_in_dim(block, block.shape[dim] - width, None, axis=dim))
            lows.append(lax.slice_in_dim(block, 0, width, axis=dim))
        lane = blocks[0].shape[-1]

        def pack(parts):
            return jnp.concatenate([p.reshape(-1, lane) for p in parts])

        def unpack(flat, like):
            out, at = [], 0
            for p in like:
                rows = p.size // lane
                out.append(flat[at:at + rows].reshape(p.shape))
                at += rows
            return out

        got_low = unpack(lax.ppermute(pack(highs), axis, forward), highs)
        got_high = unpack(lax.ppermute(pack(lows), axis, backward), lows)
        blocks = [jnp.concatenate([lo, b, hi], axis=dim)
                  for b, lo, hi, (dim, _) in zip(blocks, got_low, got_high, specs)]
    return blocks


def padded_2(block, sides, width):
    for axis, dim in sides:
        count = lax.axis_size(axis)
        forward = [(i, i + 1) for i in range(count - 1)]
        backward = [(target, source) for source, target in forward]
        low = lax.ppermute(
            lax.slice_in_dim(block, block.shape[dim] - width, None, axis=dim), axis, forward
        )
        high = lax.ppermute(lax.slice_in_dim(block, 0, width, axis=dim), axis, backward)
        block = jnp.concatenate([low, block, high], axis=dim)
    return block


def fine_laplace(padded):
    zpad = jnp.pad(padded, ((0, 0), (0, 0), (1, 1)))
    center = zpad[1:-1, 1:-1, 1:-1]
    total = zpad[2:, 1:-1, 1:-1] + zpad[:-2, 1:-1, 1:-1]
    total = total + zpad[1:-1, 2:, 1:-1] + zpad[1:-1, :-2, 1:-1]
    total = total + zpad[1:-1, 1:-1, 2:] + zpad[1:-1, 1:-1, :-2]
    return total - 6.0 * center


def advance(conc_pad, order_pad, mob_pad, last):
    chem = conc_pad - order_pad * order_pad * (3.0 - 2.0 * order_pad)
    conc_in = conc_pad[1:-1, 1:-1]
    order_in = order_pad[1:-1, 1:-1]
    chem_in = chem[1:-1, 1:-1]
    mobility = mob_pad[1:-1, 1:-1]
    conc_new = conc_in + rate_conc * fine_laplace(chem)
    dh_term = 6.0 * order_in * (1.0 - order_in)
    dg_term = 2.0 * order_in * (1.0 - order_in) * (1.0 - 2.0 * order_in)
    order_new = order_in + mobility * (
        rate_order * fine_laplace(order_pad)
        - well_height * dg_term
        + drive_coupling * chem_in * dh_term
    )
    if not last:
        conc_new = jnp.where(mobility > 0, conc_new, 0.0)
    return conc_new, order_new, mobility


def mobility_of(labels):
    return (0.5 * (labels == 0) + 1.0 * (labels == 1) + 0.25 * (labels == 2)).astype(jnp.float32)


def restrict_xzy(order_out):
    sx, sy, sz = order_out.shape
    sq = order_out * order_out
    sq = sq.reshape(sx // 2, 2, sy, sz).sum(axis=1)
    sq = sq.reshape(sx // 2, sy // 2, 2, sz).sum(axis=2)
    pairs = jnp.asarray(np.repeat(np.eye(sz // 2, dtype=np.float32), 2, axis=0))
    summed = jnp.einsum("xyz,zw->xwy", sq, pairs, precision=lax.Precision.HIGHEST)
    return 0.1 + 0.125 * summed


def y_shift(v, step):
    if step > 0:
        return jnp.pad(v[..., step:], [(0, 0)] * (v.ndim - 1) + [(0, step)])
    return jnp.pad(v[..., :step], [(0, 0)] * (v.ndim - 1) + [(-step, 0)])


def face_terms(stiff_pad):
    center = stiff_pad[1:-1, 1:-1]
    others = [stiff_pad[2:, 1:-1], stiff_pad[:-2, 1:-1], stiff_pad[1:-1, 2:], stiff_pad[1:-1, :-2],
              y_shift(center, 1), y_shift(center, -1)]
    faces = [0.5 * (center + other) for other in others]
    diag = faces[0] + faces[1] + faces[2] + faces[3] + faces[4] + faces[5] + spring_term * center
    return faces, diag, center


def neighbours(u_pad):
    center = u_pad[:, 1:-1, 1:-1]
    return center, [u_pad[:, 2:, 1:-1], u_pad[:, :-2, 1:-1], u_pad[:, 1:-1, 2:], u_pad[:, 1:-1, :-2],
                    y_shift(center, 1), y_shift(center, -1)]


def apply_op(u_pad, faces, diag):
    center, others = neighbours(u_pad)
    result = diag * center
    for face, other in zip(faces, others):
        result = result - face * other
    return result, center


def strain_energy(u_pad, faces):
    center, others = neighbours(u_pad)
    total = jnp.zeros(center.shape, jnp.float32)
    for face, other in zip(faces, others):
        diff = center - other
        total = total + face * diff * diff
    return 0.25 * jnp.sum(total, axis=0)


def on_device(concentration, order_field, phase_labels, displacement, body_load):
    h = FINE_HALO
    fields = jnp.stack([concentration, order_field, mobility_of(phase_labels)])
    m = MECH_HALO
    fields, ub = padded_many(
        [fields, jnp.concatenate([displacement, body_load])],
        [("gx", [(1, h), (1, m)]), ("gy", [(2, h), (2, m)])],
    )
    conc, order, mob = fields[0], fields[1], fields[2]
    for step in range(STEPS):
        conc, order, mob = advance(conc, order, mob, step == STEPS - 1)

    disp, load = ub[:3], ub[3:]

    coarse = restrict_xzy(order)
    stiff = lax.all_to_all(coarse, "gy", split_axis=1, concat_axis=2, tiled=True)
    stiff_pad = halo_exchange(stiff[None], m, 0)[0, :, TILE - m:TILE - m + stiff.shape[1] + 2 * m]

    faces, diag, center = face_terms(stiff_pad)
    for weight in (first_weight, second_weight):
        load = load[:, 1:-1, 1:-1]
        result, u_c = apply_op(disp, faces, diag)
        new = u_c + weight * (load - result) / diag
        disp = jnp.where(center > 0, new, 0.0)
        faces = [f[1:-1, 1:-1] for f in faces]
        diag = diag[1:-1, 1:-1]
        center = center[1:-1, 1:-1]
    energy = strain_energy(disp, faces)
    disp = disp[:, 1:-1, 1:-1]
    tiles = lax.all_to_all(energy, "gy", split_axis=2, concat_axis=1, tiled=True)
    return (conc, order, disp, jnp.transpose(tiles, (0, 2, 1)))


def solution(mesh):
    return jax.shard_map(
        on_device,
        mesh=mesh,
        in_specs=(
            P("gx", "gy", None),
            P("gx", "gy", None),
            P("gx", "gy", None),
            P(None, "gx", "gy", None),
            P(None, "gx", "gy", None),
        ),
        out_specs=(
            P("gx", "gy", None),
            P("gx", "gy", None),
            P(None, "gx", "gy", None),
            P("gx", "gy", None),
        ),
        check_vma=False,
    )
```

```python
import jax
import jax.numpy as jnp
import functools

import numpy as np
from jax import lax
from jax.experimental import pallas as pl
from jax.experimental.pallas import tpu as pltpu
from jax.sharding import PartitionSpec as P

STEPS = 4
FINE_HALO = 4
MECH_HALO = 3

rate_conc = 0.15
rate_order = 0.15
well_height = 1.0
drive_coupling = 0.5
spring_term = 0.2
first_weight = 0.5956
second_weight = 2.695


MESH = pl.DeviceIdType.MESH
TILE = 8
DIRS = [(sx, sy) for sx in (-1, 0, 1) for sy in (-1, 0, 1) if (sx, sy) != (0, 0)]


def _src_window(side, size, width):
    return {1: slice(size - width, size), -1: slice(0, width), 0: slice(0, size)}[side]


def _dst_window(side, size, width):
    return {1: slice(0, width), -1: slice(width + size, size + 2 * width), 0: slice(width, width + size)}[side]


def halo_kernel(hx, nx, ny, blk_ref, out_ref, ext, send_sem, recv_sem):
    c, x, y, z = blk_ref.shape
    t = TILE
    gx = lax.axis_index("gx")
    gy = lax.axis_index("gy")

    def exists(sx, sy):
        return (gx + sx >= 0) & (gx + sx < nx) & (gy + sy >= 0) & (gy + sy < ny)

    barrier = pltpu.get_barrier_semaphore()
    for sx, sy in DIRS:
        @pl.when(exists(sx, sy))
        def _():
            pl.semaphore_signal(barrier, inc=1, device_id=(gx + sx, gy + sy), device_id_type=MESH)
    row = (gx + nx - 1) // nx + 1 + (2 * nx - 2 - gx) // nx
    col = (gy + ny - 1) // ny + 1 + (2 * ny - 2 - gy) // ny
    pl.semaphore_wait(barrier, row * col - 1)

    copies = []
    for k, (sx, sy) in enumerate(DIRS):
        copy = pltpu.make_async_remote_copy(
            src_ref=blk_ref.at[:, _src_window(sx, x, hx), _src_window(sy, y, t), :],
            dst_ref=ext.at[:, _dst_window(sx, x, hx), _dst_window(sy, y, t), :],
            send_sem=send_sem.at[k],
            recv_sem=recv_sem.at[k],
            device_id=(lax.rem(gx + sx + nx, nx), lax.rem(gy + sy + ny, ny)),
            device_id_type=MESH,
        )
        copies.append(copy)

        @pl.when(exists(sx, sy))
        def _():
            copy.start()

    ext[:, hx:hx + x, t:t + y, :] = blk_ref[...]
    for sx, sy in DIRS:
        xs, ys = _dst_window(sx, x, hx), _dst_window(sy, y, t)

        @pl.when(jnp.logical_not(exists(-sx, -sy)))
        def _():
            ext[:, xs, ys, :] = jnp.zeros((c, xs.stop - xs.start, ys.stop - ys.start, z), ext.dtype)

    for (sx, sy), copy in zip(DIRS, copies):
        @pl.when(exists(sx, sy))
        def _():
            copy.wait_send()

        @pl.when(exists(-sx, -sy))
        def _():
            copy.wait_recv()
    out_ref[...] = ext[...]


def halo_exchange(block, hx, cid):
    c, x, y, z = block.shape
    nx, ny = lax.axis_size("gx"), lax.axis_size("gy")
    shape = (c, x + 2 * hx, y + 2 * TILE, z)
    return pl.pallas_call(
        functools.partial(halo_kernel, hx, nx, ny),
        out_shape=jax.ShapeDtypeStruct(shape, block.dtype),
        in_specs=[pl.BlockSpec(memory_space=pltpu.VMEM)],
        out_specs=pl.BlockSpec(memory_space=pltpu.VMEM),
        scratch_shapes=[
            pltpu.VMEM(shape, block.dtype),
            pltpu.SemaphoreType.DMA((len(DIRS),)),
            pltpu.SemaphoreType.DMA((len(DIRS),)),
        ],
        compiler_params=pltpu.CompilerParams(collective_id=cid, has_side_effects=True),
    )(block)


def padded_2(block, sides, width):
    for axis, dim in sides:
        count = lax.axis_size(axis)
        forward = [(i, i + 1) for i in range(count - 1)]
        backward = [(target, source) for source, target in forward]
        low = lax.ppermute(
            lax.slice_in_dim(block, block.shape[dim] - width, None, axis=dim), axis, forward
        )
        high = lax.ppermute(lax.slice_in_dim(block, 0, width, axis=dim), axis, backward)
        block = jnp.concatenate([low, block, high], axis=dim)
    return block


def fine_laplace(padded):
    zpad = jnp.pad(padded, ((0, 0), (0, 0), (1, 1)))
    center = zpad[1:-1, 1:-1, 1:-1]
    total = zpad[2:, 1:-1, 1:-1] + zpad[:-2, 1:-1, 1:-1]
    total = total + zpad[1:-1, 2:, 1:-1] + zpad[1:-1, :-2, 1:-1]
    total = total + zpad[1:-1, 1:-1, 2:] + zpad[1:-1, 1:-1, :-2]
    return total - 6.0 * center


def advance(conc_pad, order_pad, mob_pad, last):
    chem = conc_pad - order_pad * order_pad * (3.0 - 2.0 * order_pad)
    conc_in = conc_pad[1:-1, 1:-1]
    order_in = order_pad[1:-1, 1:-1]
    chem_in = chem[1:-1, 1:-1]
    mobility = mob_pad[1:-1, 1:-1]
    conc_new = conc_in + rate_conc * fine_laplace(chem)
    dh_term = 6.0 * order_in * (1.0 - order_in)
    dg_term = 2.0 * order_in * (1.0 - order_in) * (1.0 - 2.0 * order_in)
    order_new = order_in + mobility * (
        rate_order * fine_laplace(order_pad)
        - well_height * dg_term
        + drive_coupling * chem_in * dh_term
    )
    if not last:
        conc_new = jnp.where(mobility > 0, conc_new, 0.0)
    return conc_new, order_new, mobility


def mobility_of(labels):
    return (0.5 * (labels == 0) + 1.0 * (labels == 1) + 0.25 * (labels == 2)).astype(jnp.float32)


def restrict_xzy(order_out):
    sx, sy, sz = order_out.shape
    sq = order_out * order_out
    sq = sq.reshape(sx // 2, 2, sy, sz).sum(axis=1)
    sq = sq.reshape(sx // 2, sy // 2, 2, sz).sum(axis=2)
    pairs = jnp.asarray(np.repeat(np.eye(sz // 2, dtype=np.float32), 2, axis=0))
    summed = jnp.einsum("xyz,zw->xwy", sq, pairs, precision=lax.Precision.HIGHEST)
    return 0.1 + 0.125 * summed


def y_shift(v, step):
    if step > 0:
        return jnp.pad(v[..., step:], [(0, 0)] * (v.ndim - 1) + [(0, step)])
    return jnp.pad(v[..., :step], [(0, 0)] * (v.ndim - 1) + [(-step, 0)])


def face_terms(stiff_pad):
    center = stiff_pad[1:-1, 1:-1]
    others = [stiff_pad[2:, 1:-1], stiff_pad[:-2, 1:-1], stiff_pad[1:-1, 2:], stiff_pad[1:-1, :-2],
              y_shift(center, 1), y_shift(center, -1)]
    faces = [0.5 * (center + other) for other in others]
    diag = faces[0] + faces[1] + faces[2] + faces[3] + faces[4] + faces[5] + spring_term * center
    return faces, diag, center


def neighbours(u_pad):
    center = u_pad[:, 1:-1, 1:-1]
    return center, [u_pad[:, 2:, 1:-1], u_pad[:, :-2, 1:-1], u_pad[:, 1:-1, 2:], u_pad[:, 1:-1, :-2],
                    y_shift(center, 1), y_shift(center, -1)]


def apply_op(u_pad, faces, diag):
    center, others = neighbours(u_pad)
    result = diag * center
    for face, other in zip(faces, others):
        result = result - face * other
    return result, center


def strain_energy(u_pad, faces):
    center, others = neighbours(u_pad)
    total = jnp.zeros(center.shape, jnp.float32)
    for face, other in zip(faces, others):
        diff = center - other
        total = total + face * diff * diff
    return 0.25 * jnp.sum(total, axis=0)


def on_device(concentration, order_field, phase_labels, displacement, body_load):
    h = FINE_HALO
    fields = jnp.stack([concentration, order_field, mobility_of(phase_labels)])
    m = MECH_HALO
    fields = padded_2(fields, (("gx", 1),), h)
    fields, ub = lax.optimization_barrier((fields, jnp.concatenate([displacement, body_load])))
    ub = padded_2(ub, (("gx", 1),), m)
    fields = padded_2(fields, (("gy", 2),), h)
    conc, order, mob = fields[0], fields[1], fields[2]
    for step in range(STEPS):
        conc, order, mob = advance(conc, order, mob, step == STEPS - 1)

    order, ub = lax.optimization_barrier((order, ub))
    ub = padded_2(ub, (("gy", 2),), m)
    disp, load = ub[:3], ub[3:]

    coarse = restrict_xzy(order)
    stiff = lax.all_to_all(coarse, "gy", split_axis=1, concat_axis=2, tiled=True)
    stiff_pad = halo_exchange(stiff[None], m, 0)[0, :, TILE - m:TILE - m + stiff.shape[1] + 2 * m]

    faces, diag, center = face_terms(stiff_pad)
    for weight in (first_weight, second_weight):
        load = load[:, 1:-1, 1:-1]
        result, u_c = apply_op(disp, faces, diag)
        new = u_c + weight * (load - result) / diag
        disp = jnp.where(center > 0, new, 0.0)
        faces = [f[1:-1, 1:-1] for f in faces]
        diag = diag[1:-1, 1:-1]
        center = center[1:-1, 1:-1]
    energy = strain_energy(disp, faces)
    disp = disp[:, 1:-1, 1:-1]
    tiles = lax.all_to_all(energy, "gy", split_axis=2, concat_axis=1, tiled=True)
    return (conc, order, disp, jnp.transpose(tiles, (0, 2, 1)))


def solution(mesh):
    return jax.shard_map(
        on_device,
        mesh=mesh,
        in_specs=(
            P("gx", "gy", None),
            P("gx", "gy", None),
            P("gx", "gy", None),
            P(None, "gx", "gy", None),
            P(None, "gx", "gy", None),
        ),
        out_specs=(
            P("gx", "gy", None),
            P("gx", "gy", None),
            P(None, "gx", "gy", None),
            P("gx", "gy", None),
        ),
        check_vma=False,
    )
```

```python
import jax
import jax.numpy as jnp
import functools

import numpy as np
from jax import lax
from jax.experimental import pallas as pl
from jax.experimental.pallas import tpu as pltpu
from jax.sharding import PartitionSpec as P

STEPS = 4
FINE_HALO = 4
MECH_HALO = 3

rate_conc = 0.15
rate_order = 0.15
well_height = 1.0
drive_coupling = 0.5
spring_term = 0.2
first_weight = 0.5956
second_weight = 2.695


MESH = pl.DeviceIdType.MESH
TILE = 8
DIRS = [(sx, sy) for sx in (-1, 0, 1) for sy in (-1, 0, 1) if (sx, sy) != (0, 0)]


def _src_window(side, size, width):
    return {1: slice(size - width, size), -1: slice(0, width), 0: slice(0, size)}[side]


def _dst_window(side, size, width):
    return {1: slice(0, width), -1: slice(width + size, size + 2 * width), 0: slice(width, width + size)}[side]


def halo_kernel(hx, nx, ny, blk_ref, out_ref, ext, send_sem, recv_sem):
    c, x, y, z = blk_ref.shape
    t = TILE
    gx = lax.axis_index("gx")
    gy = lax.axis_index("gy")

    def exists(sx, sy):
        return (gx + sx >= 0) & (gx + sx < nx) & (gy + sy >= 0) & (gy + sy < ny)

    barrier = pltpu.get_barrier_semaphore()
    for sx, sy in DIRS:
        @pl.when(exists(sx, sy))
        def _():
            pl.semaphore_signal(barrier, inc=1, device_id=(gx + sx, gy + sy), device_id_type=MESH)
    row = (gx + nx - 1) // nx + 1 + (2 * nx - 2 - gx) // nx
    col = (gy + ny - 1) // ny + 1 + (2 * ny - 2 - gy) // ny
    pl.semaphore_wait(barrier, row * col - 1)

    copies = []
    for k, (sx, sy) in enumerate(DIRS):
        copy = pltpu.make_async_remote_copy(
            src_ref=blk_ref.at[:, _src_window(sx, x, hx), _src_window(sy, y, t), :],
            dst_ref=ext.at[:, _dst_window(sx, x, hx), _dst_window(sy, y, t), :],
            send_sem=send_sem.at[k],
            recv_sem=recv_sem.at[k],
            device_id=(lax.rem(gx + sx + nx, nx), lax.rem(gy + sy + ny, ny)),
            device_id_type=MESH,
        )
        copies.append(copy)

        @pl.when(exists(sx, sy))
        def _():
            copy.start()

    ext[:, hx:hx + x, t:t + y, :] = blk_ref[...]
    for sx, sy in DIRS:
        xs, ys = _dst_window(sx, x, hx), _dst_window(sy, y, t)

        @pl.when(jnp.logical_not(exists(-sx, -sy)))
        def _():
            ext[:, xs, ys, :] = jnp.zeros((c, xs.stop - xs.start, ys.stop - ys.start, z), ext.dtype)

    for (sx, sy), copy in zip(DIRS, copies):
        @pl.when(exists(sx, sy))
        def _():
            copy.wait_send()

        @pl.when(exists(-sx, -sy))
        def _():
            copy.wait_recv()
    out_ref[...] = ext[...]


def halo_exchange(block, hx, cid):
    c, x, y, z = block.shape
    nx, ny = lax.axis_size("gx"), lax.axis_size("gy")
    shape = (c, x + 2 * hx, y + 2 * TILE, z)
    return pl.pallas_call(
        functools.partial(halo_kernel, hx, nx, ny),
        out_shape=jax.ShapeDtypeStruct(shape, block.dtype),
        in_specs=[pl.BlockSpec(memory_space=pltpu.VMEM)],
        out_specs=pl.BlockSpec(memory_space=pltpu.VMEM),
        scratch_shapes=[
            pltpu.VMEM(shape, block.dtype),
            pltpu.SemaphoreType.DMA((len(DIRS),)),
            pltpu.SemaphoreType.DMA((len(DIRS),)),
        ],
        compiler_params=pltpu.CompilerParams(collective_id=cid, has_side_effects=True),
    )(block)


def _rolls(v):
    lane = lax.broadcasted_iota(jnp.int32, v.shape, 1)
    last = v.shape[1] - 1
    return (pltpu.roll(v, v.shape[0] - 1, 0), pltpu.roll(v, 1, 0),
            jnp.where(lane == last, 0.0, pltpu.roll(v, last, 1)), jnp.where(lane == 0, 0.0, pltpu.roll(v, 1, 1)))


def mech_kernel(zoff, s_ref, ub_ref, disp_out, energy_out, u1, u2):
    _, nxe, nz, _ = ub_ref.shape
    bx, bz = disp_out.shape[1], disp_out.shape[2]
    m = (nxe - bx) // 2
    lo = (nz - bz) // 2

    def faces_at(i):
        c = s_ref[i, pl.ds(zoff, nz), :]
        xp = s_ref[i + 1, pl.ds(zoff, nz), :]
        xm = s_ref[i - 1, pl.ds(zoff, nz), :]
        zp, zm, yp, ym = _rolls(c)
        faces = [0.5 * (c + o) for o in (xp, xm, zp, zm, yp, ym)]
        diag = faces[0] + faces[1] + faces[2] + faces[3] + faces[4] + faces[5] + spring_term * c
        return c, faces, diag

    def sweep(src, dst, weight, i):
        c, faces, diag = faces_at(i)
        for k in range(3):
            u = src[k, i]
            others = (src[k, i + 1], src[k, i - 1]) + _rolls(u)
            result = diag * u
            for face, other in zip(faces, others):
                result = result - face * other
            new = u + weight * (ub_ref[3 + k, i] - result) / diag
            dst[k, i] = jnp.where(c > 0, new, 0.0)

    def first(i, carry):
        sweep(ub_ref, u1, first_weight, i)
        return carry

    def second(i, carry):
        sweep(u1, u2, second_weight, i)
        return carry

    lax.fori_loop(1, nxe - 1, first, 0)
    lax.fori_loop(2, nxe - 2, second, 0)

    def energy_row(i, carry):
        _, faces, _ = faces_at(i)
        parts = []
        for k in range(3):
            u = u2[k, i]
            others = (u2[k, i + 1], u2[k, i - 1]) + _rolls(u)
            total = jnp.zeros(u.shape, jnp.float32)
            for face, other in zip(faces, others):
                diff = u - other
                total = total + face * diff * diff
            parts.append(total)
        u1[0, i] = 0.25 * (parts[0] + parts[1] + parts[2])
        return carry

    lax.fori_loop(m, m + bx, energy_row, 0)
    energy_out[...] = u1[0, pl.ds(m, bx), pl.ds(lo, bz), :]
    disp_out[...] = u2[:, pl.ds(m, bx), pl.ds(lo, bz), :]


def mechanics(stiff_ext, ub, zoff, bx, bz):
    _, nxe, nz, ny = ub.shape
    return pl.pallas_call(
        functools.partial(mech_kernel, zoff),
        out_shape=(jax.ShapeDtypeStruct((3, bx, bz, ny), jnp.float32),
                   jax.ShapeDtypeStruct((bx, bz, ny), jnp.float32)),
        in_specs=[pl.BlockSpec(memory_space=pltpu.VMEM)] * 2,
        out_specs=(pl.BlockSpec(memory_space=pltpu.VMEM), pl.BlockSpec(memory_space=pltpu.VMEM)),
        scratch_shapes=[pltpu.VMEM((3, nxe, nz, ny), jnp.float32), pltpu.VMEM((3, nxe, nz, ny), jnp.float32)],
    )(stiff_ext, ub)


def padded_2(block, sides, width):
    for axis, dim in sides:
        count = lax.axis_size(axis)
        forward = [(i, i + 1) for i in range(count - 1)]
        backward = [(target, source) for source, target in forward]
        low = lax.ppermute(
            lax.slice_in_dim(block, block.shape[dim] - width, None, axis=dim), axis, forward
        )
        high = lax.ppermute(lax.slice_in_dim(block, 0, width, axis=dim), axis, backward)
        block = jnp.concatenate([low, block, high], axis=dim)
    return block


def fine_laplace(padded):
    zpad = jnp.pad(padded, ((0, 0), (0, 0), (1, 1)))
    center = zpad[1:-1, 1:-1, 1:-1]
    total = zpad[2:, 1:-1, 1:-1] + zpad[:-2, 1:-1, 1:-1]
    total = total + zpad[1:-1, 2:, 1:-1] + zpad[1:-1, :-2, 1:-1]
    total = total + zpad[1:-1, 1:-1, 2:] + zpad[1:-1, 1:-1, :-2]
    return total - 6.0 * center


def advance(conc_pad, order_pad, mob_pad, last):
    chem = conc_pad - order_pad * order_pad * (3.0 - 2.0 * order_pad)
    conc_in = conc_pad[1:-1, 1:-1]
    order_in = order_pad[1:-1, 1:-1]
    chem_in = chem[1:-1, 1:-1]
    mobility = mob_pad[1:-1, 1:-1]
    conc_new = conc_in + rate_conc * fine_laplace(chem)
    dh_term = 6.0 * order_in * (1.0 - order_in)
    dg_term = 2.0 * order_in * (1.0 - order_in) * (1.0 - 2.0 * order_in)
    order_new = order_in + mobility * (
        rate_order * fine_laplace(order_pad)
        - well_height * dg_term
        + drive_coupling * chem_in * dh_term
    )
    if not last:
        conc_new = jnp.where(mobility > 0, conc_new, 0.0)
    return conc_new, order_new, mobility


def mobility_of(labels):
    return (0.5 * (labels == 0) + 1.0 * (labels == 1) + 0.25 * (labels == 2)).astype(jnp.float32)


def restrict_xzy(order_out):
    sx, sy, sz = order_out.shape
    sq = order_out * order_out
    sq = sq.reshape(sx // 2, 2, sy, sz).sum(axis=1)
    sq = sq.reshape(sx // 2, sy // 2, 2, sz).sum(axis=2)
    pairs = jnp.asarray(np.repeat(np.eye(sz // 2, dtype=np.float32), 2, axis=0))
    summed = jnp.einsum("xyz,zw->xwy", sq, pairs, precision=lax.Precision.HIGHEST)
    return 0.1 + 0.125 * summed


def y_shift(v, step):
    if step > 0:
        return jnp.pad(v[..., step:], [(0, 0)] * (v.ndim - 1) + [(0, step)])
    return jnp.pad(v[..., :step], [(0, 0)] * (v.ndim - 1) + [(-step, 0)])


def face_terms(stiff_pad):
    center = stiff_pad[1:-1, 1:-1]
    others = [stiff_pad[2:, 1:-1], stiff_pad[:-2, 1:-1], stiff_pad[1:-1, 2:], stiff_pad[1:-1, :-2],
              y_shift(center, 1), y_shift(center, -1)]
    faces = [0.5 * (center + other) for other in others]
    diag = faces[0] + faces[1] + faces[2] + faces[3] + faces[4] + faces[5] + spring_term * center
    return faces, diag, center


def neighbours(u_pad):
    center = u_pad[:, 1:-1, 1:-1]
    return center, [u_pad[:, 2:, 1:-1], u_pad[:, :-2, 1:-1], u_pad[:, 1:-1, 2:], u_pad[:, 1:-1, :-2],
                    y_shift(center, 1), y_shift(center, -1)]


def apply_op(u_pad, faces, diag):
    center, others = neighbours(u_pad)
    result = diag * center
    for face, other in zip(faces, others):
        result = result - face * other
    return result, center


def strain_energy(u_pad, faces):
    center, others = neighbours(u_pad)
    total = jnp.zeros(center.shape, jnp.float32)
    for face, other in zip(faces, others):
        diff = center - other
        total = total + face * diff * diff
    return 0.25 * jnp.sum(total, axis=0)


def on_device(concentration, order_field, phase_labels, displacement, body_load):
    h = FINE_HALO
    fields = jnp.stack([concentration, order_field, mobility_of(phase_labels)])
    m = MECH_HALO
    fields = padded_2(fields, (("gx", 1),), h)
    fields, ub = lax.optimization_barrier((fields, jnp.concatenate([displacement, body_load])))
    ub = padded_2(ub, (("gx", 1),), m)
    fields = padded_2(fields, (("gy", 2),), h)
    conc, order, mob = fields[0], fields[1], fields[2]
    for step in range(STEPS):
        conc, order, mob = advance(conc, order, mob, step == STEPS - 1)

    order, ub = lax.optimization_barrier((order, ub))
    ub = padded_2(ub, (("gy", 2),), m + 1)
    disp, load = ub[:3], ub[3:]

    coarse = restrict_xzy(order)
    stiff = lax.all_to_all(coarse, "gy", split_axis=1, concat_axis=2, tiled=True)
    stiff_ext = halo_exchange(stiff[None], m, 0)[0]
    bx, bz = stiff.shape[0], stiff.shape[1]
    disp, energy = mechanics(stiff_ext, ub, TILE - (m + 1), bx, bz)
    tiles = lax.all_to_all(energy, "gy", split_axis=2, concat_axis=1, tiled=True)
    return (conc, order, disp, jnp.transpose(tiles, (0, 2, 1)))


def solution(mesh):
    return jax.shard_map(
        on_device,
        mesh=mesh,
        in_specs=(
            P("gx", "gy", None),
            P("gx", "gy", None),
            P("gx", "gy", None),
            P(None, "gx", "gy", None),
            P(None, "gx", "gy", None),
        ),
        out_specs=(
            P("gx", "gy", None),
            P("gx", "gy", None),
            P(None, "gx", "gy", None),
            P("gx", "gy", None),
        ),
        check_vma=False,
    )
```

```python
import jax
import jax.numpy as jnp
import functools

import numpy as np
from jax import lax
from jax.experimental import pallas as pl
from jax.experimental.pallas import tpu as pltpu
from jax.sharding import PartitionSpec as P

STEPS = 4
FINE_HALO = 4
MECH_HALO = 3

rate_conc = 0.15
rate_order = 0.15
well_height = 1.0
drive_coupling = 0.5
spring_term = 0.2
first_weight = 0.5956
second_weight = 2.695


MESH = pl.DeviceIdType.MESH
TILE = 8
DIRS = [(sx, sy) for sx in (-1, 0, 1) for sy in (-1, 0, 1) if (sx, sy) != (0, 0)]


def _src_window(side, size, width):
    return {1: slice(size - width, size), -1: slice(0, width), 0: slice(0, size)}[side]


def _dst_window(side, size, width):
    return {1: slice(0, width), -1: slice(width + size, size + 2 * width), 0: slice(width, width + size)}[side]


def halo_kernel(hx, nx, ny, blk_ref, out_ref, ext, send_sem, recv_sem):
    c, x, y, z = blk_ref.shape
    t = TILE
    gx = lax.axis_index("gx")
    gy = lax.axis_index("gy")

    def exists(sx, sy):
        return (gx + sx >= 0) & (gx + sx < nx) & (gy + sy >= 0) & (gy + sy < ny)

    barrier = pltpu.get_barrier_semaphore()
    for sx, sy in DIRS:
        @pl.when(exists(sx, sy))
        def _():
            pl.semaphore_signal(barrier, inc=1, device_id=(gx + sx, gy + sy), device_id_type=MESH)
    row = (gx + nx - 1) // nx + 1 + (2 * nx - 2 - gx) // nx
    col = (gy + ny - 1) // ny + 1 + (2 * ny - 2 - gy) // ny
    pl.semaphore_wait(barrier, row * col - 1)

    copies = []
    for k, (sx, sy) in enumerate(DIRS):
        copy = pltpu.make_async_remote_copy(
            src_ref=blk_ref.at[:, _src_window(sx, x, hx), _src_window(sy, y, t), :],
            dst_ref=ext.at[:, _dst_window(sx, x, hx), _dst_window(sy, y, t), :],
            send_sem=send_sem.at[k],
            recv_sem=recv_sem.at[k],
            device_id=(lax.rem(gx + sx + nx, nx), lax.rem(gy + sy + ny, ny)),
            device_id_type=MESH,
        )
        copies.append(copy)

        @pl.when(exists(sx, sy))
        def _():
            copy.start()

    ext[:, hx:hx + x, t:t + y, :] = blk_ref[...]
    for sx, sy in DIRS:
        xs, ys = _dst_window(sx, x, hx), _dst_window(sy, y, t)

        @pl.when(jnp.logical_not(exists(-sx, -sy)))
        def _():
            ext[:, xs, ys, :] = jnp.zeros((c, xs.stop - xs.start, ys.stop - ys.start, z), ext.dtype)

    for (sx, sy), copy in zip(DIRS, copies):
        @pl.when(exists(sx, sy))
        def _():
            copy.wait_send()

        @pl.when(exists(-sx, -sy))
        def _():
            copy.wait_recv()
    out_ref[...] = ext[...]


def halo_exchange(block, hx, cid):
    c, x, y, z = block.shape
    nx, ny = lax.axis_size("gx"), lax.axis_size("gy")
    shape = (c, x + 2 * hx, y + 2 * TILE, z)
    return pl.pallas_call(
        functools.partial(halo_kernel, hx, nx, ny),
        out_shape=jax.ShapeDtypeStruct(shape, block.dtype),
        in_specs=[pl.BlockSpec(memory_space=pltpu.VMEM)],
        out_specs=pl.BlockSpec(memory_space=pltpu.VMEM),
        scratch_shapes=[
            pltpu.VMEM(shape, block.dtype),
            pltpu.SemaphoreType.DMA((len(DIRS),)),
            pltpu.SemaphoreType.DMA((len(DIRS),)),
        ],
        compiler_params=pltpu.CompilerParams(collective_id=cid, has_side_effects=True),
    )(block)


def _rolls(v):
    lane = lax.broadcasted_iota(jnp.int32, v.shape, 1)
    last = v.shape[1] - 1
    return (pltpu.roll(v, v.shape[0] - 1, 0), pltpu.roll(v, 1, 0),
            jnp.where(lane == last, 0.0, pltpu.roll(v, last, 1)), jnp.where(lane == 0, 0.0, pltpu.roll(v, 1, 1)))


def mech_kernel(zoff, s_ref, ub_ref, disp_out, energy_out, u1, u2, fc):
    _, nxe, nz, _ = ub_ref.shape
    bx, bz = disp_out.shape[1], disp_out.shape[2]
    m = (nxe - bx) // 2
    lo = (nz - bz) // 2

    def align(i, carry):
        fc[7, i] = s_ref[i, pl.ds(zoff, nz), :]
        return carry

    lax.fori_loop(0, nxe, align, 0)

    def faces_row(i, carry):
        c = fc[7, i]
        zp, zm, yp, ym = _rolls(c)
        diag = None
        for f, o in enumerate((fc[7, i + 1], fc[7, i - 1], zp, zm, yp, ym)):
            face = 0.5 * (c + o)
            fc[f, i] = face
            diag = face if diag is None else diag + face
        fc[6, i] = diag + spring_term * c
        return carry

    lax.fori_loop(1, nxe - 1, faces_row, 0)

    def sweep(src, dst, weight, i):
        c, diag = fc[7, i], fc[6, i]
        for k in range(3):
            u = src[k, i]
            others = (src[k, i + 1], src[k, i - 1]) + _rolls(u)
            result = diag * u
            for f, other in enumerate(others):
                result = result - fc[f, i] * other
            new = u + weight * (ub_ref[3 + k, i] - result) / diag
            dst[k, i] = jnp.where(c > 0, new, 0.0)

    def first(i, carry):
        sweep(ub_ref, u1, first_weight, i)
        return carry

    def second(i, carry):
        sweep(u1, u2, second_weight, i)
        return carry

    lax.fori_loop(1, nxe - 1, first, 0)
    lax.fori_loop(2, nxe - 2, second, 0)

    def energy_row(i, carry):
        parts = []
        for k in range(3):
            u = u2[k, i]
            others = (u2[k, i + 1], u2[k, i - 1]) + _rolls(u)
            total = jnp.zeros(u.shape, jnp.float32)
            for f, other in enumerate(others):
                diff = u - other
                total = total + fc[f, i] * diff * diff
            parts.append(total)
        u1[0, i] = 0.25 * (parts[0] + parts[1] + parts[2])
        return carry

    lax.fori_loop(m, m + bx, energy_row, 0)
    energy_out[...] = u1[0, pl.ds(m, bx), pl.ds(lo, bz), :]
    disp_out[...] = u2[:, pl.ds(m, bx), pl.ds(lo, bz), :]


def mechanics(stiff_ext, ub, zoff, bx, bz):
    _, nxe, nz, ny = ub.shape
    return pl.pallas_call(
        functools.partial(mech_kernel, zoff),
        out_shape=(jax.ShapeDtypeStruct((3, bx, bz, ny), jnp.float32),
                   jax.ShapeDtypeStruct((bx, bz, ny), jnp.float32)),
        in_specs=[pl.BlockSpec(memory_space=pltpu.VMEM)] * 2,
        out_specs=(pl.BlockSpec(memory_space=pltpu.VMEM), pl.BlockSpec(memory_space=pltpu.VMEM)),
        scratch_shapes=[pltpu.VMEM((3, nxe, nz, ny), jnp.float32), pltpu.VMEM((3, nxe, nz, ny), jnp.float32),
                        pltpu.VMEM((8, nxe, nz, ny), jnp.float32)],
    )(stiff_ext, ub)


def padded_2(block, sides, width):
    for axis, dim in sides:
        count = lax.axis_size(axis)
        forward = [(i, i + 1) for i in range(count - 1)]
        backward = [(target, source) for source, target in forward]
        low = lax.ppermute(
            lax.slice_in_dim(block, block.shape[dim] - width, None, axis=dim), axis, forward
        )
        high = lax.ppermute(lax.slice_in_dim(block, 0, width, axis=dim), axis, backward)
        block = jnp.concatenate([low, block, high], axis=dim)
    return block


def fine_laplace(padded):
    zpad = jnp.pad(padded, ((0, 0), (0, 0), (1, 1)))
    center = zpad[1:-1, 1:-1, 1:-1]
    total = zpad[2:, 1:-1, 1:-1] + zpad[:-2, 1:-1, 1:-1]
    total = total + zpad[1:-1, 2:, 1:-1] + zpad[1:-1, :-2, 1:-1]
    total = total + zpad[1:-1, 1:-1, 2:] + zpad[1:-1, 1:-1, :-2]
    return total - 6.0 * center


def advance(conc_pad, order_pad, mob_pad, last):
    chem = conc_pad - order_pad * order_pad * (3.0 - 2.0 * order_pad)
    conc_in = conc_pad[1:-1, 1:-1]
    order_in = order_pad[1:-1, 1:-1]
    chem_in = chem[1:-1, 1:-1]
    mobility = mob_pad[1:-1, 1:-1]
    conc_new = conc_in + rate_conc * fine_laplace(chem)
    dh_term = 6.0 * order_in * (1.0 - order_in)
    dg_term = 2.0 * order_in * (1.0 - order_in) * (1.0 - 2.0 * order_in)
    order_new = order_in + mobility * (
        rate_order * fine_laplace(order_pad)
        - well_height * dg_term
        + drive_coupling * chem_in * dh_term
    )
    if not last:
        conc_new = jnp.where(mobility > 0, conc_new, 0.0)
    return conc_new, order_new, mobility


def mobility_of(labels):
    return (0.5 * (labels == 0) + 1.0 * (labels == 1) + 0.25 * (labels == 2)).astype(jnp.float32)


def restrict_xzy(order_out):
    sx, sy, sz = order_out.shape
    sq = order_out * order_out
    sq = sq.reshape(sx // 2, 2, sy, sz).sum(axis=1)
    sq = sq.reshape(sx // 2, sy // 2, 2, sz).sum(axis=2)
    pairs = jnp.asarray(np.repeat(np.eye(sz // 2, dtype=np.float32), 2, axis=0))
    summed = jnp.einsum("xyz,zw->xwy", sq, pairs, precision=lax.Precision.HIGHEST)
    return 0.1 + 0.125 * summed


def y_shift(v, step):
    if step > 0:
        return jnp.pad(v[..., step:], [(0, 0)] * (v.ndim - 1) + [(0, step)])
    return jnp.pad(v[..., :step], [(0, 0)] * (v.ndim - 1) + [(-step, 0)])


def face_terms(stiff_pad):
    center = stiff_pad[1:-1, 1:-1]
    others = [stiff_pad[2:, 1:-1], stiff_pad[:-2, 1:-1], stiff_pad[1:-1, 2:], stiff_pad[1:-1, :-2],
              y_shift(center, 1), y_shift(center, -1)]
    faces = [0.5 * (center + other) for other in others]
    diag = faces[0] + faces[1] + faces[2] + faces[3] + faces[4] + faces[5] + spring_term * center
    return faces, diag, center


def neighbours(u_pad):
    center = u_pad[:, 1:-1, 1:-1]
    return center, [u_pad[:, 2:, 1:-1], u_pad[:, :-2, 1:-1], u_pad[:, 1:-1, 2:], u_pad[:, 1:-1, :-2],
                    y_shift(center, 1), y_shift(center, -1)]


def apply_op(u_pad, faces, diag):
    center, others = neighbours(u_pad)
    result = diag * center
    for face, other in zip(faces, others):
        result = result - face * other
    return result, center


def strain_energy(u_pad, faces):
    center, others = neighbours(u_pad)
    total = jnp.zeros(center.shape, jnp.float32)
    for face, other in zip(faces, others):
        diff = center - other
        total = total + face * diff * diff
    return 0.25 * jnp.sum(total, axis=0)


def on_device(concentration, order_field, phase_labels, displacement, body_load):
    h = FINE_HALO
    fields = jnp.stack([concentration, order_field, mobility_of(phase_labels)])
    m = MECH_HALO
    fields = padded_2(fields, (("gx", 1),), h)
    fields, ub = lax.optimization_barrier((fields, jnp.concatenate([displacement, body_load])))
    ub = padded_2(ub, (("gx", 1),), m)
    fields = padded_2(fields, (("gy", 2),), h)
    conc, order, mob = fields[0], fields[1], fields[2]
    for step in range(STEPS):
        conc, order, mob = advance(conc, order, mob, step == STEPS - 1)

    order, ub = lax.optimization_barrier((order, ub))
    ub = padded_2(ub, (("gy", 2),), m + 1)
    disp, load = ub[:3], ub[3:]

    coarse = restrict_xzy(order)
    stiff = lax.all_to_all(coarse, "gy", split_axis=1, concat_axis=2, tiled=True)
    stiff_ext = halo_exchange(stiff[None], m, 0)[0]
    bx, bz = stiff.shape[0], stiff.shape[1]
    disp, energy = mechanics(stiff_ext, ub, TILE - (m + 1), bx, bz)
    tiles = lax.all_to_all(energy, "gy", split_axis=2, concat_axis=1, tiled=True)
    return (conc, order, disp, jnp.transpose(tiles, (0, 2, 1)))


def solution(mesh):
    return jax.shard_map(
        on_device,
        mesh=mesh,
        in_specs=(
            P("gx", "gy", None),
            P("gx", "gy", None),
            P("gx", "gy", None),
            P(None, "gx", "gy", None),
            P(None, "gx", "gy", None),
        ),
        out_specs=(
            P("gx", "gy", None),
            P("gx", "gy", None),
            P(None, "gx", "gy", None),
            P("gx", "gy", None),
        ),
        check_vma=False,
    )
```

```python
import jax
import jax.numpy as jnp
import functools

import numpy as np
from jax import lax
from jax.experimental import pallas as pl
from jax.experimental.pallas import tpu as pltpu
from jax.sharding import PartitionSpec as P

STEPS = 4
FINE_HALO = 4
MECH_HALO = 3

rate_conc = 0.15
rate_order = 0.15
well_height = 1.0
drive_coupling = 0.5
spring_term = 0.2
first_weight = 0.5956
second_weight = 2.695


MESH = pl.DeviceIdType.MESH
TILE = 8
DIRS = [(sx, sy) for sx in (-1, 0, 1) for sy in (-1, 0, 1) if (sx, sy) != (0, 0)]


def _src_window(side, size, width):
    return {1: slice(size - width, size), -1: slice(0, width), 0: slice(0, size)}[side]


def _dst_window(side, size, width):
    return {1: slice(0, width), -1: slice(width + size, size + 2 * width), 0: slice(width, width + size)}[side]


def halo_kernel(hx, nx, ny, blk_ref, out_ref, ext, send_sem, recv_sem):
    c, x, y, z = blk_ref.shape
    t = TILE
    gx = lax.axis_index("gx")
    gy = lax.axis_index("gy")

    def exists(sx, sy):
        return (gx + sx >= 0) & (gx + sx < nx) & (gy + sy >= 0) & (gy + sy < ny)

    barrier = pltpu.get_barrier_semaphore()
    for sx, sy in DIRS:
        @pl.when(exists(sx, sy))
        def _():
            pl.semaphore_signal(barrier, inc=1, device_id=(gx + sx, gy + sy), device_id_type=MESH)
    row = (gx + nx - 1) // nx + 1 + (2 * nx - 2 - gx) // nx
    col = (gy + ny - 1) // ny + 1 + (2 * ny - 2 - gy) // ny
    pl.semaphore_wait(barrier, row * col - 1)

    copies = []
    for k, (sx, sy) in enumerate(DIRS):
        copy = pltpu.make_async_remote_copy(
            src_ref=blk_ref.at[:, _src_window(sx, x, hx), _src_window(sy, y, t), :],
            dst_ref=ext.at[:, _dst_window(sx, x, hx), _dst_window(sy, y, t), :],
            send_sem=send_sem.at[k],
            recv_sem=recv_sem.at[k],
            device_id=(lax.rem(gx + sx + nx, nx), lax.rem(gy + sy + ny, ny)),
            device_id_type=MESH,
        )
        copies.append(copy)

        @pl.when(exists(sx, sy))
        def _():
            copy.start()

    ext[:, hx:hx + x, t:t + y, :] = blk_ref[...]
    for sx, sy in DIRS:
        xs, ys = _dst_window(sx, x, hx), _dst_window(sy, y, t)

        @pl.when(jnp.logical_not(exists(-sx, -sy)))
        def _():
            ext[:, xs, ys, :] = jnp.zeros((c, xs.stop - xs.start, ys.stop - ys.start, z), ext.dtype)

    for (sx, sy), copy in zip(DIRS, copies):
        @pl.when(exists(sx, sy))
        def _():
            copy.wait_send()

        @pl.when(exists(-sx, -sy))
        def _():
            copy.wait_recv()
    out_ref[...] = ext[...]


def halo_exchange(block, hx, cid):
    c, x, y, z = block.shape
    nx, ny = lax.axis_size("gx"), lax.axis_size("gy")
    shape = (c, x + 2 * hx, y + 2 * TILE, z)
    return pl.pallas_call(
        functools.partial(halo_kernel, hx, nx, ny),
        out_shape=jax.ShapeDtypeStruct(shape, block.dtype),
        in_specs=[pl.BlockSpec(memory_space=pltpu.VMEM)],
        out_specs=pl.BlockSpec(memory_space=pltpu.VMEM),
        scratch_shapes=[
            pltpu.VMEM(shape, block.dtype),
            pltpu.SemaphoreType.DMA((len(DIRS),)),
            pltpu.SemaphoreType.DMA((len(DIRS),)),
        ],
        compiler_params=pltpu.CompilerParams(collective_id=cid, has_side_effects=True),
    )(block)


def _rolls(v):
    lane = lax.broadcasted_iota(jnp.int32, v.shape, 1)
    last = v.shape[1] - 1
    return (pltpu.roll(v, v.shape[0] - 1, 0), pltpu.roll(v, 1, 0),
            jnp.where(lane == last, 0.0, pltpu.roll(v, last, 1)), jnp.where(lane == 0, 0.0, pltpu.roll(v, 1, 1)))


def mech_kernel(zoff, s_ref, ub_ref, disp_out, energy_out, u1, u2, fc):
    _, nxe, nz, _ = ub_ref.shape
    bx, bz = disp_out.shape[1], disp_out.shape[2]
    m = (nxe - bx) // 2
    lo = (nz - bz) // 2

    def align(i, carry):
        fc[7, i] = s_ref[i, pl.ds(zoff, nz), :]
        return carry

    lax.fori_loop(0, nxe, align, 0, unroll=2)

    def faces_row(i, carry):
        c = fc[7, i]
        zp, zm, yp, ym = _rolls(c)
        diag = None
        for f, o in enumerate((fc[7, i + 1], fc[7, i - 1], zp, zm, yp, ym)):
            face = 0.5 * (c + o)
            fc[f, i] = face
            diag = face if diag is None else diag + face
        fc[6, i] = diag + spring_term * c
        return carry

    lax.fori_loop(1, nxe - 1, faces_row, 0, unroll=2)

    def sweep(src, dst, weight, i):
        c, diag = fc[7, i], fc[6, i]
        for k in range(3):
            u = src[k, i]
            others = (src[k, i + 1], src[k, i - 1]) + _rolls(u)
            result = diag * u
            for f, other in enumerate(others):
                result = result - fc[f, i] * other
            new = u + weight * (ub_ref[3 + k, i] - result) / diag
            dst[k, i] = jnp.where(c > 0, new, 0.0)

    def first(i, carry):
        sweep(ub_ref, u1, first_weight, i)
        return carry

    def second(i, carry):
        sweep(u1, u2, second_weight, i)
        return carry

    lax.fori_loop(1, nxe - 1, first, 0, unroll=2)
    lax.fori_loop(2, nxe - 2, second, 0, unroll=2)

    def energy_row(i, carry):
        parts = []
        for k in range(3):
            u = u2[k, i]
            others = (u2[k, i + 1], u2[k, i - 1]) + _rolls(u)
            total = jnp.zeros(u.shape, jnp.float32)
            for f, other in enumerate(others):
                diff = u - other
                total = total + fc[f, i] * diff * diff
            parts.append(total)
        u1[0, i] = 0.25 * (parts[0] + parts[1] + parts[2])
        return carry

    lax.fori_loop(m, m + bx, energy_row, 0, unroll=2)
    energy_out[...] = u1[0, pl.ds(m, bx), pl.ds(lo, bz), :]
    disp_out[...] = u2[:, pl.ds(m, bx), pl.ds(lo, bz), :]


def mechanics(stiff_ext, ub, zoff, bx, bz):
    _, nxe, nz, ny = ub.shape
    return pl.pallas_call(
        functools.partial(mech_kernel, zoff),
        out_shape=(jax.ShapeDtypeStruct((3, bx, bz, ny), jnp.float32),
                   jax.ShapeDtypeStruct((bx, bz, ny), jnp.float32)),
        in_specs=[pl.BlockSpec(memory_space=pltpu.VMEM)] * 2,
        out_specs=(pl.BlockSpec(memory_space=pltpu.VMEM), pl.BlockSpec(memory_space=pltpu.VMEM)),
        scratch_shapes=[pltpu.VMEM((3, nxe, nz, ny), jnp.float32), pltpu.VMEM((3, nxe, nz, ny), jnp.float32),
                        pltpu.VMEM((8, nxe, nz, ny), jnp.float32)],
    )(stiff_ext, ub)


def padded_2(block, sides, width):
    for axis, dim in sides:
        count = lax.axis_size(axis)
        forward = [(i, i + 1) for i in range(count - 1)]
        backward = [(target, source) for source, target in forward]
        low = lax.ppermute(
            lax.slice_in_dim(block, block.shape[dim] - width, None, axis=dim), axis, forward
        )
        high = lax.ppermute(lax.slice_in_dim(block, 0, width, axis=dim), axis, backward)
        block = jnp.concatenate([low, block, high], axis=dim)
    return block


def fine_laplace(padded):
    zpad = jnp.pad(padded, ((0, 0), (0, 0), (1, 1)))
    center = zpad[1:-1, 1:-1, 1:-1]
    total = zpad[2:, 1:-1, 1:-1] + zpad[:-2, 1:-1, 1:-1]
    total = total + zpad[1:-1, 2:, 1:-1] + zpad[1:-1, :-2, 1:-1]
    total = total + zpad[1:-1, 1:-1, 2:] + zpad[1:-1, 1:-1, :-2]
    return total - 6.0 * center


def advance(conc_pad, order_pad, mob_pad, last):
    chem = conc_pad - order_pad * order_pad * (3.0 - 2.0 * order_pad)
    conc_in = conc_pad[1:-1, 1:-1]
    order_in = order_pad[1:-1, 1:-1]
    chem_in = chem[1:-1, 1:-1]
    mobility = mob_pad[1:-1, 1:-1]
    conc_new = conc_in + rate_conc * fine_laplace(chem)
    dh_term = 6.0 * order_in * (1.0 - order_in)
    dg_term = 2.0 * order_in * (1.0 - order_in) * (1.0 - 2.0 * order_in)
    order_new = order_in + mobility * (
        rate_order * fine_laplace(order_pad)
        - well_height * dg_term
        + drive_coupling * chem_in * dh_term
    )
    if not last:
        conc_new = jnp.where(mobility > 0, conc_new, 0.0)
    return conc_new, order_new, mobility


def mobility_of(labels):
    return (0.5 * (labels == 0) + 1.0 * (labels == 1) + 0.25 * (labels == 2)).astype(jnp.float32)


def restrict_xzy(order_out):
    sx, sy, sz = order_out.shape
    sq = order_out * order_out
    sq = sq.reshape(sx // 2, 2, sy, sz).sum(axis=1)
    sq = sq.reshape(sx // 2, sy // 2, 2, sz).sum(axis=2)
    pairs = jnp.asarray(np.repeat(np.eye(sz // 2, dtype=np.float32), 2, axis=0))
    summed = jnp.einsum("xyz,zw->xwy", sq, pairs, precision=lax.Precision.HIGHEST)
    return 0.1 + 0.125 * summed


def y_shift(v, step):
    if step > 0:
        return jnp.pad(v[..., step:], [(0, 0)] * (v.ndim - 1) + [(0, step)])
    return jnp.pad(v[..., :step], [(0, 0)] * (v.ndim - 1) + [(-step, 0)])


def face_terms(stiff_pad):
    center = stiff_pad[1:-1, 1:-1]
    others = [stiff_pad[2:, 1:-1], stiff_pad[:-2, 1:-1], stiff_pad[1:-1, 2:], stiff_pad[1:-1, :-2],
              y_shift(center, 1), y_shift(center, -1)]
    faces = [0.5 * (center + other) for other in others]
    diag = faces[0] + faces[1] + faces[2] + faces[3] + faces[4] + faces[5] + spring_term * center
    return faces, diag, center


def neighbours(u_pad):
    center = u_pad[:, 1:-1, 1:-1]
    return center, [u_pad[:, 2:, 1:-1], u_pad[:, :-2, 1:-1], u_pad[:, 1:-1, 2:], u_pad[:, 1:-1, :-2],
                    y_shift(center, 1), y_shift(center, -1)]


def apply_op(u_pad, faces, diag):
    center, others = neighbours(u_pad)
    result = diag * center
    for face, other in zip(faces, others):
        result = result - face * other
    return result, center


def strain_energy(u_pad, faces):
    center, others = neighbours(u_pad)
    total = jnp.zeros(center.shape, jnp.float32)
    for face, other in zip(faces, others):
        diff = center - other
        total = total + face * diff * diff
    return 0.25 * jnp.sum(total, axis=0)


def on_device(concentration, order_field, phase_labels, displacement, body_load):
    h = FINE_HALO
    fields = jnp.stack([concentration, order_field, mobility_of(phase_labels)])
    m = MECH_HALO
    fields = padded_2(fields, (("gx", 1),), h)
    fields, ub = lax.optimization_barrier((fields, jnp.concatenate([displacement, body_load])))
    ub = padded_2(ub, (("gx", 1),), m)
    fields = padded_2(fields, (("gy", 2),), h)
    conc, order, mob = fields[0], fields[1], fields[2]
    for step in range(STEPS):
        conc, order, mob = advance(conc, order, mob, step == STEPS - 1)

    order, ub = lax.optimization_barrier((order, ub))
    ub = padded_2(ub, (("gy", 2),), m + 1)
    disp, load = ub[:3], ub[3:]

    coarse = restrict_xzy(order)
    stiff = lax.all_to_all(coarse, "gy", split_axis=1, concat_axis=2, tiled=True)
    stiff_ext = halo_exchange(stiff[None], m, 0)[0]
    bx, bz = stiff.shape[0], stiff.shape[1]
    disp, energy = mechanics(stiff_ext, ub, TILE - (m + 1), bx, bz)
    tiles = lax.all_to_all(energy, "gy", split_axis=2, concat_axis=1, tiled=True)
    return (conc, order, disp, jnp.transpose(tiles, (0, 2, 1)))


def solution(mesh):
    return jax.shard_map(
        on_device,
        mesh=mesh,
        in_specs=(
            P("gx", "gy", None),
            P("gx", "gy", None),
            P("gx", "gy", None),
            P(None, "gx", "gy", None),
            P(None, "gx", "gy", None),
        ),
        out_specs=(
            P("gx", "gy", None),
            P("gx", "gy", None),
            P(None, "gx", "gy", None),
            P("gx", "gy", None),
        ),
        check_vma=False,
    )
```

```python
import jax
import jax.numpy as jnp
import functools

import numpy as np
from jax import lax
from jax.experimental import pallas as pl
from jax.experimental.pallas import tpu as pltpu
from jax.sharding import PartitionSpec as P

STEPS = 4
FINE_HALO = 4
MECH_HALO = 3

rate_conc = 0.15
rate_order = 0.15
well_height = 1.0
drive_coupling = 0.5
spring_term = 0.2
first_weight = 0.5956
second_weight = 2.695


MESH = pl.DeviceIdType.MESH
TILE = 8
DIRS = [(sx, sy) for sx in (-1, 0, 1) for sy in (-1, 0, 1) if (sx, sy) != (0, 0)]


def _src_window(side, size, width):
    return {1: slice(size - width, size), -1: slice(0, width), 0: slice(0, size)}[side]


def _dst_window(side, size, width):
    return {1: slice(0, width), -1: slice(width + size, size + 2 * width), 0: slice(width, width + size)}[side]


def halo_kernel(hx, nx, ny, blk_ref, out_ref, ext, send_sem, recv_sem):
    c, x, y, z = blk_ref.shape
    t = TILE
    gx = lax.axis_index("gx")
    gy = lax.axis_index("gy")

    def exists(sx, sy):
        return (gx + sx >= 0) & (gx + sx < nx) & (gy + sy >= 0) & (gy + sy < ny)

    barrier = pltpu.get_barrier_semaphore()
    for sx, sy in DIRS:
        @pl.when(exists(sx, sy))
        def _():
            pl.semaphore_signal(barrier, inc=1, device_id=(gx + sx, gy + sy), device_id_type=MESH)
    row = (gx + nx - 1) // nx + 1 + (2 * nx - 2 - gx) // nx
    col = (gy + ny - 1) // ny + 1 + (2 * ny - 2 - gy) // ny
    pl.semaphore_wait(barrier, row * col - 1)

    copies = []
    for k, (sx, sy) in enumerate(DIRS):
        copy = pltpu.make_async_remote_copy(
            src_ref=blk_ref.at[:, _src_window(sx, x, hx), _src_window(sy, y, t), :],
            dst_ref=ext.at[:, _dst_window(sx, x, hx), _dst_window(sy, y, t), :],
            send_sem=send_sem.at[k],
            recv_sem=recv_sem.at[k],
            device_id=(lax.rem(gx + sx + nx, nx), lax.rem(gy + sy + ny, ny)),
            device_id_type=MESH,
        )
        copies.append(copy)

        @pl.when(exists(sx, sy))
        def _():
            copy.start()

    ext[:, hx:hx + x, t:t + y, :] = blk_ref[...]
    for sx, sy in DIRS:
        xs, ys = _dst_window(sx, x, hx), _dst_window(sy, y, t)

        @pl.when(jnp.logical_not(exists(-sx, -sy)))
        def _():
            ext[:, xs, ys, :] = jnp.zeros((c, xs.stop - xs.start, ys.stop - ys.start, z), ext.dtype)

    for (sx, sy), copy in zip(DIRS, copies):
        @pl.when(exists(sx, sy))
        def _():
            copy.wait_send()

        @pl.when(exists(-sx, -sy))
        def _():
            copy.wait_recv()
    out_ref[...] = ext[...]


def halo_exchange(block, hx, cid):
    c, x, y, z = block.shape
    nx, ny = lax.axis_size("gx"), lax.axis_size("gy")
    shape = (c, x + 2 * hx, y + 2 * TILE, z)
    return pl.pallas_call(
        functools.partial(halo_kernel, hx, nx, ny),
        out_shape=jax.ShapeDtypeStruct(shape, block.dtype),
        in_specs=[pl.BlockSpec(memory_space=pltpu.VMEM)],
        out_specs=pl.BlockSpec(memory_space=pltpu.VMEM),
        scratch_shapes=[
            pltpu.VMEM(shape, block.dtype),
            pltpu.SemaphoreType.DMA((len(DIRS),)),
            pltpu.SemaphoreType.DMA((len(DIRS),)),
        ],
        compiler_params=pltpu.CompilerParams(collective_id=cid, has_side_effects=True),
    )(block)


def _rolls(v):
    lane = lax.broadcasted_iota(jnp.int32, v.shape, 1)
    last = v.shape[1] - 1
    return (pltpu.roll(v, v.shape[0] - 1, 0), pltpu.roll(v, 1, 0),
            jnp.where(lane == last, 0.0, pltpu.roll(v, last, 1)), jnp.where(lane == 0, 0.0, pltpu.roll(v, 1, 1)))


def mech_kernel(zoff, s_ref, ub_ref, disp_out, energy_out, u1, u2, fc):
    _, nxe, nz, _ = ub_ref.shape
    bx, bz = disp_out.shape[1], disp_out.shape[2]
    m = (nxe - bx) // 2
    lo = (nz - bz) // 2

    def align(i, carry):
        fc[7, i] = s_ref[i, pl.ds(zoff, nz), :]
        return carry

    lax.fori_loop(0, nxe, align, 0, unroll=4)

    def faces_row(i, carry):
        c = fc[7, i]
        zp, zm, yp, ym = _rolls(c)
        diag = None
        for f, o in enumerate((fc[7, i + 1], fc[7, i - 1], zp, zm, yp, ym)):
            face = 0.5 * (c + o)
            fc[f, i] = face
            diag = face if diag is None else diag + face
        fc[6, i] = diag + spring_term * c
        return carry

    lax.fori_loop(1, nxe - 1, faces_row, 0, unroll=4)

    def sweep(src, dst, weight, i):
        c, diag = fc[7, i], fc[6, i]
        for k in range(3):
            u = src[k, i]
            others = (src[k, i + 1], src[k, i - 1]) + _rolls(u)
            result = diag * u
            for f, other in enumerate(others):
                result = result - fc[f, i] * other
            new = u + weight * (ub_ref[3 + k, i] - result) / diag
            dst[k, i] = jnp.where(c > 0, new, 0.0)

    def first(i, carry):
        sweep(ub_ref, u1, first_weight, i)
        return carry

    def second(i, carry):
        sweep(u1, u2, second_weight, i)
        return carry

    lax.fori_loop(1, nxe - 1, first, 0, unroll=4)
    lax.fori_loop(2, nxe - 2, second, 0, unroll=4)

    def energy_row(i, carry):
        parts = []
        for k in range(3):
            u = u2[k, i]
            others = (u2[k, i + 1], u2[k, i - 1]) + _rolls(u)
            total = jnp.zeros(u.shape, jnp.float32)
            for f, other in enumerate(others):
                diff = u - other
                total = total + fc[f, i] * diff * diff
            parts.append(total)
        u1[0, i] = 0.25 * (parts[0] + parts[1] + parts[2])
        return carry

    lax.fori_loop(m, m + bx, energy_row, 0, unroll=4)
    energy_out[...] = u1[0, pl.ds(m, bx), pl.ds(lo, bz), :]
    disp_out[...] = u2[:, pl.ds(m, bx), pl.ds(lo, bz), :]


def mechanics(stiff_ext, ub, zoff, bx, bz):
    _, nxe, nz, ny = ub.shape
    return pl.pallas_call(
        functools.partial(mech_kernel, zoff),
        out_shape=(jax.ShapeDtypeStruct((3, bx, bz, ny), jnp.float32),
                   jax.ShapeDtypeStruct((bx, bz, ny), jnp.float32)),
        in_specs=[pl.BlockSpec(memory_space=pltpu.VMEM)] * 2,
        out_specs=(pl.BlockSpec(memory_space=pltpu.VMEM), pl.BlockSpec(memory_space=pltpu.VMEM)),
        scratch_shapes=[pltpu.VMEM((3, nxe, nz, ny), jnp.float32), pltpu.VMEM((3, nxe, nz, ny), jnp.float32),
                        pltpu.VMEM((8, nxe, nz, ny), jnp.float32)],
    )(stiff_ext, ub)


def padded_2(block, sides, width):
    for axis, dim in sides:
        count = lax.axis_size(axis)
        forward = [(i, i + 1) for i in range(count - 1)]
        backward = [(target, source) for source, target in forward]
        low = lax.ppermute(
            lax.slice_in_dim(block, block.shape[dim] - width, None, axis=dim), axis, forward
        )
        high = lax.ppermute(lax.slice_in_dim(block, 0, width, axis=dim), axis, backward)
        block = jnp.concatenate([low, block, high], axis=dim)
    return block


def fine_laplace(padded):
    zpad = jnp.pad(padded, ((0, 0), (0, 0), (1, 1)))
    center = zpad[1:-1, 1:-1, 1:-1]
    total = zpad[2:, 1:-1, 1:-1] + zpad[:-2, 1:-1, 1:-1]
    total = total + zpad[1:-1, 2:, 1:-1] + zpad[1:-1, :-2, 1:-1]
    total = total + zpad[1:-1, 1:-1, 2:] + zpad[1:-1, 1:-1, :-2]
    return total - 6.0 * center


def advance(conc_pad, order_pad, mob_pad, last):
    chem = conc_pad - order_pad * order_pad * (3.0 - 2.0 * order_pad)
    conc_in = conc_pad[1:-1, 1:-1]
    order_in = order_pad[1:-1, 1:-1]
    chem_in = chem[1:-1, 1:-1]
    mobility = mob_pad[1:-1, 1:-1]
    conc_new = conc_in + rate_conc * fine_laplace(chem)
    dh_term = 6.0 * order_in * (1.0 - order_in)
    dg_term = 2.0 * order_in * (1.0 - order_in) * (1.0 - 2.0 * order_in)
    order_new = order_in + mobility * (
        rate_order * fine_laplace(order_pad)
        - well_height * dg_term
        + drive_coupling * chem_in * dh_term
    )
    if not last:
        conc_new = jnp.where(mobility > 0, conc_new, 0.0)
    return conc_new, order_new, mobility


def mobility_of(labels):
    return (0.5 * (labels == 0) + 1.0 * (labels == 1) + 0.25 * (labels == 2)).astype(jnp.float32)


def restrict_xzy(order_out):
    sx, sy, sz = order_out.shape
    sq = order_out * order_out
    sq = sq.reshape(sx // 2, 2, sy, sz).sum(axis=1)
    sq = sq.reshape(sx // 2, sy // 2, 2, sz).sum(axis=2)
    pairs = jnp.asarray(np.repeat(np.eye(sz // 2, dtype=np.float32), 2, axis=0))
    summed = jnp.einsum("xyz,zw->xwy", sq, pairs, precision=lax.Precision.HIGHEST)
    return 0.1 + 0.125 * summed


def y_shift(v, step):
    if step > 0:
        return jnp.pad(v[..., step:], [(0, 0)] * (v.ndim - 1) + [(0, step)])
    return jnp.pad(v[..., :step], [(0, 0)] * (v.ndim - 1) + [(-step, 0)])


def face_terms(stiff_pad):
    center = stiff_pad[1:-1, 1:-1]
    others = [stiff_pad[2:, 1:-1], stiff_pad[:-2, 1:-1], stiff_pad[1:-1, 2:], stiff_pad[1:-1, :-2],
              y_shift(center, 1), y_shift(center, -1)]
    faces = [0.5 * (center + other) for other in others]
    diag = faces[0] + faces[1] + faces[2] + faces[3] + faces[4] + faces[5] + spring_term * center
    return faces, diag, center


def neighbours(u_pad):
    center = u_pad[:, 1:-1, 1:-1]
    return center, [u_pad[:, 2:, 1:-1], u_pad[:, :-2, 1:-1], u_pad[:, 1:-1, 2:], u_pad[:, 1:-1, :-2],
                    y_shift(center, 1), y_shift(center, -1)]


def apply_op(u_pad, faces, diag):
    center, others = neighbours(u_pad)
    result = diag * center
    for face, other in zip(faces, others):
        result = result - face * other
    return result, center


def strain_energy(u_pad, faces):
    center, others = neighbours(u_pad)
    total = jnp.zeros(center.shape, jnp.float32)
    for face, other in zip(faces, others):
        diff = center - other
        total = total + face * diff * diff
    return 0.25 * jnp.sum(total, axis=0)


def on_device(concentration, order_field, phase_labels, displacement, body_load):
    h = FINE_HALO
    fields = jnp.stack([concentration, order_field, mobility_of(phase_labels)])
    m = MECH_HALO
    fields = padded_2(fields, (("gx", 1),), h)
    fields, ub = lax.optimization_barrier((fields, jnp.concatenate([displacement, body_load])))
    ub = padded_2(ub, (("gx", 1),), m)
    fields = padded_2(fields, (("gy", 2),), h)
    conc, order, mob = fields[0], fields[1], fields[2]
    for step in range(STEPS):
        conc, order, mob = advance(conc, order, mob, step == STEPS - 1)

    order, ub = lax.optimization_barrier((order, ub))
    ub = padded_2(ub, (("gy", 2),), m + 1)
    disp, load = ub[:3], ub[3:]

    coarse = restrict_xzy(order)
    stiff = lax.all_to_all(coarse, "gy", split_axis=1, concat_axis=2, tiled=True)
    stiff_ext = halo_exchange(stiff[None], m, 0)[0]
    bx, bz = stiff.shape[0], stiff.shape[1]
    disp, energy = mechanics(stiff_ext, ub, TILE - (m + 1), bx, bz)
    tiles = lax.all_to_all(energy, "gy", split_axis=2, concat_axis=1, tiled=True)
    return (conc, order, disp, jnp.transpose(tiles, (0, 2, 1)))


def solution(mesh):
    return jax.shard_map(
        on_device,
        mesh=mesh,
        in_specs=(
            P("gx", "gy", None),
            P("gx", "gy", None),
            P("gx", "gy", None),
            P(None, "gx", "gy", None),
            P(None, "gx", "gy", None),
        ),
        out_specs=(
            P("gx", "gy", None),
            P("gx", "gy", None),
            P(None, "gx", "gy", None),
            P("gx", "gy", None),
        ),
        check_vma=False,
    )
```

```python
import jax
import jax.numpy as jnp
import functools

import numpy as np
from jax import lax
from jax.experimental import pallas as pl
from jax.experimental.pallas import tpu as pltpu
from jax.sharding import PartitionSpec as P

STEPS = 4
FINE_HALO = 4
MECH_HALO = 3

rate_conc = 0.15
rate_order = 0.15
well_height = 1.0
drive_coupling = 0.5
spring_term = 0.2
first_weight = 0.5956
second_weight = 2.695


MESH = pl.DeviceIdType.MESH
TILE = 8
DIRS = [(sx, sy) for sx in (-1, 0, 1) for sy in (-1, 0, 1) if (sx, sy) != (0, 0)]


def _src_window(side, size, width):
    return {1: slice(size - width, size), -1: slice(0, width), 0: slice(0, size)}[side]


def _dst_window(side, size, width):
    return {1: slice(0, width), -1: slice(width + size, size + 2 * width), 0: slice(width, width + size)}[side]


def halo_kernel(hx, nx, ny, blk_ref, out_ref, ext, send_sem, recv_sem):
    c, x, y, z = blk_ref.shape
    t = TILE
    gx = lax.axis_index("gx")
    gy = lax.axis_index("gy")

    def exists(sx, sy):
        return (gx + sx >= 0) & (gx + sx < nx) & (gy + sy >= 0) & (gy + sy < ny)

    barrier = pltpu.get_barrier_semaphore()
    for sx, sy in DIRS:
        @pl.when(exists(sx, sy))
        def _():
            pl.semaphore_signal(barrier, inc=1, device_id=(gx + sx, gy + sy), device_id_type=MESH)
    row = (gx + nx - 1) // nx + 1 + (2 * nx - 2 - gx) // nx
    col = (gy + ny - 1) // ny + 1 + (2 * ny - 2 - gy) // ny
    pl.semaphore_wait(barrier, row * col - 1)

    copies = []
    for k, (sx, sy) in enumerate(DIRS):
        copy = pltpu.make_async_remote_copy(
            src_ref=blk_ref.at[:, _src_window(sx, x, hx), _src_window(sy, y, t), :],
            dst_ref=ext.at[:, _dst_window(sx, x, hx), _dst_window(sy, y, t), :],
            send_sem=send_sem.at[k],
            recv_sem=recv_sem.at[k],
            device_id=(lax.rem(gx + sx + nx, nx), lax.rem(gy + sy + ny, ny)),
            device_id_type=MESH,
        )
        copies.append(copy)

        @pl.when(exists(sx, sy))
        def _():
            copy.start()

    ext[:, hx:hx + x, t:t + y, :] = blk_ref[...]
    for sx, sy in DIRS:
        xs, ys = _dst_window(sx, x, hx), _dst_window(sy, y, t)

        @pl.when(jnp.logical_not(exists(-sx, -sy)))
        def _():
            ext[:, xs, ys, :] = jnp.zeros((c, xs.stop - xs.start, ys.stop - ys.start, z), ext.dtype)

    for (sx, sy), copy in zip(DIRS, copies):
        @pl.when(exists(sx, sy))
        def _():
            copy.wait_send()

        @pl.when(exists(-sx, -sy))
        def _():
            copy.wait_recv()
    out_ref[...] = ext[...]


def halo_exchange(block, hx, cid):
    c, x, y, z = block.shape
    nx, ny = lax.axis_size("gx"), lax.axis_size("gy")
    shape = (c, x + 2 * hx, y + 2 * TILE, z)
    return pl.pallas_call(
        functools.partial(halo_kernel, hx, nx, ny),
        out_shape=jax.ShapeDtypeStruct(shape, block.dtype),
        in_specs=[pl.BlockSpec(memory_space=pltpu.VMEM)],
        out_specs=pl.BlockSpec(memory_space=pltpu.VMEM),
        scratch_shapes=[
            pltpu.VMEM(shape, block.dtype),
            pltpu.SemaphoreType.DMA((len(DIRS),)),
            pltpu.SemaphoreType.DMA((len(DIRS),)),
        ],
        compiler_params=pltpu.CompilerParams(collective_id=cid, has_side_effects=True),
    )(block)


def _rolls(v):
    lane = lax.broadcasted_iota(jnp.int32, v.shape, 1)
    last = v.shape[1] - 1
    return (pltpu.roll(v, v.shape[0] - 1, 0), pltpu.roll(v, 1, 0),
            jnp.where(lane == last, 0.0, pltpu.roll(v, last, 1)), jnp.where(lane == 0, 0.0, pltpu.roll(v, 1, 1)))


def mech_kernel(zoff, ext_ref, disp_out, energy_out, u1, u2, fc, ub_ref):
    _, nxe, nz, _ = ub_ref.shape
    bx, bz = disp_out.shape[1], disp_out.shape[2]
    m = (nxe - bx) // 2
    lo = (nz - bz) // 2

    def align(i, carry):
        fc[7, i] = ext_ref[0, i, pl.ds(zoff, nz), :]
        for k in range(6):
            ub_ref[k, i] = ext_ref[1 + k, i, pl.ds(zoff, nz), :]
        return carry

    lax.fori_loop(0, nxe, align, 0, unroll=4)

    def faces_row(i, carry):
        c = fc[7, i]
        zp, zm, yp, ym = _rolls(c)
        diag = None
        for f, o in enumerate((fc[7, i + 1], fc[7, i - 1], zp, zm, yp, ym)):
            face = 0.5 * (c + o)
            fc[f, i] = face
            diag = face if diag is None else diag + face
        fc[6, i] = diag + spring_term * c
        return carry

    lax.fori_loop(1, nxe - 1, faces_row, 0, unroll=4)

    def sweep(src, dst, weight, i):
        c, diag = fc[7, i], fc[6, i]
        for k in range(3):
            u = src[k, i]
            others = (src[k, i + 1], src[k, i - 1]) + _rolls(u)
            result = diag * u
            for f, other in enumerate(others):
                result = result - fc[f, i] * other
            new = u + weight * (ub_ref[3 + k, i] - result) / diag
            dst[k, i] = jnp.where(c > 0, new, 0.0)

    def first(i, carry):
        sweep(ub_ref, u1, first_weight, i)
        return carry

    def second(i, carry):
        sweep(u1, u2, second_weight, i)
        return carry

    lax.fori_loop(1, nxe - 1, first, 0, unroll=4)
    lax.fori_loop(2, nxe - 2, second, 0, unroll=4)

    def energy_row(i, carry):
        parts = []
        for k in range(3):
            u = u2[k, i]
            others = (u2[k, i + 1], u2[k, i - 1]) + _rolls(u)
            total = jnp.zeros(u.shape, jnp.float32)
            for f, other in enumerate(others):
                diff = u - other
                total = total + fc[f, i] * diff * diff
            parts.append(total)
        u1[0, i] = 0.25 * (parts[0] + parts[1] + parts[2])
        return carry

    lax.fori_loop(m, m + bx, energy_row, 0, unroll=4)
    energy_out[...] = u1[0, pl.ds(m, bx), pl.ds(lo, bz), :]
    disp_out[...] = u2[:, pl.ds(m, bx), pl.ds(lo, bz), :]


def mechanics(ext, zoff, nz, bx, bz):
    _, nxe, _, ny = ext.shape
    return pl.pallas_call(
        functools.partial(mech_kernel, zoff),
        out_shape=(jax.ShapeDtypeStruct((3, bx, bz, ny), jnp.float32),
                   jax.ShapeDtypeStruct((bx, bz, ny), jnp.float32)),
        in_specs=[pl.BlockSpec(memory_space=pltpu.VMEM)],
        out_specs=(pl.BlockSpec(memory_space=pltpu.VMEM), pl.BlockSpec(memory_space=pltpu.VMEM)),
        scratch_shapes=[pltpu.VMEM((3, nxe, nz, ny), jnp.float32), pltpu.VMEM((3, nxe, nz, ny), jnp.float32),
                        pltpu.VMEM((8, nxe, nz, ny), jnp.float32), pltpu.VMEM((6, nxe, nz, ny), jnp.float32)],
    )(ext)


def padded_2(block, sides, width):
    for axis, dim in sides:
        count = lax.axis_size(axis)
        forward = [(i, i + 1) for i in range(count - 1)]
        backward = [(target, source) for source, target in forward]
        low = lax.ppermute(
            lax.slice_in_dim(block, block.shape[dim] - width, None, axis=dim), axis, forward
        )
        high = lax.ppermute(lax.slice_in_dim(block, 0, width, axis=dim), axis, backward)
        block = jnp.concatenate([low, block, high], axis=dim)
    return block


def fine_laplace(padded):
    zpad = jnp.pad(padded, ((0, 0), (0, 0), (1, 1)))
    center = zpad[1:-1, 1:-1, 1:-1]
    total = zpad[2:, 1:-1, 1:-1] + zpad[:-2, 1:-1, 1:-1]
    total = total + zpad[1:-1, 2:, 1:-1] + zpad[1:-1, :-2, 1:-1]
    total = total + zpad[1:-1, 1:-1, 2:] + zpad[1:-1, 1:-1, :-2]
    return total - 6.0 * center


def advance(conc_pad, order_pad, mob_pad, last):
    chem = conc_pad - order_pad * order_pad * (3.0 - 2.0 * order_pad)
    conc_in = conc_pad[1:-1, 1:-1]
    order_in = order_pad[1:-1, 1:-1]
    chem_in = chem[1:-1, 1:-1]
    mobility = mob_pad[1:-1, 1:-1]
    conc_new = conc_in + rate_conc * fine_laplace(chem)
    dh_term = 6.0 * order_in * (1.0 - order_in)
    dg_term = 2.0 * order_in * (1.0 - order_in) * (1.0 - 2.0 * order_in)
    order_new = order_in + mobility * (
        rate_order * fine_laplace(order_pad)
        - well_height * dg_term
        + drive_coupling * chem_in * dh_term
    )
    if not last:
        conc_new = jnp.where(mobility > 0, conc_new, 0.0)
    return conc_new, order_new, mobility


def mobility_of(labels):
    return (0.5 * (labels == 0) + 1.0 * (labels == 1) + 0.25 * (labels == 2)).astype(jnp.float32)


def restrict_xzy(order_out):
    sx, sy, sz = order_out.shape
    sq = order_out * order_out
    sq = sq.reshape(sx // 2, 2, sy, sz).sum(axis=1)
    sq = sq.reshape(sx // 2, sy // 2, 2, sz).sum(axis=2)
    pairs = jnp.asarray(np.repeat(np.eye(sz // 2, dtype=np.float32), 2, axis=0))
    summed = jnp.einsum("xyz,zw->xwy", sq, pairs, precision=lax.Precision.HIGHEST)
    return 0.1 + 0.125 * summed


def y_shift(v, step):
    if step > 0:
        return jnp.pad(v[..., step:], [(0, 0)] * (v.ndim - 1) + [(0, step)])
    return jnp.pad(v[..., :step], [(0, 0)] * (v.ndim - 1) + [(-step, 0)])


def face_terms(stiff_pad):
    center = stiff_pad[1:-1, 1:-1]
    others = [stiff_pad[2:, 1:-1], stiff_pad[:-2, 1:-1], stiff_pad[1:-1, 2:], stiff_pad[1:-1, :-2],
              y_shift(center, 1), y_shift(center, -1)]
    faces = [0.5 * (center + other) for other in others]
    diag = faces[0] + faces[1] + faces[2] + faces[3] + faces[4] + faces[5] + spring_term * center
    return faces, diag, center


def neighbours(u_pad):
    center = u_pad[:, 1:-1, 1:-1]
    return center, [u_pad[:, 2:, 1:-1], u_pad[:, :-2, 1:-1], u_pad[:, 1:-1, 2:], u_pad[:, 1:-1, :-2],
                    y_shift(center, 1), y_shift(center, -1)]


def apply_op(u_pad, faces, diag):
    center, others = neighbours(u_pad)
    result = diag * center
    for face, other in zip(faces, others):
        result = result - face * other
    return result, center


def strain_energy(u_pad, faces):
    center, others = neighbours(u_pad)
    total = jnp.zeros(center.shape, jnp.float32)
    for face, other in zip(faces, others):
        diff = center - other
        total = total + face * diff * diff
    return 0.25 * jnp.sum(total, axis=0)


def on_device(concentration, order_field, phase_labels, displacement, body_load):
    h = FINE_HALO
    fields = jnp.stack([concentration, order_field, mobility_of(phase_labels)])
    m = MECH_HALO
    fields = padded_2(fields, (("gx", 1), ("gy", 2)), h)
    conc, order, mob = fields[0], fields[1], fields[2]
    for step in range(STEPS):
        conc, order, mob = advance(conc, order, mob, step == STEPS - 1)


    coarse = restrict_xzy(order)
    stiff = lax.all_to_all(coarse, "gy", split_axis=1, concat_axis=2, tiled=True)
    ext = halo_exchange(jnp.concatenate([stiff[None], displacement, body_load]), m, 0)
    bx, bz = stiff.shape[0], stiff.shape[1]
    disp, energy = mechanics(ext, TILE - (m + 1), bz + 2 * (m + 1), bx, bz)
    tiles = lax.all_to_all(energy, "gy", split_axis=2, concat_axis=1, tiled=True)
    return (conc, order, disp, jnp.transpose(tiles, (0, 2, 1)))


def solution(mesh):
    return jax.shard_map(
        on_device,
        mesh=mesh,
        in_specs=(
            P("gx", "gy", None),
            P("gx", "gy", None),
            P("gx", "gy", None),
            P(None, "gx", "gy", None),
            P(None, "gx", "gy", None),
        ),
        out_specs=(
            P("gx", "gy", None),
            P("gx", "gy", None),
            P(None, "gx", "gy", None),
            P("gx", "gy", None),
        ),
        check_vma=False,
    )
```

```python
import jax
import jax.numpy as jnp
import functools

import numpy as np
from jax import lax
from jax.experimental import pallas as pl
from jax.experimental.pallas import tpu as pltpu
from jax.sharding import PartitionSpec as P

STEPS = 4
FINE_HALO = 4
MECH_HALO = 3

rate_conc = 0.15
rate_order = 0.15
well_height = 1.0
drive_coupling = 0.5
spring_term = 0.2
first_weight = 0.5956
second_weight = 2.695


MESH = pl.DeviceIdType.MESH
TILE = 8
DIRS = [(sx, sy) for sx in (-1, 0, 1) for sy in (-1, 0, 1) if (sx, sy) != (0, 0)]


def _src_window(side, size, width):
    return {1: slice(size - width, size), -1: slice(0, width), 0: slice(0, size)}[side]


def _dst_window(side, size, width):
    return {1: slice(0, width), -1: slice(width + size, size + 2 * width), 0: slice(width, width + size)}[side]


def halo_kernel(hx, nx, ny, blk_ref, out_ref, ext, send_sem, recv_sem):
    c, x, y, z = blk_ref.shape
    t = TILE
    gx = lax.axis_index("gx")
    gy = lax.axis_index("gy")

    def exists(sx, sy):
        return (gx + sx >= 0) & (gx + sx < nx) & (gy + sy >= 0) & (gy + sy < ny)

    barrier = pltpu.get_barrier_semaphore()
    for sx, sy in DIRS:
        @pl.when(exists(sx, sy))
        def _():
            pl.semaphore_signal(barrier, inc=1, device_id=(gx + sx, gy + sy), device_id_type=MESH)
    row = (gx + nx - 1) // nx + 1 + (2 * nx - 2 - gx) // nx
    col = (gy + ny - 1) // ny + 1 + (2 * ny - 2 - gy) // ny
    pl.semaphore_wait(barrier, row * col - 1)

    copies = []
    for k, (sx, sy) in enumerate(DIRS):
        copy = pltpu.make_async_remote_copy(
            src_ref=blk_ref.at[:, _src_window(sx, x, hx), _src_window(sy, y, t), :],
            dst_ref=ext.at[:, _dst_window(sx, x, hx), _dst_window(sy, y, t), :],
            send_sem=send_sem.at[k],
            recv_sem=recv_sem.at[k],
            device_id=(lax.rem(gx + sx + nx, nx), lax.rem(gy + sy + ny, ny)),
            device_id_type=MESH,
        )
        copies.append(copy)

        @pl.when(exists(sx, sy))
        def _():
            copy.start()

    ext[:, hx:hx + x, t:t + y, :] = blk_ref[...]
    for sx, sy in DIRS:
        xs, ys = _dst_window(sx, x, hx), _dst_window(sy, y, t)

        @pl.when(jnp.logical_not(exists(-sx, -sy)))
        def _():
            ext[:, xs, ys, :] = jnp.zeros((c, xs.stop - xs.start, ys.stop - ys.start, z), ext.dtype)

    for (sx, sy), copy in zip(DIRS, copies):
        @pl.when(exists(sx, sy))
        def _():
            copy.wait_send()

        @pl.when(exists(-sx, -sy))
        def _():
            copy.wait_recv()
    out_ref[...] = ext[...]


def halo_exchange(block, hx, cid):
    c, x, y, z = block.shape
    nx, ny = lax.axis_size("gx"), lax.axis_size("gy")
    shape = (c, x + 2 * hx, y + 2 * TILE, z)
    return pl.pallas_call(
        functools.partial(halo_kernel, hx, nx, ny),
        out_shape=jax.ShapeDtypeStruct(shape, block.dtype),
        in_specs=[pl.BlockSpec(memory_space=pltpu.VMEM)],
        out_specs=pl.BlockSpec(memory_space=pltpu.VMEM),
        scratch_shapes=[
            pltpu.VMEM(shape, block.dtype),
            pltpu.SemaphoreType.DMA((len(DIRS),)),
            pltpu.SemaphoreType.DMA((len(DIRS),)),
        ],
        compiler_params=pltpu.CompilerParams(collective_id=cid, has_side_effects=True),
    )(block)


def _rolls(v):
    lane = lax.broadcasted_iota(jnp.int32, v.shape, 1)
    last = v.shape[1] - 1
    return (pltpu.roll(v, v.shape[0] - 1, 0), pltpu.roll(v, 1, 0),
            jnp.where(lane == last, 0.0, pltpu.roll(v, last, 1)), jnp.where(lane == 0, 0.0, pltpu.roll(v, 1, 1)))


def mech_kernel(zoff, s_ref, ub_ref, disp_out, energy_out, u1, u2, fc):
    _, nxe, nz, _ = ub_ref.shape
    bx, bz = disp_out.shape[1], disp_out.shape[2]
    m = (nxe - bx) // 2
    lo = (nz - bz) // 2

    def align(i, carry):
        fc[7, i] = s_ref[i, pl.ds(zoff, nz), :]
        return carry

    lax.fori_loop(0, nxe, align, 0, unroll=4)

    def faces_row(i, carry):
        c = fc[7, i]
        zp, zm, yp, ym = _rolls(c)
        diag = None
        for f, o in enumerate((fc[7, i + 1], fc[7, i - 1], zp, zm, yp, ym)):
            face = 0.5 * (c + o)
            fc[f, i] = face
            diag = face if diag is None else diag + face
        fc[6, i] = diag + spring_term * c
        return carry

    lax.fori_loop(1, nxe - 1, faces_row, 0, unroll=4)

    def sweep(src, dst, weight, i):
        c, diag = fc[7, i], fc[6, i]
        for k in range(3):
            u = src[k, i]
            others = (src[k, i + 1], src[k, i - 1]) + _rolls(u)
            result = diag * u
            for f, other in enumerate(others):
                result = result - fc[f, i] * other
            new = u + weight * (ub_ref[3 + k, i] - result) / diag
            dst[k, i] = jnp.where(c > 0, new, 0.0)

    def first(i, carry):
        sweep(ub_ref, u1, first_weight, i)
        return carry

    def second(i, carry):
        sweep(u1, u2, second_weight, i)
        return carry

    lax.fori_loop(1, nxe - 1, first, 0, unroll=4)
    lax.fori_loop(2, nxe - 2, second, 0, unroll=4)

    def energy_row(i, carry):
        parts = []
        for k in range(3):
            u = u2[k, i]
            others = (u2[k, i + 1], u2[k, i - 1]) + _rolls(u)
            total = jnp.zeros(u.shape, jnp.float32)
            for f, other in enumerate(others):
                diff = u - other
                total = total + fc[f, i] * diff * diff
            parts.append(total)
        u1[0, i] = 0.25 * (parts[0] + parts[1] + parts[2])
        return carry

    lax.fori_loop(m, m + bx, energy_row, 0, unroll=4)
    energy_out[...] = u1[0, pl.ds(m, bx), pl.ds(lo, bz), :]
    disp_out[...] = u2[:, pl.ds(m, bx), pl.ds(lo, bz), :]


def mechanics(stiff_ext, ub, zoff, bx, bz):
    _, nxe, nz, ny = ub.shape
    return pl.pallas_call(
        functools.partial(mech_kernel, zoff),
        out_shape=(jax.ShapeDtypeStruct((3, bx, bz, ny), jnp.float32),
                   jax.ShapeDtypeStruct((bx, bz, ny), jnp.float32)),
        in_specs=[pl.BlockSpec(memory_space=pltpu.VMEM)] * 2,
        out_specs=(pl.BlockSpec(memory_space=pltpu.VMEM), pl.BlockSpec(memory_space=pltpu.VMEM)),
        scratch_shapes=[pltpu.VMEM((3, nxe, nz, ny), jnp.float32), pltpu.VMEM((3, nxe, nz, ny), jnp.float32),
                        pltpu.VMEM((8, nxe, nz, ny), jnp.float32)],
    )(stiff_ext, ub)


def padded_2(block, sides, width):
    for axis, dim in sides:
        count = lax.axis_size(axis)
        forward = [(i, i + 1) for i in range(count - 1)]
        backward = [(target, source) for source, target in forward]
        low = lax.ppermute(
            lax.slice_in_dim(block, block.shape[dim] - width, None, axis=dim), axis, forward
        )
        high = lax.ppermute(lax.slice_in_dim(block, 0, width, axis=dim), axis, backward)
        block = jnp.concatenate([low, block, high], axis=dim)
    return block


def fine_laplace(padded):
    zpad = jnp.pad(padded, ((0, 0), (0, 0), (1, 1)))
    center = zpad[1:-1, 1:-1, 1:-1]
    total = zpad[2:, 1:-1, 1:-1] + zpad[:-2, 1:-1, 1:-1]
    total = total + zpad[1:-1, 2:, 1:-1] + zpad[1:-1, :-2, 1:-1]
    total = total + zpad[1:-1, 1:-1, 2:] + zpad[1:-1, 1:-1, :-2]
    return total - 6.0 * center


def advance(conc_pad, order_pad, mob_pad, last):
    chem = conc_pad - order_pad * order_pad * (3.0 - 2.0 * order_pad)
    conc_in = conc_pad[1:-1, 1:-1]
    order_in = order_pad[1:-1, 1:-1]
    chem_in = chem[1:-1, 1:-1]
    mobility = mob_pad[1:-1, 1:-1]
    conc_new = conc_in + rate_conc * fine_laplace(chem)
    dh_term = 6.0 * order_in * (1.0 - order_in)
    dg_term = 2.0 * order_in * (1.0 - order_in) * (1.0 - 2.0 * order_in)
    order_new = order_in + mobility * (
        rate_order * fine_laplace(order_pad)
        - well_height * dg_term
        + drive_coupling * chem_in * dh_term
    )
    if not last:
        conc_new = jnp.where(mobility > 0, conc_new, 0.0)
    return conc_new, order_new, mobility


def mobility_of(labels):
    return (0.5 * (labels == 0) + 1.0 * (labels == 1) + 0.25 * (labels == 2)).astype(jnp.float32)


def restrict_xzy(order_out):
    sx, sy, sz = order_out.shape
    sq = order_out * order_out
    sq = sq.reshape(sx // 2, 2, sy, sz).sum(axis=1)
    sq = sq.reshape(sx // 2, sy // 2, 2, sz).sum(axis=2)
    pairs = jnp.asarray(np.repeat(np.eye(sz // 2, dtype=np.float32), 2, axis=0))
    summed = jnp.einsum("xyz,zw->xwy", sq, pairs, precision=lax.Precision.HIGHEST)
    return 0.1 + 0.125 * summed


def y_shift(v, step):
    if step > 0:
        return jnp.pad(v[..., step:], [(0, 0)] * (v.ndim - 1) + [(0, step)])
    return jnp.pad(v[..., :step], [(0, 0)] * (v.ndim - 1) + [(-step, 0)])


def face_terms(stiff_pad):
    center = stiff_pad[1:-1, 1:-1]
    others = [stiff_pad[2:, 1:-1], stiff_pad[:-2, 1:-1], stiff_pad[1:-1, 2:], stiff_pad[1:-1, :-2],
              y_shift(center, 1), y_shift(center, -1)]
    faces = [0.5 * (center + other) for other in others]
    diag = faces[0] + faces[1] + faces[2] + faces[3] + faces[4] + faces[5] + spring_term * center
    return faces, diag, center


def neighbours(u_pad):
    center = u_pad[:, 1:-1, 1:-1]
    return center, [u_pad[:, 2:, 1:-1], u_pad[:, :-2, 1:-1], u_pad[:, 1:-1, 2:], u_pad[:, 1:-1, :-2],
                    y_shift(center, 1), y_shift(center, -1)]


def apply_op(u_pad, faces, diag):
    center, others = neighbours(u_pad)
    result = diag * center
    for face, other in zip(faces, others):
        result = result - face * other
    return result, center


def strain_energy(u_pad, faces):
    center, others = neighbours(u_pad)
    total = jnp.zeros(center.shape, jnp.float32)
    for face, other in zip(faces, others):
        diff = center - other
        total = total + face * diff * diff
    return 0.25 * jnp.sum(total, axis=0)


def on_device(concentration, order_field, phase_labels, displacement, body_load):
    h = FINE_HALO
    fields = jnp.stack([concentration, order_field, mobility_of(phase_labels)])
    m = MECH_HALO
    fields = padded_2(fields, (("gx", 1),), h)
    fields, ub = lax.optimization_barrier((fields, jnp.concatenate([displacement, body_load])))
    ub = padded_2(ub, (("gx", 1),), m)
    fields = padded_2(fields, (("gy", 2),), h)
    conc, order, mob = fields[0], fields[1], fields[2]
    for step in range(STEPS):
        conc, order, mob = advance(conc, order, mob, step == STEPS - 1)

    coarse = restrict_xzy(order)
    coarse, ub = lax.optimization_barrier((coarse, ub))
    ub = padded_2(ub, (("gy", 2),), m + 1)
    stiff = lax.all_to_all(coarse, "gy", split_axis=1, concat_axis=2, tiled=True)
    stiff_ext = halo_exchange(stiff[None], m, 0)[0]
    bx, bz = stiff.shape[0], stiff.shape[1]
    disp, energy = mechanics(stiff_ext, ub, TILE - (m + 1), bx, bz)
    tiles = lax.all_to_all(energy, "gy", split_axis=2, concat_axis=1, tiled=True)
    return (conc, order, disp, jnp.transpose(tiles, (0, 2, 1)))


def solution(mesh):
    return jax.shard_map(
        on_device,
        mesh=mesh,
        in_specs=(
            P("gx", "gy", None),
            P("gx", "gy", None),
            P("gx", "gy", None),
            P(None, "gx", "gy", None),
            P(None, "gx", "gy", None),
        ),
        out_specs=(
            P("gx", "gy", None),
            P("gx", "gy", None),
            P(None, "gx", "gy", None),
            P("gx", "gy", None),
        ),
        check_vma=False,
    )
```

```python
import jax
import jax.numpy as jnp
import functools

import numpy as np
from jax import lax
from jax.experimental import pallas as pl
from jax.experimental.pallas import tpu as pltpu
from jax.sharding import PartitionSpec as P

STEPS = 4
FINE_HALO = 4
MECH_HALO = 3

rate_conc = 0.15
rate_order = 0.15
well_height = 1.0
drive_coupling = 0.5
spring_term = 0.2
first_weight = 0.5956
second_weight = 2.695


MESH = pl.DeviceIdType.MESH
TILE = 8
DIRS = [(sx, sy) for sx in (-1, 0, 1) for sy in (-1, 0, 1) if (sx, sy) != (0, 0)]


def _src_window(side, size, width):
    return {1: slice(size - width, size), -1: slice(0, width), 0: slice(0, size)}[side]


def _dst_window(side, size, width):
    return {1: slice(0, width), -1: slice(width + size, size + 2 * width), 0: slice(width, width + size)}[side]


def halo_kernel(hx, nx, ny, blk_ref, out_ref, ext, send_sem, recv_sem):
    c, x, y, z = blk_ref.shape
    t = TILE
    gx = lax.axis_index("gx")
    gy = lax.axis_index("gy")

    def exists(sx, sy):
        return (gx + sx >= 0) & (gx + sx < nx) & (gy + sy >= 0) & (gy + sy < ny)

    barrier = pltpu.get_barrier_semaphore()
    for sx, sy in DIRS:
        @pl.when(exists(sx, sy))
        def _():
            pl.semaphore_signal(barrier, inc=1, device_id=(gx + sx, gy + sy), device_id_type=MESH)
    row = (gx + nx - 1) // nx + 1 + (2 * nx - 2 - gx) // nx
    col = (gy + ny - 1) // ny + 1 + (2 * ny - 2 - gy) // ny
    pl.semaphore_wait(barrier, row * col - 1)

    copies = []
    for k, (sx, sy) in enumerate(DIRS):
        copy = pltpu.make_async_remote_copy(
            src_ref=blk_ref.at[:, _src_window(sx, x, hx), _src_window(sy, y, t), :],
            dst_ref=ext.at[:, _dst_window(sx, x, hx), _dst_window(sy, y, t), :],
            send_sem=send_sem.at[k],
            recv_sem=recv_sem.at[k],
            device_id=(lax.rem(gx + sx + nx, nx), lax.rem(gy + sy + ny, ny)),
            device_id_type=MESH,
        )
        copies.append(copy)

        @pl.when(exists(sx, sy))
        def _():
            copy.start()

    ext[:, hx:hx + x, t:t + y, :] = blk_ref[...]
    for sx, sy in DIRS:
        xs, ys = _dst_window(sx, x, hx), _dst_window(sy, y, t)

        @pl.when(jnp.logical_not(exists(-sx, -sy)))
        def _():
            ext[:, xs, ys, :] = jnp.zeros((c, xs.stop - xs.start, ys.stop - ys.start, z), ext.dtype)

    for (sx, sy), copy in zip(DIRS, copies):
        @pl.when(exists(sx, sy))
        def _():
            copy.wait_send()

        @pl.when(exists(-sx, -sy))
        def _():
            copy.wait_recv()
    out_ref[...] = ext[...]


def halo_exchange(block, hx, cid):
    c, x, y, z = block.shape
    nx, ny = lax.axis_size("gx"), lax.axis_size("gy")
    shape = (c, x + 2 * hx, y + 2 * TILE, z)
    return pl.pallas_call(
        functools.partial(halo_kernel, hx, nx, ny),
        out_shape=jax.ShapeDtypeStruct(shape, block.dtype),
        in_specs=[pl.BlockSpec(memory_space=pltpu.VMEM)],
        out_specs=pl.BlockSpec(memory_space=pltpu.VMEM),
        scratch_shapes=[
            pltpu.VMEM(shape, block.dtype),
            pltpu.SemaphoreType.DMA((len(DIRS),)),
            pltpu.SemaphoreType.DMA((len(DIRS),)),
        ],
        compiler_params=pltpu.CompilerParams(collective_id=cid, has_side_effects=True),
    )(block)


def _rolls(v):
    lane = lax.broadcasted_iota(jnp.int32, v.shape, 1)
    last = v.shape[1] - 1
    return (pltpu.roll(v, v.shape[0] - 1, 0), pltpu.roll(v, 1, 0),
            jnp.where(lane == last, 0.0, pltpu.roll(v, last, 1)), jnp.where(lane == 0, 0.0, pltpu.roll(v, 1, 1)))


def mech_kernel(zoff, s_ref, ub_ref, disp_out, energy_out, u1, u2, fc):
    _, nxe, nz, _ = ub_ref.shape
    bx, bz = disp_out.shape[1], disp_out.shape[2]
    m = (nxe - bx) // 2
    lo = (nz - bz) // 2

    def align(i, carry):
        fc[7, i] = s_ref[i, pl.ds(zoff, nz), :]
        return carry

    lax.fori_loop(0, nxe, align, 0, unroll=True)

    def faces_row(i, carry):
        c = fc[7, i]
        zp, zm, yp, ym = _rolls(c)
        diag = None
        for f, o in enumerate((fc[7, i + 1], fc[7, i - 1], zp, zm, yp, ym)):
            face = 0.5 * (c + o)
            fc[f, i] = face
            diag = face if diag is None else diag + face
        fc[6, i] = diag + spring_term * c
        return carry

    lax.fori_loop(1, nxe - 1, faces_row, 0, unroll=True)

    def sweep(src, dst, weight, i):
        c, diag = fc[7, i], fc[6, i]
        for k in range(3):
            u = src[k, i]
            others = (src[k, i + 1], src[k, i - 1]) + _rolls(u)
            result = diag * u
            for f, other in enumerate(others):
                result = result - fc[f, i] * other
            new = u + weight * (ub_ref[3 + k, i] - result) / diag
            dst[k, i] = jnp.where(c > 0, new, 0.0)

    def first(i, carry):
        sweep(ub_ref, u1, first_weight, i)
        return carry

    def second(i, carry):
        sweep(u1, u2, second_weight, i)
        return carry

    lax.fori_loop(1, nxe - 1, first, 0, unroll=True)
    lax.fori_loop(2, nxe - 2, second, 0, unroll=True)

    def energy_row(i, carry):
        parts = []
        for k in range(3):
            u = u2[k, i]
            others = (u2[k, i + 1], u2[k, i - 1]) + _rolls(u)
            total = jnp.zeros(u.shape, jnp.float32)
            for f, other in enumerate(others):
                diff = u - other
                total = total + fc[f, i] * diff * diff
            parts.append(total)
        u1[0, i] = 0.25 * (parts[0] + parts[1] + parts[2])
        return carry

    lax.fori_loop(m, m + bx, energy_row, 0, unroll=True)
    energy_out[...] = u1[0, pl.ds(m, bx), pl.ds(lo, bz), :]
    disp_out[...] = u2[:, pl.ds(m, bx), pl.ds(lo, bz), :]


def mechanics(stiff_ext, ub, zoff, bx, bz):
    _, nxe, nz, ny = ub.shape
    return pl.pallas_call(
        functools.partial(mech_kernel, zoff),
        out_shape=(jax.ShapeDtypeStruct((3, bx, bz, ny), jnp.float32),
                   jax.ShapeDtypeStruct((bx, bz, ny), jnp.float32)),
        in_specs=[pl.BlockSpec(memory_space=pltpu.VMEM)] * 2,
        out_specs=(pl.BlockSpec(memory_space=pltpu.VMEM), pl.BlockSpec(memory_space=pltpu.VMEM)),
        scratch_shapes=[pltpu.VMEM((3, nxe, nz, ny), jnp.float32), pltpu.VMEM((3, nxe, nz, ny), jnp.float32),
                        pltpu.VMEM((8, nxe, nz, ny), jnp.float32)],
    )(stiff_ext, ub)


def padded_2(block, sides, width):
    for axis, dim in sides:
        count = lax.axis_size(axis)
        forward = [(i, i + 1) for i in range(count - 1)]
        backward = [(target, source) for source, target in forward]
        low = lax.ppermute(
            lax.slice_in_dim(block, block.shape[dim] - width, None, axis=dim), axis, forward
        )
        high = lax.ppermute(lax.slice_in_dim(block, 0, width, axis=dim), axis, backward)
        block = jnp.concatenate([low, block, high], axis=dim)
    return block


def fine_laplace(padded):
    zpad = jnp.pad(padded, ((0, 0), (0, 0), (1, 1)))
    center = zpad[1:-1, 1:-1, 1:-1]
    total = zpad[2:, 1:-1, 1:-1] + zpad[:-2, 1:-1, 1:-1]
    total = total + zpad[1:-1, 2:, 1:-1] + zpad[1:-1, :-2, 1:-1]
    total = total + zpad[1:-1, 1:-1, 2:] + zpad[1:-1, 1:-1, :-2]
    return total - 6.0 * center


def advance(conc_pad, order_pad, mob_pad, last):
    chem = conc_pad - order_pad * order_pad * (3.0 - 2.0 * order_pad)
    conc_in = conc_pad[1:-1, 1:-1]
    order_in = order_pad[1:-1, 1:-1]
    chem_in = chem[1:-1, 1:-1]
    mobility = mob_pad[1:-1, 1:-1]
    conc_new = conc_in + rate_conc * fine_laplace(chem)
    dh_term = 6.0 * order_in * (1.0 - order_in)
    dg_term = 2.0 * order_in * (1.0 - order_in) * (1.0 - 2.0 * order_in)
    order_new = order_in + mobility * (
        rate_order * fine_laplace(order_pad)
        - well_height * dg_term
        + drive_coupling * chem_in * dh_term
    )
    if not last:
        conc_new = jnp.where(mobility > 0, conc_new, 0.0)
    return conc_new, order_new, mobility


def mobility_of(labels):
    return (0.5 * (labels == 0) + 1.0 * (labels == 1) + 0.25 * (labels == 2)).astype(jnp.float32)


def restrict_xzy(order_out):
    sx, sy, sz = order_out.shape
    sq = order_out * order_out
    sq = sq.reshape(sx // 2, 2, sy, sz).sum(axis=1)
    sq = sq.reshape(sx // 2, sy // 2, 2, sz).sum(axis=2)
    pairs = jnp.asarray(np.repeat(np.eye(sz // 2, dtype=np.float32), 2, axis=0))
    summed = jnp.einsum("xyz,zw->xwy", sq, pairs, precision=lax.Precision.HIGHEST)
    return 0.1 + 0.125 * summed


def y_shift(v, step):
    if step > 0:
        return jnp.pad(v[..., step:], [(0, 0)] * (v.ndim - 1) + [(0, step)])
    return jnp.pad(v[..., :step], [(0, 0)] * (v.ndim - 1) + [(-step, 0)])


def face_terms(stiff_pad):
    center = stiff_pad[1:-1, 1:-1]
    others = [stiff_pad[2:, 1:-1], stiff_pad[:-2, 1:-1], stiff_pad[1:-1, 2:], stiff_pad[1:-1, :-2],
              y_shift(center, 1), y_shift(center, -1)]
    faces = [0.5 * (center + other) for other in others]
    diag = faces[0] + faces[1] + faces[2] + faces[3] + faces[4] + faces[5] + spring_term * center
    return faces, diag, center


def neighbours(u_pad):
    center = u_pad[:, 1:-1, 1:-1]
    return center, [u_pad[:, 2:, 1:-1], u_pad[:, :-2, 1:-1], u_pad[:, 1:-1, 2:], u_pad[:, 1:-1, :-2],
                    y_shift(center, 1), y_shift(center, -1)]


def apply_op(u_pad, faces, diag):
    center, others = neighbours(u_pad)
    result = diag * center
    for face, other in zip(faces, others):
        result = result - face * other
    return result, center


def strain_energy(u_pad, faces):
    center, others = neighbours(u_pad)
    total = jnp.zeros(center.shape, jnp.float32)
    for face, other in zip(faces, others):
        diff = center - other
        total = total + face * diff * diff
    return 0.25 * jnp.sum(total, axis=0)


def on_device(concentration, order_field, phase_labels, displacement, body_load):
    h = FINE_HALO
    fields = jnp.stack([concentration, order_field, mobility_of(phase_labels)])
    m = MECH_HALO
    fields = padded_2(fields, (("gx", 1),), h)
    fields, ub = lax.optimization_barrier((fields, jnp.concatenate([displacement, body_load])))
    ub = padded_2(ub, (("gx", 1),), m)
    fields = padded_2(fields, (("gy", 2),), h)
    conc, order, mob = fields[0], fields[1], fields[2]
    for step in range(STEPS):
        conc, order, mob = advance(conc, order, mob, step == STEPS - 1)

    order, ub = lax.optimization_barrier((order, ub))
    ub = padded_2(ub, (("gy", 2),), m + 1)
    disp, load = ub[:3], ub[3:]

    coarse = restrict_xzy(order)
    stiff = lax.all_to_all(coarse, "gy", split_axis=1, concat_axis=2, tiled=True)
    stiff_ext = halo_exchange(stiff[None], m, 0)[0]
    bx, bz = stiff.shape[0], stiff.shape[1]
    disp, energy = mechanics(stiff_ext, ub, TILE - (m + 1), bx, bz)
    tiles = lax.all_to_all(energy, "gy", split_axis=2, concat_axis=1, tiled=True)
    return (conc, order, disp, jnp.transpose(tiles, (0, 2, 1)))


def solution(mesh):
    return jax.shard_map(
        on_device,
        mesh=mesh,
        in_specs=(
            P("gx", "gy", None),
            P("gx", "gy", None),
            P("gx", "gy", None),
            P(None, "gx", "gy", None),
            P(None, "gx", "gy", None),
        ),
        out_specs=(
            P("gx", "gy", None),
            P("gx", "gy", None),
            P(None, "gx", "gy", None),
            P("gx", "gy", None),
        ),
        check_vma=False,
    )
```

```python
import jax
import jax.numpy as jnp
import functools

import numpy as np
from jax import lax
from jax.experimental import pallas as pl
from jax.experimental.pallas import tpu as pltpu
from jax.sharding import PartitionSpec as P

STEPS = 4
FINE_HALO = 4
MECH_HALO = 3

rate_conc = 0.15
rate_order = 0.15
well_height = 1.0
drive_coupling = 0.5
spring_term = 0.2
first_weight = 0.5956
second_weight = 2.695


MESH = pl.DeviceIdType.MESH
TILE = 8
DIRS = [(sx, sy) for sx in (-1, 0, 1) for sy in (-1, 0, 1) if (sx, sy) != (0, 0)]


def _src_window(side, size, width):
    return {1: slice(size - width, size), -1: slice(0, width), 0: slice(0, size)}[side]


def _dst_window(side, size, width):
    return {1: slice(0, width), -1: slice(width + size, size + 2 * width), 0: slice(width, width + size)}[side]


def halo_kernel(hx, nx, ny, blk_ref, out_ref, ext, send_sem, recv_sem):
    c, x, y, z = blk_ref.shape
    t = TILE
    gx = lax.axis_index("gx")
    gy = lax.axis_index("gy")

    def exists(sx, sy):
        return (gx + sx >= 0) & (gx + sx < nx) & (gy + sy >= 0) & (gy + sy < ny)

    barrier = pltpu.get_barrier_semaphore()
    for sx, sy in DIRS:
        @pl.when(exists(sx, sy))
        def _():
            pl.semaphore_signal(barrier, inc=1, device_id=(gx + sx, gy + sy), device_id_type=MESH)
    row = (gx + nx - 1) // nx + 1 + (2 * nx - 2 - gx) // nx
    col = (gy + ny - 1) // ny + 1 + (2 * ny - 2 - gy) // ny
    pl.semaphore_wait(barrier, row * col - 1)

    copies = []
    for k, (sx, sy) in enumerate(DIRS):
        copy = pltpu.make_async_remote_copy(
            src_ref=blk_ref.at[:, _src_window(sx, x, hx), _src_window(sy, y, t), :],
            dst_ref=ext.at[:, _dst_window(sx, x, hx), _dst_window(sy, y, t), :],
            send_sem=send_sem.at[k],
            recv_sem=recv_sem.at[k],
            device_id=(lax.rem(gx + sx + nx, nx), lax.rem(gy + sy + ny, ny)),
            device_id_type=MESH,
        )
        copies.append(copy)

        @pl.when(exists(sx, sy))
        def _():
            copy.start()

    ext[:, hx:hx + x, t:t + y, :] = blk_ref[...]
    for sx, sy in DIRS:
        xs, ys = _dst_window(sx, x, hx), _dst_window(sy, y, t)

        @pl.when(jnp.logical_not(exists(-sx, -sy)))
        def _():
            ext[:, xs, ys, :] = jnp.zeros((c, xs.stop - xs.start, ys.stop - ys.start, z), ext.dtype)

    for (sx, sy), copy in zip(DIRS, copies):
        @pl.when(exists(sx, sy))
        def _():
            copy.wait_send()

        @pl.when(exists(-sx, -sy))
        def _():
            copy.wait_recv()
    out_ref[...] = ext[...]


def halo_exchange(block, hx, cid):
    c, x, y, z = block.shape
    nx, ny = lax.axis_size("gx"), lax.axis_size("gy")
    shape = (c, x + 2 * hx, y + 2 * TILE, z)
    return pl.pallas_call(
        functools.partial(halo_kernel, hx, nx, ny),
        out_shape=jax.ShapeDtypeStruct(shape, block.dtype),
        in_specs=[pl.BlockSpec(memory_space=pltpu.VMEM)],
        out_specs=pl.BlockSpec(memory_space=pltpu.VMEM),
        scratch_shapes=[
            pltpu.VMEM(shape, block.dtype),
            pltpu.SemaphoreType.DMA((len(DIRS),)),
            pltpu.SemaphoreType.DMA((len(DIRS),)),
        ],
        compiler_params=pltpu.CompilerParams(collective_id=cid, has_side_effects=True),
    )(block)


def _rolls(v):
    lane = lax.broadcasted_iota(jnp.int32, v.shape, 1)
    last = v.shape[1] - 1
    return (pltpu.roll(v, v.shape[0] - 1, 0), pltpu.roll(v, 1, 0),
            jnp.where(lane == last, 0.0, pltpu.roll(v, last, 1)), jnp.where(lane == 0, 0.0, pltpu.roll(v, 1, 1)))


def mech_kernel(zoff, s_ref, low_ref, mid_ref, high_ref, disp_out, energy_out, u1, u2, fc, ub_ref, z3):
    _, nxe, nz, _ = ub_ref.shape
    bx, bz = disp_out.shape[1], disp_out.shape[2]
    m = (nxe - bx) // 2
    lo = (nz - bz) // 2
    t = mid_ref.shape[2]

    def align(i, carry):
        fc[7, i] = s_ref[i, pl.ds(zoff, nz), :]
        for k in range(6):
            z3[k, i, pl.ds(0, t), :] = low_ref[k, i]
            z3[k, i, pl.ds(t, t), :] = mid_ref[k, i]
            z3[k, i, pl.ds(2 * t, t), :] = high_ref[k, i]
            ub_ref[k, i] = z3[k, i, pl.ds(zoff, nz), :]
        return carry

    lax.fori_loop(0, nxe, align, 0, unroll=True)

    def faces_row(i, carry):
        c = fc[7, i]
        zp, zm, yp, ym = _rolls(c)
        diag = None
        for f, o in enumerate((fc[7, i + 1], fc[7, i - 1], zp, zm, yp, ym)):
            face = 0.5 * (c + o)
            fc[f, i] = face
            diag = face if diag is None else diag + face
        fc[6, i] = diag + spring_term * c
        return carry

    lax.fori_loop(1, nxe - 1, faces_row, 0, unroll=True)

    def sweep(src, dst, weight, i):
        c, diag = fc[7, i], fc[6, i]
        for k in range(3):
            u = src[k, i]
            others = (src[k, i + 1], src[k, i - 1]) + _rolls(u)
            result = diag * u
            for f, other in enumerate(others):
                result = result - fc[f, i] * other
            new = u + weight * (ub_ref[3 + k, i] - result) / diag
            dst[k, i] = jnp.where(c > 0, new, 0.0)

    def first(i, carry):
        sweep(ub_ref, u1, first_weight, i)
        return carry

    def second(i, carry):
        sweep(u1, u2, second_weight, i)
        return carry

    lax.fori_loop(1, nxe - 1, first, 0, unroll=True)
    lax.fori_loop(2, nxe - 2, second, 0, unroll=True)

    def energy_row(i, carry):
        parts = []
        for k in range(3):
            u = u2[k, i]
            others = (u2[k, i + 1], u2[k, i - 1]) + _rolls(u)
            total = jnp.zeros(u.shape, jnp.float32)
            for f, other in enumerate(others):
                diff = u - other
                total = total + fc[f, i] * diff * diff
            parts.append(total)
        u1[0, i] = 0.25 * (parts[0] + parts[1] + parts[2])
        return carry

    lax.fori_loop(m, m + bx, energy_row, 0, unroll=True)
    energy_out[...] = u1[0, pl.ds(m, bx), pl.ds(lo, bz), :]
    disp_out[...] = u2[:, pl.ds(m, bx), pl.ds(lo, bz), :]


def mechanics(stiff_ext, low, mid, high, zoff, nz, bx, bz):
    _, nxe, t, ny = mid.shape
    return pl.pallas_call(
        functools.partial(mech_kernel, zoff),
        out_shape=(jax.ShapeDtypeStruct((3, bx, bz, ny), jnp.float32),
                   jax.ShapeDtypeStruct((bx, bz, ny), jnp.float32)),
        in_specs=[pl.BlockSpec(memory_space=pltpu.VMEM)] * 4,
        out_specs=(pl.BlockSpec(memory_space=pltpu.VMEM), pl.BlockSpec(memory_space=pltpu.VMEM)),
        scratch_shapes=[pltpu.VMEM((3, nxe, nz, ny), jnp.float32), pltpu.VMEM((3, nxe, nz, ny), jnp.float32),
                        pltpu.VMEM((8, nxe, nz, ny), jnp.float32), pltpu.VMEM((6, nxe, nz, ny), jnp.float32),
                        pltpu.VMEM((6, nxe, 3 * t, ny), jnp.float32)],
    )(stiff_ext, low, mid, high)


def padded_2(block, sides, width):
    for axis, dim in sides:
        count = lax.axis_size(axis)
        forward = [(i, i + 1) for i in range(count - 1)]
        backward = [(target, source) for source, target in forward]
        low = lax.ppermute(
            lax.slice_in_dim(block, block.shape[dim] - width, None, axis=dim), axis, forward
        )
        high = lax.ppermute(lax.slice_in_dim(block, 0, width, axis=dim), axis, backward)
        block = jnp.concatenate([low, block, high], axis=dim)
    return block


def fine_laplace(padded):
    zpad = jnp.pad(padded, ((0, 0), (0, 0), (1, 1)))
    center = zpad[1:-1, 1:-1, 1:-1]
    total = zpad[2:, 1:-1, 1:-1] + zpad[:-2, 1:-1, 1:-1]
    total = total + zpad[1:-1, 2:, 1:-1] + zpad[1:-1, :-2, 1:-1]
    total = total + zpad[1:-1, 1:-1, 2:] + zpad[1:-1, 1:-1, :-2]
    return total - 6.0 * center


def advance(conc_pad, order_pad, mob_pad, last):
    chem = conc_pad - order_pad * order_pad * (3.0 - 2.0 * order_pad)
    conc_in = conc_pad[1:-1, 1:-1]
    order_in = order_pad[1:-1, 1:-1]
    chem_in = chem[1:-1, 1:-1]
    mobility = mob_pad[1:-1, 1:-1]
    conc_new = conc_in + rate_conc * fine_laplace(chem)
    dh_term = 6.0 * order_in * (1.0 - order_in)
    dg_term = 2.0 * order_in * (1.0 - order_in) * (1.0 - 2.0 * order_in)
    order_new = order_in + mobility * (
        rate_order * fine_laplace(order_pad)
        - well_height * dg_term
        + drive_coupling * chem_in * dh_term
    )
    if not last:
        conc_new = jnp.where(mobility > 0, conc_new, 0.0)
    return conc_new, order_new, mobility


def mobility_of(labels):
    return (0.5 * (labels == 0) + 1.0 * (labels == 1) + 0.25 * (labels == 2)).astype(jnp.float32)


def restrict_xzy(order_out):
    sx, sy, sz = order_out.shape
    sq = order_out * order_out
    sq = sq.reshape(sx // 2, 2, sy, sz).sum(axis=1)
    sq = sq.reshape(sx // 2, sy // 2, 2, sz).sum(axis=2)
    pairs = jnp.asarray(np.repeat(np.eye(sz // 2, dtype=np.float32), 2, axis=0))
    summed = jnp.einsum("xyz,zw->xwy", sq, pairs, precision=lax.Precision.HIGHEST)
    return 0.1 + 0.125 * summed


def y_shift(v, step):
    if step > 0:
        return jnp.pad(v[..., step:], [(0, 0)] * (v.ndim - 1) + [(0, step)])
    return jnp.pad(v[..., :step], [(0, 0)] * (v.ndim - 1) + [(-step, 0)])


def face_terms(stiff_pad):
    center = stiff_pad[1:-1, 1:-1]
    others = [stiff_pad[2:, 1:-1], stiff_pad[:-2, 1:-1], stiff_pad[1:-1, 2:], stiff_pad[1:-1, :-2],
              y_shift(center, 1), y_shift(center, -1)]
    faces = [0.5 * (center + other) for other in others]
    diag = faces[0] + faces[1] + faces[2] + faces[3] + faces[4] + faces[5] + spring_term * center
    return faces, diag, center


def neighbours(u_pad):
    center = u_pad[:, 1:-1, 1:-1]
    return center, [u_pad[:, 2:, 1:-1], u_pad[:, :-2, 1:-1], u_pad[:, 1:-1, 2:], u_pad[:, 1:-1, :-2],
                    y_shift(center, 1), y_shift(center, -1)]


def apply_op(u_pad, faces, diag):
    center, others = neighbours(u_pad)
    result = diag * center
    for face, other in zip(faces, others):
        result = result - face * other
    return result, center


def strain_energy(u_pad, faces):
    center, others = neighbours(u_pad)
    total = jnp.zeros(center.shape, jnp.float32)
    for face, other in zip(faces, others):
        diff = center - other
        total = total + face * diff * diff
    return 0.25 * jnp.sum(total, axis=0)


def on_device(concentration, order_field, phase_labels, displacement, body_load):
    h = FINE_HALO
    fields = jnp.stack([concentration, order_field, mobility_of(phase_labels)])
    m = MECH_HALO
    fields = padded_2(fields, (("gx", 1),), h)
    fields, ub = lax.optimization_barrier((fields, jnp.concatenate([displacement, body_load])))
    ub = padded_2(ub, (("gx", 1),), m)
    fields = padded_2(fields, (("gy", 2),), h)
    conc, order, mob = fields[0], fields[1], fields[2]
    for step in range(STEPS):
        conc, order, mob = advance(conc, order, mob, step == STEPS - 1)

    order, ub = lax.optimization_barrier((order, ub))
    count = lax.axis_size("gy")
    forward = [(i, i + 1) for i in range(count - 1)]
    ub_low = lax.ppermute(ub, "gy", forward)
    ub_high = lax.ppermute(ub, "gy", [(b, a) for a, b in forward])

    coarse = restrict_xzy(order)
    stiff = lax.all_to_all(coarse, "gy", split_axis=1, concat_axis=2, tiled=True)
    stiff_ext = halo_exchange(stiff[None], m, 0)[0]
    bx, bz = stiff.shape[0], stiff.shape[1]
    disp, energy = mechanics(stiff_ext, ub_low, ub, ub_high, TILE - (m + 1), bz + 2 * (m + 1), bx, bz)
    tiles = lax.all_to_all(energy, "gy", split_axis=2, concat_axis=1, tiled=True)
    return (conc, order, disp, jnp.transpose(tiles, (0, 2, 1)))


def solution(mesh):
    return jax.shard_map(
        on_device,
        mesh=mesh,
        in_specs=(
            P("gx", "gy", None),
            P("gx", "gy", None),
            P("gx", "gy", None),
            P(None, "gx", "gy", None),
            P(None, "gx", "gy", None),
        ),
        out_specs=(
            P("gx", "gy", None),
            P("gx", "gy", None),
            P(None, "gx", "gy", None),
            P("gx", "gy", None),
        ),
        check_vma=False,
    )
```

```python
import jax
import jax.numpy as jnp
import functools

import numpy as np
from jax import lax
from jax.experimental import pallas as pl
from jax.experimental.pallas import tpu as pltpu
from jax.sharding import PartitionSpec as P

STEPS = 4
FINE_HALO = 4
MECH_HALO = 3

rate_conc = 0.15
rate_order = 0.15
well_height = 1.0
drive_coupling = 0.5
spring_term = 0.2
first_weight = 0.5956
second_weight = 2.695


MESH = pl.DeviceIdType.MESH
TILE = 8
DIRS = [(sx, sy) for sx in (-1, 0, 1) for sy in (-1, 0, 1) if (sx, sy) != (0, 0)]


def _src_window(side, size, width):
    return {1: slice(size - width, size), -1: slice(0, width), 0: slice(0, size)}[side]


def _dst_window(side, size, width):
    return {1: slice(0, width), -1: slice(width + size, size + 2 * width), 0: slice(width, width + size)}[side]


def halo_kernel(hx, nx, ny, blk_ref, out_ref, ext, send_sem, recv_sem):
    c, x, y, z = blk_ref.shape
    t = TILE
    gx = lax.axis_index("gx")
    gy = lax.axis_index("gy")

    def exists(sx, sy):
        return (gx + sx >= 0) & (gx + sx < nx) & (gy + sy >= 0) & (gy + sy < ny)

    barrier = pltpu.get_barrier_semaphore()
    for sx, sy in DIRS:
        @pl.when(exists(sx, sy))
        def _():
            pl.semaphore_signal(barrier, inc=1, device_id=(gx + sx, gy + sy), device_id_type=MESH)
    row = (gx + nx - 1) // nx + 1 + (2 * nx - 2 - gx) // nx
    col = (gy + ny - 1) // ny + 1 + (2 * ny - 2 - gy) // ny
    pl.semaphore_wait(barrier, row * col - 1)

    copies = []
    for k, (sx, sy) in enumerate(DIRS):
        copy = pltpu.make_async_remote_copy(
            src_ref=blk_ref.at[:, _src_window(sx, x, hx), _src_window(sy, y, t), :],
            dst_ref=ext.at[:, _dst_window(sx, x, hx), _dst_window(sy, y, t), :],
            send_sem=send_sem.at[k],
            recv_sem=recv_sem.at[k],
            device_id=(lax.rem(gx + sx + nx, nx), lax.rem(gy + sy + ny, ny)),
            device_id_type=MESH,
        )
        copies.append(copy)

        @pl.when(exists(sx, sy))
        def _():
            copy.start()

    ext[:, hx:hx + x, t:t + y, :] = blk_ref[...]
    for sx, sy in DIRS:
        xs, ys = _dst_window(sx, x, hx), _dst_window(sy, y, t)

        @pl.when(jnp.logical_not(exists(-sx, -sy)))
        def _():
            ext[:, xs, ys, :] = jnp.zeros((c, xs.stop - xs.start, ys.stop - ys.start, z), ext.dtype)

    for (sx, sy), copy in zip(DIRS, copies):
        @pl.when(exists(sx, sy))
        def _():
            copy.wait_send()

        @pl.when(exists(-sx, -sy))
        def _():
            copy.wait_recv()
    out_ref[...] = ext[...]


def halo_exchange(block, hx, cid):
    c, x, y, z = block.shape
    nx, ny = lax.axis_size("gx"), lax.axis_size("gy")
    shape = (c, x + 2 * hx, y + 2 * TILE, z)
    return pl.pallas_call(
        functools.partial(halo_kernel, hx, nx, ny),
        out_shape=jax.ShapeDtypeStruct(shape, block.dtype),
        in_specs=[pl.BlockSpec(memory_space=pltpu.VMEM)],
        out_specs=pl.BlockSpec(memory_space=pltpu.VMEM),
        scratch_shapes=[
            pltpu.VMEM(shape, block.dtype),
            pltpu.SemaphoreType.DMA((len(DIRS),)),
            pltpu.SemaphoreType.DMA((len(DIRS),)),
        ],
        compiler_params=pltpu.CompilerParams(collective_id=cid, has_side_effects=True),
    )(block)


def _rolls(v):
    lane = lax.broadcasted_iota(jnp.int32, v.shape, 1)
    last = v.shape[1] - 1
    return (pltpu.roll(v, v.shape[0] - 1, 0), pltpu.roll(v, 1, 0),
            jnp.where(lane == last, 0.0, pltpu.roll(v, last, 1)), jnp.where(lane == 0, 0.0, pltpu.roll(v, 1, 1)))


def mech_kernel(zoff, s_ref, ub_ref, disp_out, energy_out, u1, u2, fc):
    _, nxe, nz, _ = ub_ref.shape
    bx, bz = disp_out.shape[1], disp_out.shape[2]
    m = (nxe - bx) // 2
    lo = (nz - bz) // 2

    def align(i, carry):
        fc[7, i] = s_ref[i, pl.ds(zoff, nz), :]
        return carry

    lax.fori_loop(0, nxe, align, 0, unroll=True)

    def faces_row(i, carry):
        c = fc[7, i]
        zp, zm, yp, ym = _rolls(c)
        diag = None
        for f, o in enumerate((fc[7, i + 1], fc[7, i - 1], zp, zm, yp, ym)):
            face = 0.5 * (c + o)
            fc[f, i] = face
            diag = face if diag is None else diag + face
        fc[6, i] = diag + spring_term * c
        return carry

    lax.fori_loop(1, nxe - 1, faces_row, 0, unroll=True)

    def sweep(src, dst, weight, i):
        c, diag = fc[7, i], fc[6, i]
        for k in range(3):
            u = src[k, i]
            others = (src[k, i + 1], src[k, i - 1]) + _rolls(u)
            result = diag * u
            for f, other in enumerate(others):
                result = result - fc[f, i] * other
            new = u + weight * (ub_ref[3 + k, i] - result) / diag
            dst[k, i] = jnp.where(c > 0, new, 0.0)

    def first(i, carry):
        sweep(ub_ref, u1, first_weight, i)
        return carry

    def second(i, carry):
        sweep(u1, u2, second_weight, i)
        return carry

    lax.fori_loop(1, nxe - 1, first, 0, unroll=True)
    lax.fori_loop(2, nxe - 2, second, 0, unroll=True)

    def energy_row(i, carry):
        parts = []
        for k in range(3):
            u = u2[k, i]
            others = (u2[k, i + 1], u2[k, i - 1]) + _rolls(u)
            total = jnp.zeros(u.shape, jnp.float32)
            for f, other in enumerate(others):
                diff = u - other
                total = total + fc[f, i] * diff * diff
            parts.append(total)
        u1[0, i] = 0.25 * (parts[0] + parts[1] + parts[2])
        return carry

    lax.fori_loop(m, m + bx, energy_row, 0, unroll=True)
    energy_out[...] = u1[0, pl.ds(m, bx), pl.ds(lo, bz), :]
    disp_out[...] = u2[:, pl.ds(m, bx), pl.ds(lo, bz), :]


def mechanics(stiff_ext, ub, zoff, bx, bz):
    _, nxe, nz, ny = ub.shape
    return pl.pallas_call(
        functools.partial(mech_kernel, zoff),
        out_shape=(jax.ShapeDtypeStruct((3, bx, bz, ny), jnp.float32),
                   jax.ShapeDtypeStruct((bx, bz, ny), jnp.float32)),
        in_specs=[pl.BlockSpec(memory_space=pltpu.VMEM)] * 2,
        out_specs=(pl.BlockSpec(memory_space=pltpu.VMEM), pl.BlockSpec(memory_space=pltpu.VMEM)),
        scratch_shapes=[pltpu.VMEM((3, nxe, nz, ny), jnp.float32), pltpu.VMEM((3, nxe, nz, ny), jnp.float32),
                        pltpu.VMEM((8, nxe, nz, ny), jnp.float32)],
    )(stiff_ext, ub)


def padded_2(block, sides, width):
    for axis, dim in sides:
        count = lax.axis_size(axis)
        forward = [(i, i + 1) for i in range(count - 1)]
        backward = [(target, source) for source, target in forward]
        low = lax.ppermute(
            lax.slice_in_dim(block, block.shape[dim] - width, None, axis=dim), axis, forward
        )
        high = lax.ppermute(lax.slice_in_dim(block, 0, width, axis=dim), axis, backward)
        block = jnp.concatenate([low, block, high], axis=dim)
    return block


def fine_laplace(padded):
    zpad = jnp.pad(padded, ((0, 0), (0, 0), (1, 1)))
    center = zpad[1:-1, 1:-1, 1:-1]
    total = zpad[2:, 1:-1, 1:-1] + zpad[:-2, 1:-1, 1:-1]
    total = total + zpad[1:-1, 2:, 1:-1] + zpad[1:-1, :-2, 1:-1]
    total = total + zpad[1:-1, 1:-1, 2:] + zpad[1:-1, 1:-1, :-2]
    return total - 6.0 * center


def advance(conc_pad, order_pad, mob_pad, last):
    chem = conc_pad - order_pad * order_pad * (3.0 - 2.0 * order_pad)
    conc_in = conc_pad[1:-1, 1:-1]
    order_in = order_pad[1:-1, 1:-1]
    chem_in = chem[1:-1, 1:-1]
    mobility = mob_pad[1:-1, 1:-1]
    conc_new = conc_in + rate_conc * fine_laplace(chem)
    dh_term = 6.0 * order_in * (1.0 - order_in)
    dg_term = 2.0 * order_in * (1.0 - order_in) * (1.0 - 2.0 * order_in)
    order_new = order_in + mobility * (
        rate_order * fine_laplace(order_pad)
        - well_height * dg_term
        + drive_coupling * chem_in * dh_term
    )
    if not last:
        conc_new = jnp.where(mobility > 0, conc_new, 0.0)
    return conc_new, order_new, mobility


def mobility_of(labels):
    return (0.5 * (labels == 0) + 1.0 * (labels == 1) + 0.25 * (labels == 2)).astype(jnp.float32)


def restrict_xzy(order_out):
    sx, sy, sz = order_out.shape
    sq = order_out * order_out
    sq = sq.reshape(sx // 2, 2, sy, sz).sum(axis=1)
    sq = sq.reshape(sx // 2, sy // 2, 2, sz).sum(axis=2)
    pairs = jnp.asarray(np.repeat(np.eye(sz // 2, dtype=np.float32), 2, axis=0))
    summed = jnp.einsum("xyz,zw->xwy", sq, pairs, precision=lax.Precision.HIGHEST)
    return 0.1 + 0.125 * summed


def y_shift(v, step):
    if step > 0:
        return jnp.pad(v[..., step:], [(0, 0)] * (v.ndim - 1) + [(0, step)])
    return jnp.pad(v[..., :step], [(0, 0)] * (v.ndim - 1) + [(-step, 0)])


def face_terms(stiff_pad):
    center = stiff_pad[1:-1, 1:-1]
    others = [stiff_pad[2:, 1:-1], stiff_pad[:-2, 1:-1], stiff_pad[1:-1, 2:], stiff_pad[1:-1, :-2],
              y_shift(center, 1), y_shift(center, -1)]
    faces = [0.5 * (center + other) for other in others]
    diag = faces[0] + faces[1] + faces[2] + faces[3] + faces[4] + faces[5] + spring_term * center
    return faces, diag, center


def neighbours(u_pad):
    center = u_pad[:, 1:-1, 1:-1]
    return center, [u_pad[:, 2:, 1:-1], u_pad[:, :-2, 1:-1], u_pad[:, 1:-1, 2:], u_pad[:, 1:-1, :-2],
                    y_shift(center, 1), y_shift(center, -1)]


def apply_op(u_pad, faces, diag):
    center, others = neighbours(u_pad)
    result = diag * center
    for face, other in zip(faces, others):
        result = result - face * other
    return result, center


def strain_energy(u_pad, faces):
    center, others = neighbours(u_pad)
    total = jnp.zeros(center.shape, jnp.float32)
    for face, other in zip(faces, others):
        diff = center - other
        total = total + face * diff * diff
    return 0.25 * jnp.sum(total, axis=0)


def on_device(concentration, order_field, phase_labels, displacement, body_load):
    h = FINE_HALO
    fields = jnp.stack([concentration, order_field, mobility_of(phase_labels)])
    m = MECH_HALO
    fields = padded_2(fields, (("gy", 2),), h)
    fields, ub = lax.optimization_barrier((fields, jnp.concatenate([displacement, body_load])))
    ub = padded_2(ub, (("gx", 1),), m)
    fields = padded_2(fields, (("gx", 1),), h)
    conc, order, mob = fields[0], fields[1], fields[2]
    for step in range(STEPS):
        conc, order, mob = advance(conc, order, mob, step == STEPS - 1)

    order, ub = lax.optimization_barrier((order, ub))
    ub = padded_2(ub, (("gy", 2),), m + 1)
    disp, load = ub[:3], ub[3:]

    coarse = restrict_xzy(order)
    stiff = lax.all_to_all(coarse, "gy", split_axis=1, concat_axis=2, tiled=True)
    stiff_ext = halo_exchange(stiff[None], m, 0)[0]
    bx, bz = stiff.shape[0], stiff.shape[1]
    disp, energy = mechanics(stiff_ext, ub, TILE - (m + 1), bx, bz)
    tiles = lax.all_to_all(energy, "gy", split_axis=2, concat_axis=1, tiled=True)
    return (conc, order, disp, jnp.transpose(tiles, (0, 2, 1)))


def solution(mesh):
    return jax.shard_map(
        on_device,
        mesh=mesh,
        in_specs=(
            P("gx", "gy", None),
            P("gx", "gy", None),
            P("gx", "gy", None),
            P(None, "gx", "gy", None),
            P(None, "gx", "gy", None),
        ),
        out_specs=(
            P("gx", "gy", None),
            P("gx", "gy", None),
            P(None, "gx", "gy", None),
            P("gx", "gy", None),
        ),
        check_vma=False,
    )
```

```python
import jax
import jax.numpy as jnp
import functools

import numpy as np
from jax import lax
from jax.experimental import pallas as pl
from jax.experimental.pallas import tpu as pltpu
from jax.sharding import PartitionSpec as P

STEPS = 4
FINE_HALO = 4
MECH_HALO = 3

rate_conc = 0.15
rate_order = 0.15
well_height = 1.0
drive_coupling = 0.5
spring_term = 0.2
first_weight = 0.5956
second_weight = 2.695


MESH = pl.DeviceIdType.MESH
TILE = 8
DIRS = [(sx, sy) for sx in (-1, 0, 1) for sy in (-1, 0, 1) if (sx, sy) != (0, 0)]


def _src_window(side, size, width):
    return {1: slice(size - width, size), -1: slice(0, width), 0: slice(0, size)}[side]


def _dst_window(side, size, width):
    return {1: slice(0, width), -1: slice(width + size, size + 2 * width), 0: slice(width, width + size)}[side]


def halo_kernel(hx, nx, ny, blk_ref, out_ref, ext, send_sem, recv_sem):
    c, x, y, z = blk_ref.shape
    t = TILE
    gx = lax.axis_index("gx")
    gy = lax.axis_index("gy")

    def exists(sx, sy):
        return (gx + sx >= 0) & (gx + sx < nx) & (gy + sy >= 0) & (gy + sy < ny)

    barrier = pltpu.get_barrier_semaphore()
    for sx, sy in DIRS:
        @pl.when(exists(sx, sy))
        def _():
            pl.semaphore_signal(barrier, inc=1, device_id=(gx + sx, gy + sy), device_id_type=MESH)
    row = (gx + nx - 1) // nx + 1 + (2 * nx - 2 - gx) // nx
    col = (gy + ny - 1) // ny + 1 + (2 * ny - 2 - gy) // ny
    pl.semaphore_wait(barrier, row * col - 1)

    copies = []
    for k, (sx, sy) in enumerate(DIRS):
        copy = pltpu.make_async_remote_copy(
            src_ref=blk_ref.at[:, _src_window(sx, x, hx), _src_window(sy, y, t), :],
            dst_ref=ext.at[:, _dst_window(sx, x, hx), _dst_window(sy, y, t), :],
            send_sem=send_sem.at[k],
            recv_sem=recv_sem.at[k],
            device_id=(lax.rem(gx + sx + nx, nx), lax.rem(gy + sy + ny, ny)),
            device_id_type=MESH,
        )
        copies.append(copy)

        @pl.when(exists(sx, sy))
        def _():
            copy.start()

    ext[:, hx:hx + x, t:t + y, :] = blk_ref[...]
    for sx, sy in DIRS:
        xs, ys = _dst_window(sx, x, hx), _dst_window(sy, y, t)

        @pl.when(jnp.logical_not(exists(-sx, -sy)))
        def _():
            ext[:, xs, ys, :] = jnp.zeros((c, xs.stop - xs.start, ys.stop - ys.start, z), ext.dtype)

    for (sx, sy), copy in zip(DIRS, copies):
        @pl.when(exists(sx, sy))
        def _():
            copy.wait_send()

        @pl.when(exists(-sx, -sy))
        def _():
            copy.wait_recv()
    out_ref[...] = ext[...]


def halo_exchange(block, hx, cid):
    c, x, y, z = block.shape
    nx, ny = lax.axis_size("gx"), lax.axis_size("gy")
    shape = (c, x + 2 * hx, y + 2 * TILE, z)
    return pl.pallas_call(
        functools.partial(halo_kernel, hx, nx, ny),
        out_shape=jax.ShapeDtypeStruct(shape, block.dtype),
        in_specs=[pl.BlockSpec(memory_space=pltpu.VMEM)],
        out_specs=pl.BlockSpec(memory_space=pltpu.VMEM),
        scratch_shapes=[
            pltpu.VMEM(shape, block.dtype),
            pltpu.SemaphoreType.DMA((len(DIRS),)),
            pltpu.SemaphoreType.DMA((len(DIRS),)),
        ],
        compiler_params=pltpu.CompilerParams(collective_id=cid, has_side_effects=True),
    )(block)


def _rolls(v):
    lane = lax.broadcasted_iota(jnp.int32, v.shape, 1)
    last = v.shape[1] - 1
    return (pltpu.roll(v, v.shape[0] - 1, 0), pltpu.roll(v, 1, 0),
            jnp.where(lane == last, 0.0, pltpu.roll(v, last, 1)), jnp.where(lane == 0, 0.0, pltpu.roll(v, 1, 1)))


def mech_kernel(zoff, s_ref, ub_ref, disp_out, energy_out, u1, u2, fc):
    _, nxe, nz, _ = ub_ref.shape
    bx, bz = disp_out.shape[1], disp_out.shape[2]
    m = (nxe - bx) // 2
    lo = (nz - bz) // 2

    def align(i, carry):
        fc[7, i] = s_ref[i, pl.ds(zoff, nz), :]
        return carry

    lax.fori_loop(0, nxe, align, 0, unroll=True)

    def faces_row(i, carry):
        c = fc[7, i]
        zp, zm, yp, ym = _rolls(c)
        diag = None
        for f, o in enumerate((fc[7, i + 1], fc[7, i - 1], zp, zm, yp, ym)):
            face = 0.5 * (c + o)
            fc[f, i] = face
            diag = face if diag is None else diag + face
        fc[6, i] = diag + spring_term * c
        return carry

    lax.fori_loop(1, nxe - 1, faces_row, 0, unroll=True)

    def sweep(src, dst, weight, i):
        c, diag = fc[7, i], fc[6, i]
        for k in range(3):
            u = src[k, i]
            others = (src[k, i + 1], src[k, i - 1]) + _rolls(u)
            result = diag * u
            for f, other in enumerate(others):
                result = result - fc[f, i] * other
            new = u + weight * (ub_ref[3 + k, i] - result) / diag
            dst[k, i] = jnp.where(c > 0, new, 0.0)

    def first(i, carry):
        sweep(ub_ref, u1, first_weight, i)
        return carry

    def second(i, carry):
        sweep(u1, u2, second_weight, i)
        return carry

    lax.fori_loop(1, nxe - 1, first, 0, unroll=True)
    lax.fori_loop(2, nxe - 2, second, 0, unroll=True)

    def energy_row(i, carry):
        parts = []
        for k in range(3):
            u = u2[k, i]
            others = (u2[k, i + 1], u2[k, i - 1]) + _rolls(u)
            total = jnp.zeros(u.shape, jnp.float32)
            for f, other in enumerate(others):
                diff = u - other
                total = total + fc[f, i] * diff * diff
            parts.append(total)
        u1[0, i] = 0.25 * (parts[0] + parts[1] + parts[2])
        return carry

    lax.fori_loop(m, m + bx, energy_row, 0, unroll=True)
    energy_out[...] = u1[0, pl.ds(m, bx), pl.ds(lo, bz), :]
    disp_out[...] = u2[:, pl.ds(m, bx), pl.ds(lo, bz), :]


def mechanics(stiff_ext, ub, zoff, bx, bz):
    _, nxe, nz, ny = ub.shape
    return pl.pallas_call(
        functools.partial(mech_kernel, zoff),
        out_shape=(jax.ShapeDtypeStruct((3, bx, bz, ny), jnp.float32),
                   jax.ShapeDtypeStruct((bx, bz, ny), jnp.float32)),
        in_specs=[pl.BlockSpec(memory_space=pltpu.VMEM)] * 2,
        out_specs=(pl.BlockSpec(memory_space=pltpu.VMEM), pl.BlockSpec(memory_space=pltpu.VMEM)),
        scratch_shapes=[pltpu.VMEM((3, nxe, nz, ny), jnp.float32), pltpu.VMEM((3, nxe, nz, ny), jnp.float32),
                        pltpu.VMEM((8, nxe, nz, ny), jnp.float32)],
    )(stiff_ext, ub)


def padded_2(block, sides, width):
    for axis, dim in sides:
        count = lax.axis_size(axis)
        forward = [(i, i + 1) for i in range(count - 1)]
        backward = [(target, source) for source, target in forward]
        low = lax.ppermute(
            lax.slice_in_dim(block, block.shape[dim] - width, None, axis=dim), axis, forward
        )
        high = lax.ppermute(lax.slice_in_dim(block, 0, width, axis=dim), axis, backward)
        block = jnp.concatenate([low, block, high], axis=dim)
    return block


def fine_laplace(padded):
    zpad = jnp.pad(padded, ((0, 0), (0, 0), (1, 1)))
    center = zpad[1:-1, 1:-1, 1:-1]
    total = zpad[2:, 1:-1, 1:-1] + zpad[:-2, 1:-1, 1:-1]
    total = total + zpad[1:-1, 2:, 1:-1] + zpad[1:-1, :-2, 1:-1]
    total = total + zpad[1:-1, 1:-1, 2:] + zpad[1:-1, 1:-1, :-2]
    return total - 6.0 * center


def advance(conc_pad, order_pad, mob_pad, last):
    chem = conc_pad - order_pad * order_pad * (3.0 - 2.0 * order_pad)
    conc_in = conc_pad[1:-1, 1:-1]
    order_in = order_pad[1:-1, 1:-1]
    chem_in = chem[1:-1, 1:-1]
    mobility = mob_pad[1:-1, 1:-1]
    conc_new = conc_in + rate_conc * fine_laplace(chem)
    dh_term = 6.0 * order_in * (1.0 - order_in)
    dg_term = 2.0 * order_in * (1.0 - order_in) * (1.0 - 2.0 * order_in)
    order_new = order_in + mobility * (
        rate_order * fine_laplace(order_pad)
        - well_height * dg_term
        + drive_coupling * chem_in * dh_term
    )
    if not last:
        conc_new = jnp.where(mobility > 0, conc_new, 0.0)
    return conc_new, order_new, mobility


def mobility_of(labels):
    return (0.5 * (labels == 0) + 1.0 * (labels == 1) + 0.25 * (labels == 2)).astype(jnp.float32)


def restrict_xzy(order_out):
    sx, sy, sz = order_out.shape
    sq = order_out * order_out
    sq = sq.reshape(sx // 2, 2, sy, sz).sum(axis=1)
    sq = sq.reshape(sx // 2, sy // 2, 2, sz).sum(axis=2)
    pairs = jnp.asarray(np.repeat(np.eye(sz // 2, dtype=np.float32), 2, axis=0))
    summed = jnp.einsum("xyz,zw->xwy", sq, pairs, precision=lax.Precision.HIGHEST)
    return 0.1 + 0.125 * summed


def y_shift(v, step):
    if step > 0:
        return jnp.pad(v[..., step:], [(0, 0)] * (v.ndim - 1) + [(0, step)])
    return jnp.pad(v[..., :step], [(0, 0)] * (v.ndim - 1) + [(-step, 0)])


def face_terms(stiff_pad):
    center = stiff_pad[1:-1, 1:-1]
    others = [stiff_pad[2:, 1:-1], stiff_pad[:-2, 1:-1], stiff_pad[1:-1, 2:], stiff_pad[1:-1, :-2],
              y_shift(center, 1), y_shift(center, -1)]
    faces = [0.5 * (center + other) for other in others]
    diag = faces[0] + faces[1] + faces[2] + faces[3] + faces[4] + faces[5] + spring_term * center
    return faces, diag, center


def neighbours(u_pad):
    center = u_pad[:, 1:-1, 1:-1]
    return center, [u_pad[:, 2:, 1:-1], u_pad[:, :-2, 1:-1], u_pad[:, 1:-1, 2:], u_pad[:, 1:-1, :-2],
                    y_shift(center, 1), y_shift(center, -1)]


def apply_op(u_pad, faces, diag):
    center, others = neighbours(u_pad)
    result = diag * center
    for face, other in zip(faces, others):
        result = result - face * other
    return result, center


def strain_energy(u_pad, faces):
    center, others = neighbours(u_pad)
    total = jnp.zeros(center.shape, jnp.float32)
    for face, other in zip(faces, others):
        diff = center - other
        total = total + face * diff * diff
    return 0.25 * jnp.sum(total, axis=0)


def on_device(concentration, order_field, phase_labels, displacement, body_load):
    h = FINE_HALO
    fields = jnp.stack([concentration, order_field, mobility_of(phase_labels)])
    m = MECH_HALO
    fields = padded_2(fields, (("gx", 1),), h)
    fields, ub = lax.optimization_barrier((fields, jnp.concatenate([displacement, body_load])))
    ub = padded_2(ub, (("gx", 1),), m)
    fields = padded_2(fields, (("gy", 2),), h)
    conc, order, mob = fields[0], fields[1], fields[2].astype(jnp.bfloat16)
    for step in range(STEPS):
        conc, order, mob = advance(conc, order, mob, step == STEPS - 1)

    order, ub = lax.optimization_barrier((order, ub))
    ub = padded_2(ub, (("gy", 2),), m + 1)
    disp, load = ub[:3], ub[3:]

    coarse = restrict_xzy(order)
    stiff = lax.all_to_all(coarse, "gy", split_axis=1, concat_axis=2, tiled=True)
    stiff_ext = halo_exchange(stiff[None], m, 0)[0]
    bx, bz = stiff.shape[0], stiff.shape[1]
    disp, energy = mechanics(stiff_ext, ub, TILE - (m + 1), bx, bz)
    tiles = lax.all_to_all(energy, "gy", split_axis=2, concat_axis=1, tiled=True)
    return (conc, order, disp, jnp.transpose(tiles, (0, 2, 1)))


def solution(mesh):
    return jax.shard_map(
        on_device,
        mesh=mesh,
        in_specs=(
            P("gx", "gy", None),
            P("gx", "gy", None),
            P("gx", "gy", None),
            P(None, "gx", "gy", None),
            P(None, "gx", "gy", None),
        ),
        out_specs=(
            P("gx", "gy", None),
            P("gx", "gy", None),
            P(None, "gx", "gy", None),
            P("gx", "gy", None),
        ),
        check_vma=False,
    )
```

```python
import jax
import jax.numpy as jnp
import functools

import numpy as np
from jax import lax
from jax.experimental import pallas as pl
from jax.experimental.pallas import tpu as pltpu
from jax.sharding import PartitionSpec as P

STEPS = 4
FINE_HALO = 4
MECH_HALO = 3

rate_conc = 0.15
rate_order = 0.15
well_height = 1.0
drive_coupling = 0.5
spring_term = 0.2
first_weight = 0.5956
second_weight = 2.695


MESH = pl.DeviceIdType.MESH
TILE = 8
DIRS = [(sx, sy) for sx in (-1, 0, 1) for sy in (-1, 0, 1) if (sx, sy) != (0, 0)]


def _src_window(side, size, width):
    return {1: slice(size - width, size), -1: slice(0, width), 0: slice(0, size)}[side]


def _dst_window(side, size, width):
    return {1: slice(0, width), -1: slice(width + size, size + 2 * width), 0: slice(width, width + size)}[side]


def halo_kernel(hx, nx, ny, blk_ref, out_ref, ext, send_sem, recv_sem):
    c, x, y, z = blk_ref.shape
    t = TILE
    gx = lax.axis_index("gx")
    gy = lax.axis_index("gy")

    def exists(sx, sy):
        return (gx + sx >= 0) & (gx + sx < nx) & (gy + sy >= 0) & (gy + sy < ny)

    barrier = pltpu.get_barrier_semaphore()
    for sx, sy in DIRS:
        @pl.when(exists(sx, sy))
        def _():
            pl.semaphore_signal(barrier, inc=1, device_id=(gx + sx, gy + sy), device_id_type=MESH)
    row = (gx + nx - 1) // nx + 1 + (2 * nx - 2 - gx) // nx
    col = (gy + ny - 1) // ny + 1 + (2 * ny - 2 - gy) // ny
    pl.semaphore_wait(barrier, row * col - 1)

    copies = []
    for k, (sx, sy) in enumerate(DIRS):
        copy = pltpu.make_async_remote_copy(
            src_ref=blk_ref.at[:, _src_window(sx, x, hx), _src_window(sy, y, t), :],
            dst_ref=ext.at[:, _dst_window(sx, x, hx), _dst_window(sy, y, t), :],
            send_sem=send_sem.at[k],
            recv_sem=recv_sem.at[k],
            device_id=(lax.rem(gx + sx + nx, nx), lax.rem(gy + sy + ny, ny)),
            device_id_type=MESH,
        )
        copies.append(copy)

        @pl.when(exists(sx, sy))
        def _():
            copy.start()

    ext[:, hx:hx + x, t:t + y, :] = blk_ref[...]
    for sx, sy in DIRS:
        xs, ys = _dst_window(sx, x, hx), _dst_window(sy, y, t)

        @pl.when(jnp.logical_not(exists(-sx, -sy)))
        def _():
            ext[:, xs, ys, :] = jnp.zeros((c, xs.stop - xs.start, ys.stop - ys.start, z), ext.dtype)

    for (sx, sy), copy in zip(DIRS, copies):
        @pl.when(exists(sx, sy))
        def _():
            copy.wait_send()

        @pl.when(exists(-sx, -sy))
        def _():
            copy.wait_recv()
    out_ref[...] = ext[...]


def halo_exchange(block, hx, cid):
    c, x, y, z = block.shape
    nx, ny = lax.axis_size("gx"), lax.axis_size("gy")
    shape = (c, x + 2 * hx, y + 2 * TILE, z)
    return pl.pallas_call(
        functools.partial(halo_kernel, hx, nx, ny),
        out_shape=jax.ShapeDtypeStruct(shape, block.dtype),
        in_specs=[pl.BlockSpec(memory_space=pltpu.VMEM)],
        out_specs=pl.BlockSpec(memory_space=pltpu.VMEM),
        scratch_shapes=[
            pltpu.VMEM(shape, block.dtype),
            pltpu.SemaphoreType.DMA((len(DIRS),)),
            pltpu.SemaphoreType.DMA((len(DIRS),)),
        ],
        compiler_params=pltpu.CompilerParams(collective_id=cid, has_side_effects=True),
    )(block)


def _rolls(v):
    lane = lax.broadcasted_iota(jnp.int32, v.shape, 1)
    last = v.shape[1] - 1
    return (pltpu.roll(v, v.shape[0] - 1, 0), pltpu.roll(v, 1, 0),
            jnp.where(lane == last, 0.0, pltpu.roll(v, last, 1)), jnp.where(lane == 0, 0.0, pltpu.roll(v, 1, 1)))


def mech_kernel(zoff, s_ref, ub_ref, disp_out, energy_out, u1, u2, fc):
    _, nxe, nz, _ = ub_ref.shape
    bx, bz = disp_out.shape[1], disp_out.shape[2]
    m = (nxe - bx) // 2
    lo = (nz - bz) // 2

    def align(i, carry):
        fc[7, i] = s_ref[i, pl.ds(zoff, nz), :]
        return carry

    lax.fori_loop(0, nxe, align, 0, unroll=True)

    def faces_row(i, carry):
        c = fc[7, i]
        zp, zm, yp, ym = _rolls(c)
        diag = None
        for f, o in enumerate((fc[7, i + 1], fc[7, i - 1], zp, zm, yp, ym)):
            face = 0.5 * (c + o)
            fc[f, i] = face
            diag = face if diag is None else diag + face
        fc[6, i] = diag + spring_term * c
        return carry

    lax.fori_loop(1, nxe - 1, faces_row, 0, unroll=True)

    def sweep(src, dst, weight, i):
        c, diag = fc[7, i], fc[6, i]
        inv = 1.0 / diag
        for k in range(3):
            u = src[k, i]
            others = (src[k, i + 1], src[k, i - 1]) + _rolls(u)
            result = diag * u
            for f, other in enumerate(others):
                result = result - fc[f, i] * other
            new = u + weight * (ub_ref[3 + k, i] - result) * inv
            dst[k, i] = jnp.where(c > 0, new, 0.0)

    def first(i, carry):
        sweep(ub_ref, u1, first_weight, i)
        return carry

    def second(i, carry):
        sweep(u1, u2, second_weight, i)
        return carry

    lax.fori_loop(1, nxe - 1, first, 0, unroll=True)
    lax.fori_loop(2, nxe - 2, second, 0, unroll=True)

    def energy_row(i, carry):
        parts = []
        for k in range(3):
            u = u2[k, i]
            others = (u2[k, i + 1], u2[k, i - 1]) + _rolls(u)
            total = jnp.zeros(u.shape, jnp.float32)
            for f, other in enumerate(others):
                diff = u - other
                total = total + fc[f, i] * diff * diff
            parts.append(total)
        u1[0, i] = 0.25 * (parts[0] + parts[1] + parts[2])
        return carry

    lax.fori_loop(m, m + bx, energy_row, 0, unroll=True)
    energy_out[...] = u1[0, pl.ds(m, bx), pl.ds(lo, bz), :]
    disp_out[...] = u2[:, pl.ds(m, bx), pl.ds(lo, bz), :]


def mechanics(stiff_ext, ub, zoff, bx, bz):
    _, nxe, nz, ny = ub.shape
    return pl.pallas_call(
        functools.partial(mech_kernel, zoff),
        out_shape=(jax.ShapeDtypeStruct((3, bx, bz, ny), jnp.float32),
                   jax.ShapeDtypeStruct((bx, bz, ny), jnp.float32)),
        in_specs=[pl.BlockSpec(memory_space=pltpu.VMEM)] * 2,
        out_specs=(pl.BlockSpec(memory_space=pltpu.VMEM), pl.BlockSpec(memory_space=pltpu.VMEM)),
        scratch_shapes=[pltpu.VMEM((3, nxe, nz, ny), jnp.float32), pltpu.VMEM((3, nxe, nz, ny), jnp.float32),
                        pltpu.VMEM((8, nxe, nz, ny), jnp.float32)],
    )(stiff_ext, ub)


def padded_2(block, sides, width):
    for axis, dim in sides:
        count = lax.axis_size(axis)
        forward = [(i, i + 1) for i in range(count - 1)]
        backward = [(target, source) for source, target in forward]
        low = lax.ppermute(
            lax.slice_in_dim(block, block.shape[dim] - width, None, axis=dim), axis, forward
        )
        high = lax.ppermute(lax.slice_in_dim(block, 0, width, axis=dim), axis, backward)
        block = jnp.concatenate([low, block, high], axis=dim)
    return block


def fine_laplace(padded):
    zpad = jnp.pad(padded, ((0, 0), (0, 0), (1, 1)))
    center = zpad[1:-1, 1:-1, 1:-1]
    total = zpad[2:, 1:-1, 1:-1] + zpad[:-2, 1:-1, 1:-1]
    total = total + zpad[1:-1, 2:, 1:-1] + zpad[1:-1, :-2, 1:-1]
    total = total + zpad[1:-1, 1:-1, 2:] + zpad[1:-1, 1:-1, :-2]
    return total - 6.0 * center


def advance(conc_pad, order_pad, mob_pad, last):
    chem = conc_pad - order_pad * order_pad * (3.0 - 2.0 * order_pad)
    conc_in = conc_pad[1:-1, 1:-1]
    order_in = order_pad[1:-1, 1:-1]
    chem_in = chem[1:-1, 1:-1]
    mobility = mob_pad[1:-1, 1:-1]
    conc_new = conc_in + rate_conc * fine_laplace(chem)
    dh_term = 6.0 * order_in * (1.0 - order_in)
    dg_term = 2.0 * order_in * (1.0 - order_in) * (1.0 - 2.0 * order_in)
    order_new = order_in + mobility * (
        rate_order * fine_laplace(order_pad)
        - well_height * dg_term
        + drive_coupling * chem_in * dh_term
    )
    if not last:
        conc_new = jnp.where(mobility > 0, conc_new, 0.0)
    return conc_new, order_new, mobility


def mobility_of(labels):
    return (0.5 * (labels == 0) + 1.0 * (labels == 1) + 0.25 * (labels == 2)).astype(jnp.float32)


def restrict_xzy(order_out):
    sx, sy, sz = order_out.shape
    sq = order_out * order_out
    sq = sq.reshape(sx // 2, 2, sy, sz).sum(axis=1)
    sq = sq.reshape(sx // 2, sy // 2, 2, sz).sum(axis=2)
    pairs = jnp.asarray(np.repeat(np.eye(sz // 2, dtype=np.float32), 2, axis=0))
    summed = jnp.einsum("xyz,zw->xwy", sq, pairs, precision=lax.Precision.HIGHEST)
    return 0.1 + 0.125 * summed


def y_shift(v, step):
    if step > 0:
        return jnp.pad(v[..., step:], [(0, 0)] * (v.ndim - 1) + [(0, step)])
    return jnp.pad(v[..., :step], [(0, 0)] * (v.ndim - 1) + [(-step, 0)])


def face_terms(stiff_pad):
    center = stiff_pad[1:-1, 1:-1]
    others = [stiff_pad[2:, 1:-1], stiff_pad[:-2, 1:-1], stiff_pad[1:-1, 2:], stiff_pad[1:-1, :-2],
              y_shift(center, 1), y_shift(center, -1)]
    faces = [0.5 * (center + other) for other in others]
    diag = faces[0] + faces[1] + faces[2] + faces[3] + faces[4] + faces[5] + spring_term * center
    return faces, diag, center


def neighbours(u_pad):
    center = u_pad[:, 1:-1, 1:-1]
    return center, [u_pad[:, 2:, 1:-1], u_pad[:, :-2, 1:-1], u_pad[:, 1:-1, 2:], u_pad[:, 1:-1, :-2],
                    y_shift(center, 1), y_shift(center, -1)]


def apply_op(u_pad, faces, diag):
    center, others = neighbours(u_pad)
    result = diag * center
    for face, other in zip(faces, others):
        result = result - face * other
    return result, center


def strain_energy(u_pad, faces):
    center, others = neighbours(u_pad)
    total = jnp.zeros(center.shape, jnp.float32)
    for face, other in zip(faces, others):
        diff = center - other
        total = total + face * diff * diff
    return 0.25 * jnp.sum(total, axis=0)


def on_device(concentration, order_field, phase_labels, displacement, body_load):
    h = FINE_HALO
    fields = jnp.stack([concentration, order_field, mobility_of(phase_labels)])
    m = MECH_HALO
    fields = padded_2(fields, (("gx", 1),), h)
    fields, ub = lax.optimization_barrier((fields, jnp.concatenate([displacement, body_load])))
    ub = padded_2(ub, (("gx", 1),), m)
    fields = padded_2(fields, (("gy", 2),), h)
    conc, order, mob = fields[0], fields[1], fields[2].astype(jnp.bfloat16)
    for step in range(STEPS):
        conc, order, mob = advance(conc, order, mob, step == STEPS - 1)

    order, ub = lax.optimization_barrier((order, ub))
    ub = padded_2(ub, (("gy", 2),), m + 1)
    disp, load = ub[:3], ub[3:]

    coarse = restrict_xzy(order)
    stiff = lax.all_to_all(coarse, "gy", split_axis=1, concat_axis=2, tiled=True)
    stiff_ext = halo_exchange(stiff[None], m, 0)[0]
    bx, bz = stiff.shape[0], stiff.shape[1]
    disp, energy = mechanics(stiff_ext, ub, TILE - (m + 1), bx, bz)
    tiles = lax.all_to_all(energy, "gy", split_axis=2, concat_axis=1, tiled=True)
    return (conc, order, disp, jnp.transpose(tiles, (0, 2, 1)))


def solution(mesh):
    return jax.shard_map(
        on_device,
        mesh=mesh,
        in_specs=(
            P("gx", "gy", None),
            P("gx", "gy", None),
            P("gx", "gy", None),
            P(None, "gx", "gy", None),
            P(None, "gx", "gy", None),
        ),
        out_specs=(
            P("gx", "gy", None),
            P("gx", "gy", None),
            P(None, "gx", "gy", None),
            P("gx", "gy", None),
        ),
        check_vma=False,
    )
```
